32 devices in a mesh: dp: 4 (over x, core), fsdp: 8 (over z, y).
Axes of the slice: x: 2, y: 2, z: 4, core: 2. Of those that a mesh axis runs over, the one named last changes fastest.
Arguments:
- tokens: bfloat16 [3, 32768, 512], P(None, ('dp', 'fsdp')), may hold values from -6 to 6
- cotangent: bfloat16 [3, 32768, 512], P(None, ('dp', 'fsdp')), may hold values from -6 to 6
- lengths: int32 [3, 16], replicated, may hold values from 16 to 48, as said below
- stretch_order: int32 [3, 512], replicated, may hold values from 0 to 511, as said below
- ln1_gain: bfloat16 [512], P(('dp', 'fsdp')), may hold values from 0.099609375 to 1.8984375
- ln1_bias: bfloat16 [512], P(('dp', 'fsdp')), may hold values from -3 to 3
- w_qkv: bfloat16 [512, 1536], P(('dp', 'fsdp')), may hold values from -0.25 to 0.25
- b_qkv: bfloat16 [1536], P(('dp', 'fsdp')), may hold values from -2 to 2
- w_out: bfloat16 [512, 512], P(('dp', 'fsdp')), may hold values from -1 to 1
- b_out: bfloat16 [512], P(('dp', 'fsdp')), may hold values from -3 to 3
- ln2_gain: bfloat16 [512], P(('dp', 'fsdp')), may hold values from 0.099609375 to 1.8984375
- ln2_bias: bfloat16 [512], P(('dp', 'fsdp')), may hold values from -3 to 3
- w_up: bfloat16 [512, 2048], P(('dp', 'fsdp')), may hold values from -0.25 to 0.25
- b_up: bfloat16 [2048], P(('dp', 'fsdp')), may hold values from -3 to 3
- w_down: bfloat16 [2048, 512], P(('dp', 'fsdp')), may hold values from -0.125 to 0.125
- b_down: bfloat16 [512], P(('dp', 'fsdp')), may hold values from -3 to 3
Outputs:
- result: bfloat16 [3, 32768, 512], P(None, ('dp', 'fsdp'))
- input_grad: bfloat16 [3, 32768, 512], P(None, ('dp', 'fsdp'))
- grad_ln1_gain: float32 [512], P(('dp', 'fsdp'))
- grad_ln1_bias: float32 [512], P(('dp', 'fsdp'))
- grad_w_qkv: float32 [512, 1536], P(('dp', 'fsdp'))
- grad_b_qk: float32 [1024], P(('dp', 'fsdp'))
- grad_b_value: float32 [512], P(('dp', 'fsdp'))
- grad_w_out: float32 [512, 512], P(('dp', 'fsdp'))
- grad_b_out: float32 [512], P(('dp', 'fsdp'))
- grad_ln2_gain: float32 [512], P(('dp', 'fsdp'))
- grad_ln2_bias: float32 [512], P(('dp', 'fsdp'))
- grad_w_up: float32 [512, 2048], P(('dp', 'fsdp'))
- grad_b_up: float32 [2048], P(('dp', 'fsdp'))
- grad_w_down: float32 [2048, 512], P(('dp', 'fsdp'))
- grad_b_down: float32 [512], P(('dp', 'fsdp'))
The draws below stay inside these ranges and needn't reach their ends.
Inputs may be any that keep to these rules, and one draw needn't show every extreme that they name: `lengths`: each row sums to 512: the sequences of a micro-batch lie end to end from its first layout row and fill it. No sequence crosses from the layout stretches of one dp index to those of the next: each aligned block of 1024 / 64 * 8 layout stretches holds whole sequences. `stretch_order`: each row is a permutation of the stretches. Layout position p belongs to the device p // 16 of dp+fsdp; the stretch placed there arrives on a device with the same fsdp index, and every device receives exactly 1024 / 64 / 4 stretches from each device of the same fsdp index.
All inputs are finite; a program needn't handle non-finite values.
Results may differ from the reference program's by a relative error of at most 0.0085.
Values may be sent and summed in bfloat16 or wider, within the bound.
No kernel may reach another device: no remote copies, remote signals or barrier semaphores. Data moves between devices by JAX's collectives and lax.ppermute only.
A program may use at most 384 MiB of HBM per device.

```python
from functools import partial
import jax
import jax.numpy as jnp
from jax import lax

D = 512
HEADS = 8
HEAD_DIM = 64
FF = 2048
STRETCH = 64
SEQ_STRETCHES = 32
MICRO = 3
TOK_MB = 1024
TOKENS = 32768
NSEQ = 16
N_DP = 4
N_FSDP = 8


def draw_tokens(key, part):
    key_row, key_common = jax.random.split(key, 2)
    stretch_total = TOKENS // STRETCH
    common = jax.random.normal(key_common, (MICRO, stretch_total, 1, D), jnp.float32)
    row_part = jax.random.normal(key_row, (MICRO, stretch_total, STRETCH, D), jnp.float32)
    values = 0.7 * row_part + 0.7 * common
    return jnp.clip(values, -6.0, 6.0).reshape(MICRO, TOKENS, D).astype(jnp.bfloat16)


def shuffle_block(seed_key):
    return jax.random.permutation(seed_key, NSEQ // N_DP)


def draw_lengths(key, part):
    pair_count = NSEQ // 2
    half_span = SEQ_STRETCHES // 2
    key_offset, key_pick, key_order = jax.random.split(key, 3)
    offsets = jax.random.randint(key_offset, (MICRO, pair_count), 0, half_span + 1)
    picked = jax.random.randint(key_pick, (MICRO, 1), 0, pair_count)
    column = jnp.arange(pair_count, dtype=jnp.int32)[None, :]
    offsets = jnp.where(column == picked, half_span, offsets)
    paired = jnp.stack([SEQ_STRETCHES + offsets, SEQ_STRETCHES - offsets], axis=2).reshape(MICRO * N_DP, NSEQ // N_DP)
    orders = jax.vmap(shuffle_block)(jax.random.split(key_order, MICRO * N_DP))
    shuffled = jnp.take_along_axis(paired, orders, axis=1)
    return shuffled.reshape(MICRO, NSEQ).astype(jnp.int32)


def shuffle_device(seed_key):
    return jax.random.permutation(seed_key, TOK_MB // STRETCH).astype(jnp.int32)


def order_micro(micro_key):
    per_device = TOK_MB // STRETCH
    group_size = per_device // N_DP
    devices = N_DP * N_FSDP
    key_local, key_shift, key_deal = jax.random.split(micro_key, 3)
    local_perm = jax.vmap(shuffle_device)(jax.random.split(key_local, devices))
    source_ids = jnp.arange(devices, dtype=jnp.int32)[:, None] * per_device + local_perm
    source_ids = source_ids.reshape(N_DP, N_FSDP, N_DP, group_size)
    shifts = jax.random.randint(key_shift, (N_FSDP,), 0, N_DP).astype(jnp.int32)
    target = jnp.arange(N_DP, dtype=jnp.int32)[:, None, None]
    source = jnp.arange(N_DP, dtype=jnp.int32)[None, :, None]
    column = jnp.arange(N_FSDP, dtype=jnp.int32)[None, None, :]
    which = (target - source - shifts[None, None, :]) % N_DP
    picked = source_ids[source, column, which]
    received = picked.transpose(0, 2, 1, 3).reshape(devices, per_device)
    dealing = jax.vmap(shuffle_device)(jax.random.split(key_deal, devices))
    return jnp.take_along_axis(received, dealing, axis=1).reshape(-1)


def draw_stretch_order(key, part):
    return jax.vmap(order_micro)(jax.random.split(key, MICRO)).astype(jnp.int32)


def steps_of(rng, dims, cuts, least, top_value):
    def one(axis_at, shards_of):
        steps = jax.random.uniform(jax.random.fold_in(jax.random.fold_in(rng, 6), axis_at), (shards_of,), jnp.float32, least / len(cuts), top_value / len(cuts))
        return jnp.repeat(jnp.exp(steps), dims[axis_at] // shards_of).reshape((-1,) + (1,) * (len(dims) - axis_at - 1))

    level = one(*cuts[0])
    for cut in cuts[1:]:
        level = level * one(*cut)
    return level


def noise(own_key, shape, deviation, limit, cuts=(), kind=jnp.bfloat16):
    gain = steps_of(own_key, shape, cuts, -0.22, 0.18) if cuts else 1.0
    entries = jax.random.normal(own_key, shape, jnp.float32) * deviation * gain
    return jnp.minimum(jnp.maximum(entries, -limit), limit).astype(kind)


def setup_inputs(seed: int = 0) -> dict:
    key_of = jax.random.split(jax.random.key(seed), 17)
    return {
        "tokens": draw_tokens(jax.random.fold_in(key_of[16], 71), 0),
        "cotangent": noise(key_of[1], (MICRO, TOKENS, D), 1.0, 6.0, ((1, 32),)),
        "lengths": draw_lengths(jax.random.fold_in(key_of[16], 71), 0),
        "stretch_order": draw_stretch_order(jax.random.fold_in(key_of[16], 71), 0),
        "ln1_gain": jnp.clip(1.0 + 0.18 * jax.random.normal(key_of[4], (D,), jnp.float32), 0.099609375, 1.8984375).astype(jnp.bfloat16),
        "ln1_bias": noise(key_of[5], (D,), 0.3, 3.0, ((0, 32),)),
        "w_qkv": noise(key_of[6], (D, 3 * D), D ** -0.5, 0.25, ((0, 32),)),
        "b_qkv": noise(key_of[7], (3 * D,), 0.2, 2.0, ((0, 32),)),
        "w_out": noise(key_of[8], (D, D), (D // 16) ** -0.5, 1.0, ((0, 32),)),
        "b_out": noise(key_of[9], (D,), 0.3, 3.0, ((0, 32),)),
        "ln2_gain": jnp.clip(1.0 + 0.18 * jax.random.normal(key_of[10], (D,), jnp.float32), 0.099609375, 1.8984375).astype(jnp.bfloat16),
        "ln2_bias": noise(key_of[11], (D,), 0.3, 3.0, ((0, 32),)),
        "w_up": noise(key_of[12], (D, FF), D ** -0.5, 0.25, ((0, 32),)),
        "b_up": noise(key_of[13], (FF,), 0.3, 3.0, ((0, 32),)),
        "w_down": noise(key_of[14], (FF, D), FF ** -0.5, 0.125, ((0, 32),)),
        "b_down": noise(key_of[15], (D,), 0.3, 3.0, ((0, 32),)),
    }


@jax.custom_vjp
def low(v):
    return lax.optimization_barrier(v.astype(jnp.bfloat16)).astype(jnp.float32)

@jax.custom_vjp
def low_back(v):
    return v

def low_keep(v):
    return (low(v), None)

def low_pass(kept, grad):
    return (grad,)

def back_keep(v):
    return (v, None)

def back_low(kept, grad):
    return (low(grad),)
low.defvjp(low_keep, low_pass)
low_back.defvjp(back_keep, back_low)
highest = lax.Precision.HIGHEST
eps_norm = 1e-05

def layer_norm(values, gain_vec, shift_vec):
    centre = lax.optimization_barrier(jnp.mean(values, axis=-1, keepdims=True))
    centred = values - centre
    spread = lax.optimization_barrier(jnp.mean(centred * centred, axis=-1, keepdims=True))
    return centred * lax.rsqrt(spread + eps_norm) * gain_vec + shift_vec

def feature(values):
    return jax.nn.elu(values) + 1.0

def split_heads(matrix):
    return matrix.reshape(-1, STRETCH, HEADS, HEAD_DIM).transpose(0, 2, 1, 3)

def merge_heads(blocked):
    return blocked.transpose(0, 2, 1, 3).reshape(-1, HEADS * HEAD_DIM)

def stretch_step(carried, inputs):
    running, key_sum = carried
    queries, key_rows, value_rows = inputs
    causal = jnp.tril(jnp.ones((STRETCH, STRETCH), queries.dtype))
    mixing = jnp.einsum('hid,hjd->hij', queries, key_rows, precision=highest) * causal
    numerator = jnp.einsum('hij,hje->hie', mixing, value_rows, precision=highest)
    numerator = numerator + jnp.einsum('hid,hde->hie', queries, running, precision=highest)
    denominator = lax.optimization_barrier(jnp.sum(mixing, axis=-1)) + jnp.einsum('hid,hd->hi', queries, key_sum, precision=highest)
    attended = numerator / denominator[..., None]
    running = running + jnp.einsum('hjd,hje->hde', key_rows, value_rows, precision=highest)
    key_sum = key_sum + lax.optimization_barrier(jnp.sum(key_rows, axis=1))
    return ((running, key_sum), attended)

def attend(queries, key_rows, value_rows, starts, positions):
    longest = SEQ_STRETCHES + SEQ_STRETCHES // 2
    query_blocks = split_heads(queries)
    key_blocks = split_heads(key_rows)
    value_blocks = split_heads(value_rows)
    pad_shape = (longest,) + query_blocks.shape[1:]
    query_pad = jnp.concatenate([query_blocks, jnp.ones(pad_shape, query_blocks.dtype)], axis=0)
    key_pad = jnp.concatenate([key_blocks, jnp.ones(pad_shape, key_blocks.dtype)], axis=0)
    value_pad = jnp.concatenate([value_blocks, jnp.zeros(pad_shape, value_blocks.dtype)], axis=0)
    initial = (jnp.zeros((HEADS, HEAD_DIM, HEAD_DIM), queries.dtype), jnp.zeros((HEADS, HEAD_DIM), queries.dtype))

    def one_sequence(start):
        pieces = (lax.dynamic_slice_in_dim(query_pad, start, longest, 0), lax.dynamic_slice_in_dim(key_pad, start, longest, 0), lax.dynamic_slice_in_dim(value_pad, start, longest, 0))
        _, outputs = lax.scan(jax.checkpoint(stretch_step), initial, pieces)
        return outputs
    padded = lax.map(one_sequence, starts)
    flat = padded.reshape((-1,) + padded.shape[2:])
    return merge_heads(jnp.take(flat, positions, axis=0))

def forward(starts, positions, rows_in, params):
    gain_one, shift_one, qkv_weight, qkv_bias, out_weight, out_bias, gain_two, shift_two, up_weight, up_bias, down_weight, down_bias = params
    model_width = HEADS * HEAD_DIM
    normed = low(layer_norm(rows_in, gain_one, shift_one))
    mixed = low_back(jnp.dot(normed, qkv_weight, precision=highest) + qkv_bias)
    queries = low(feature(mixed[:, :model_width]))
    key_rows = low(feature(mixed[:, model_width:2 * model_width]))
    value_rows = low(mixed[:, 2 * model_width:])
    attended = low(low_back(attend(queries, key_rows, value_rows, starts, positions)))
    branch = low_back(jnp.dot(attended, out_weight, precision=highest) + out_bias)
    middle = rows_in + branch
    normed_two = low(layer_norm(middle, gain_two, shift_two))
    hidden = low_back(jnp.dot(normed_two, up_weight, precision=highest) + up_bias)
    active = low(jax.nn.gelu(hidden))
    return middle + jnp.dot(active, down_weight, precision=highest) + down_bias

def reorder(matrix, indices):
    width = matrix.shape[-1]
    blocks = matrix.reshape(-1, STRETCH, width)
    return jnp.take(blocks, indices, axis=0).reshape(-1, width)

def reference(tokens, cotangent, lengths, stretch_order, ln1_gain, ln1_bias, w_qkv, b_qkv, w_out, b_out, ln2_gain, ln2_bias, w_up, b_up, w_down, b_down):
    params = tuple((weight_arg.astype(jnp.float32) for weight_arg in (ln1_gain, ln1_bias, w_qkv, b_qkv, w_out, b_out, ln2_gain, ln2_bias, w_up, b_up, w_down, b_down)))
    stretch_count = tokens.shape[1] // STRETCH
    longest = SEQ_STRETCHES + SEQ_STRETCHES // 2
    stretch_index = jnp.arange(stretch_count, dtype=jnp.int32)
    results = []
    input_grads = []
    totals = [jnp.zeros_like(item) for item in params]
    for micro_idx in range(MICRO):
        seq_lengths = lengths[micro_idx].astype(jnp.int32)
        starts = (jnp.cumsum(seq_lengths) - seq_lengths).astype(jnp.int32)
        restarts = jnp.any(stretch_index[:, None] == starts[None, :], axis=1).astype(jnp.int32)
        seq_ids = (jnp.cumsum(restarts) - 1).astype(jnp.int32)
        offsets = (stretch_index - starts[seq_ids]).astype(jnp.int32)
        positions = (seq_ids * longest + offsets).astype(jnp.int32)
        order_row = stretch_order[micro_idx].astype(jnp.int32)
        inverse = jnp.argsort(order_row).astype(jnp.int32)
        rows_in = reorder(tokens[micro_idx].astype(jnp.float32), order_row)
        grad_in = reorder(cotangent[micro_idx].astype(jnp.float32), order_row)
        output, pullback = jax.vjp(partial(forward, starts, positions), rows_in, params)
        grad_rows, grad_params = pullback(grad_in)
        results.append(reorder(output, inverse).astype(jnp.bfloat16))
        input_grads.append(reorder(grad_rows, inverse).astype(jnp.bfloat16))
        totals = [before + added for before, added in zip(totals, grad_params)]
    return (jnp.stack(results), jnp.stack(input_grads), totals[0], totals[1], totals[2], totals[3][:2 * D], totals[3][2 * D:], totals[4], totals[5], totals[6], totals[7], totals[8], totals[9], totals[10], totals[11])
```

```python
import functools

import jax
import jax.numpy as jnp
from jax import lax
from jax.experimental import pallas as pl
from jax.experimental.pallas import tpu as pltpu
from jax.sharding import PartitionSpec as P

HEADS = 8
HEAD_DIM = 64
STRETCH = 64
LONGEST = 48
CHUNK = 2 * STRETCH
TILE = 2 * CHUNK
PAIRS = HEADS // 2
PAIR = 2 * HEAD_DIM
MODEL = HEADS * HEAD_DIM
BOTH = ("dp", "fsdp")
EPS = 1e-05
VMEM_LIMIT = 60 * 1024 * 1024

f32 = jnp.float32
bf16 = jnp.bfloat16


def nn(a, b):
    return lax.dot_general(a, b, (((1,), (0,)), ((), ())), preferred_element_type=f32)


def nt(a, b):
    return lax.dot_general(a, b, (((1,), (1,)), ((), ())), preferred_element_type=f32)


def tn(a, b):
    return lax.dot_general(a, b, (((0,), (0,)), ((), ())), preferred_element_type=f32)


def lanes(rows, width):
    return lax.broadcasted_iota(jnp.int32, (rows, width), 1)


def sublanes(rows, width):
    return lax.broadcasted_iota(jnp.int32, (rows, width), 0)


def first_head(rows):
    return lanes(rows, PAIR) < HEAD_DIM


def same_head():
    return (sublanes(PAIR, PAIR) // HEAD_DIM) == (lanes(PAIR, PAIR) // HEAD_DIM)


def by_head(x, rows):
    low = first_head(rows)
    zero = jnp.zeros_like(x)
    return jnp.concatenate([jnp.where(low, x, zero), jnp.where(low, zero, x)], axis=0)


def flag(value):
    return value.astype(f32)


def col(pair):
    return slice(pair * PAIR, (pair + 1) * PAIR)


def standardize(x):
    centre = jnp.mean(x, axis=-1, keepdims=True)
    centred = x - centre
    spread = jnp.mean(centred * centred, axis=-1, keepdims=True)
    scale = lax.rsqrt(spread + EPS)
    return centred * scale, scale


def norm_back(upstream, gain, n, scale):
    ug = upstream * gain
    return scale * (
        ug
        - jnp.mean(ug, axis=-1, keepdims=True)
        - n * jnp.mean(ug * n, axis=-1, keepdims=True)
    )


def unpack_state(block, pair):
    part = block[:HEAD_DIM, col(pair)]
    low = first_head(HEAD_DIM)
    zero = jnp.zeros_like(part)
    state = jnp.concatenate([jnp.where(low, part, zero), jnp.where(low, zero, part)], axis=0)
    row = block[HEAD_DIM : HEAD_DIM + 1, col(pair)]
    eye = sublanes(PAIR, PAIR) == lanes(PAIR, PAIR)
    diagonal = jnp.where(eye, row, 0.0)
    ones = jnp.where(same_head(), 1.0, 0.0).astype(bf16)
    high = diagonal.astype(bf16)
    low_part = (diagonal - high.astype(f32)).astype(bf16)
    sums = nn(high, ones) + nn(low_part, ones)
    return jnp.concatenate([state, sums], axis=1)


def pack_state(ref, pair, state, row):
    low = first_head(HEAD_DIM)
    ref[:HEAD_DIM, col(pair)] = jnp.where(low, state[:HEAD_DIM], state[HEAD_DIM:])
    ref[HEAD_DIM : HEAD_DIM + 1, col(pair)] = row
    ref[HEAD_DIM + 1 :, col(pair)] = jnp.zeros((7, PAIR), f32)


def qkv_kernel(
    placing, closing, rows, weight, bias, gain, shift, x_out, normed_out, qkv_out, state_out, acc, sums
):
    step = pl.program_id(0)
    per = TILE // STRETCH

    @pl.when(step == 0)
    def _():
        acc[...] = jnp.zeros_like(acc)
        sums[...] = jnp.zeros_like(sums)

    for i in range(per):
        x_out[i * STRETCH : (i + 1) * STRETCH, :] = rows[placing[step * per + i]]
    x = x_out[...].astype(f32)
    n, _ = standardize(x)
    normed = (n * gain[...] + shift[...]).astype(bf16)
    normed_out[...] = normed
    for part in range(2):
        at = slice(part * MODEL, (part + 1) * MODEL)
        mixed = nn(normed, weight[:, at]) + bias[:, at]
        feature = jnp.where(mixed > 0, mixed + 1.0, jnp.exp(jnp.minimum(mixed, 0.0)))
        qkv_out[:, at] = feature.astype(bf16)
    at = slice(2 * MODEL, 3 * MODEL)
    qkv_out[:, at] = (nn(normed, weight[:, at]) + bias[:, at]).astype(bf16)
    keep = jnp.concatenate(
        [jnp.full((STRETCH, 1), flag(closing[step * per + i]), f32) for i in range(per)], axis=0
    )
    for pair in range(PAIRS):
        k = qkv_out[:, MODEL + pair * PAIR : MODEL + (pair + 1) * PAIR].astype(f32) * keep
        v = qkv_out[:, 2 * MODEL + pair * PAIR : 2 * MODEL + (pair + 1) * PAIR]
        acc[pair] += tn(k.astype(bf16), v)
        sums[:, col(pair)] += jnp.sum(k, axis=0, keepdims=True)

    @pl.when(step == pl.num_programs(0) - 1)
    def _():
        for pair in range(PAIRS):
            pack_state(state_out, pair, acc[pair], sums[:, col(pair)])


def whole(shape):
    zeros = (0,) * len(shape)
    return pl.BlockSpec(shape, lambda i, *_: zeros)


def fixed(shape):
    zeros = (0,) * len(shape)
    return pl.BlockSpec(shape, lambda i, *_: zeros, pipeline_mode=pl.Buffered(1))


def tiled(width, flip=0):
    if flip:
        return pl.BlockSpec((TILE, width), lambda i, *_: (flip - 1 - i, 0))
    return pl.BlockSpec((TILE, width), lambda i, *_: (i, 0))


def params(steps=1):
    return pltpu.CompilerParams(
        dimension_semantics=("arbitrary",) * steps, vmem_limit_bytes=VMEM_LIMIT
    )


def run_qkv(placing, closing, rows, weight, bias, gain, shift):
    stretches, _, width = rows.shape
    count = stretches * STRETCH
    return pl.pallas_call(
        qkv_kernel,
        name="qkv",
        grid_spec=pltpu.PrefetchScalarGridSpec(
            num_scalar_prefetch=2,
            grid=(count // TILE,),
            in_specs=[
                fixed(rows.shape),
                fixed(weight.shape),
                fixed(bias.shape),
                fixed(gain.shape),
                fixed(shift.shape),
            ],
            out_specs=[
                tiled(width),
                tiled(width),
                tiled(3 * MODEL),
                whole((HEAD_DIM + 8, MODEL)),
            ],
            scratch_shapes=[
                pltpu.VMEM((PAIRS, PAIR, PAIR), f32),
                pltpu.VMEM((1, MODEL), f32),
            ],
        ),
        out_shape=[
            jax.ShapeDtypeStruct((count, width), bf16),
            jax.ShapeDtypeStruct((count, width), bf16),
            jax.ShapeDtypeStruct((count, 3 * MODEL), bf16),
            jax.ShapeDtypeStruct((HEAD_DIM + 8, MODEL), f32),
        ],
        compiler_params=params(),
        cost_estimate=pl.CostEstimate(
            flops=2 * count * width * 3 * MODEL, bytes_accessed=8 << 20, transcendentals=count * 1024
        ),
    )(placing, closing, rows, weight, bias, gain, shift)


def causal(second, transposed):
    i = sublanes(CHUNK, 2 * CHUNK)
    j = lanes(CHUNK, 2 * CHUNK) % CHUNK
    if transposed:
        i, j = j, i
    crosses = (i >= STRETCH) & (j < STRETCH)
    return jnp.where(crosses, 1.0 - second, jnp.where(j <= i, 1.0, 0.0))


def mid_kernel(
    placing,
    restart,
    opened,
    x_ref,
    qkv_ref,
    cot_ref,
    inc_ref,
    w_out,
    w_up,
    w_down,
    b_out,
    gain,
    shift,
    b_up,
    b_down,
    result,
    active_out,
    hidden_out,
    normed_out,
    att_out,
    branch_out,
    gn_out,
    gd_out,
    middle_out,
    states_out,
    state_out,
    vec_out,
    cot_out,
    carry,
    back,
    back_sum,
    slope,
    att_scr,
    inv_scr,
):
    step = pl.program_id(0)
    per = TILE // STRETCH

    @pl.when(step == 0)
    def _():
        for pair in range(PAIRS):
            carry[pair] = unpack_state(inc_ref[...], pair)
        back[...] = jnp.zeros_like(back)
        back_sum[...] = jnp.zeros_like(back_sum)
        vec_out[...] = jnp.zeros_like(vec_out)

    block = same_head()
    ones_head = jnp.where(block, 1.0, 0.0).astype(bf16)
    low = first_head(CHUNK)
    one_low = jnp.where(low, 1.0, 0.0).astype(bf16)
    one_high = jnp.where(low, 0.0, 1.0).astype(bf16)
    ones_both = jnp.concatenate([one_low, one_high], axis=0)
    ones_all = jnp.ones((CHUNK, PAIR), bf16)
    wide_block = jnp.concatenate([block, block], axis=1)
    upper = sublanes(CHUNK, PAIR) < STRETCH
    inner = lanes(PAIR, PAIR) % HEAD_DIM
    zero_s = jnp.zeros((PAIR, PAIR), bf16)
    for i in range(per):
        cot_out[i * STRETCH : (i + 1) * STRETCH, :] = cot_ref[placing[step * per + i]]

    for chunk in range(TILE // CHUNK):
        rows = slice(chunk * CHUNK, (chunk + 1) * CHUNK)
        r0 = flag(restart[step * per + 2 * chunk])
        r1 = flag(restart[step * per + 2 * chunk + 1])
        mask = causal(r1, False)
        keep_low = jnp.where(upper, 1.0, 1.0 - r1)
        keep_key = jnp.where(upper, 1.0 - r1, 1.0)
        for pair in range(PAIRS):
            q = qkv_ref[rows, pair * PAIR : (pair + 1) * PAIR]
            k = qkv_ref[rows, MODEL + pair * PAIR : MODEL + (pair + 1) * PAIR]
            v = qkv_ref[rows, 2 * MODEL + pair * PAIR : 2 * MODEL + (pair + 1) * PAIR]
            state = carry[pair] * (1.0 - r0)
            state_b = state.astype(bf16)
            state_low = (state - state_b.astype(f32)).astype(bf16)
            states_out[chunk, pair * PAIR : (pair + 1) * PAIR, :] = jnp.concatenate(
                [
                    state_b[:, :PAIR],
                    jnp.where(
                        inner < 2, state_b[:, PAIR:], jnp.where(inner == 2, state_low[:, PAIR:], zero_s)
                    ),
                    state_low[:, :PAIR],
                ],
                axis=1,
            )
            mixing = nt(q, by_head(k, CHUNK)) * mask
            values = jnp.concatenate([by_head(v, CHUNK), ones_both], axis=1)
            out = nn(mixing.astype(bf16), values)
            out = out + nn((q.astype(f32) * keep_low).astype(bf16), state_b)
            inv = 1.0 / out[:, PAIR:]
            att = out[:, :PAIR] * inv
            att_scr[rows, col(pair)] = att
            inv_scr[rows, col(pair)] = inv
            att_out[rows, col(pair)] = att.astype(bf16)
            k_keep = (k.astype(f32) * keep_key).astype(bf16)
            added = tn(k_keep, jnp.concatenate([v, ones_all], axis=1))
            carry[pair] = state * (1.0 - r1) + jnp.where(wide_block, added, 0.0)

    middle = x_ref[...].astype(f32) + nn(att_out[...], w_out[...]) + b_out[...]
    n, scale = standardize(middle)
    normed = (n * gain[...] + shift[...]).astype(bf16)
    normed_out[...] = normed
    ff = w_up.shape[1]
    total = middle + b_down[...]
    for part in range(ff // MODEL):
        at = slice(part * MODEL, (part + 1) * MODEL)
        u = nn(normed, w_up[:, at]) + b_up[:, at]
        u2 = u * u
        t = jnp.tanh(u * (0.7978845608028654 + 0.035677408136300125 * u2))
        half = 0.5 + 0.5 * t
        act = (u * half).astype(bf16)
        active_out[:, at] = act
        rise = 0.7978845608028654 + 0.10703222440890037 * u2
        slope[:, at] = (half + 0.5 * u * (1.0 - t * t) * rise).astype(bf16)
        total = total + nn(act, w_down[at, :])
    total = total.astype(bf16)
    for i in range(per):
        result[placing[step * per + i]] = total[i * STRETCH : (i + 1) * STRETCH, :]

    cot = cot_out[...]
    up_grad = jnp.zeros((TILE, MODEL), f32)
    for part in range(ff // MODEL):
        at = slice(part * MODEL, (part + 1) * MODEL)
        g = (nt(cot, w_down[at, :]) * slope[:, at].astype(f32)).astype(bf16)
        hidden_out[:, at] = g
        vec_out[0:1, at] += jnp.sum(g.astype(f32), axis=0, keepdims=True)
        up_grad = up_grad + nt(g, w_up[:, at])
    cot_f = cot.astype(f32)
    vec_out[1:2, :MODEL] += jnp.sum(up_grad * n, axis=0, keepdims=True)
    vec_out[1:2, MODEL : 2 * MODEL] += jnp.sum(up_grad, axis=0, keepdims=True)
    vec_out[1:2, 3 * MODEL : 4 * MODEL] += jnp.sum(cot_f, axis=0, keepdims=True)
    grad_middle = cot_f + norm_back(up_grad, gain[...], n, scale)
    middle_out[...] = grad_middle
    branch = grad_middle.astype(bf16)
    branch_out[...] = branch
    vec_out[1:2, 2 * MODEL : 3 * MODEL] += jnp.sum(branch.astype(f32), axis=0, keepdims=True)
    grad_att = nt(branch, w_out[...])
    lane = lanes(CHUNK, PAIR) % HEAD_DIM
    for chunk in range(TILE // CHUNK):
        rows = slice(chunk * CHUNK, (chunk + 1) * CHUNK)
        o0 = flag(opened[step * per + 2 * chunk])
        o1 = flag(opened[step * per + 2 * chunk + 1])
        keep = jnp.where(upper, o0, o1)
        for pair in range(PAIRS):
            inv = inv_scr[rows, col(pair)]
            gn = (grad_att[rows, col(pair)].astype(bf16).astype(f32) * inv).astype(bf16)
            product = gn.astype(f32) * att_scr[rows, col(pair)]
            high = product.astype(bf16)
            low_part = (product - high.astype(f32)).astype(bf16)
            gd = -(nn(high, ones_head) + nn(low_part, ones_head))
            gd_high = gd.astype(bf16)
            gd_low = (gd - gd_high.astype(f32)).astype(bf16)
            zero = jnp.zeros_like(gd_high)
            gn_out[rows, col(pair)] = gn
            gd_out[rows, col(pair)] = jnp.where(
                (lane == 0) | (lane == 2), gd_high, jnp.where(lane == 1, gd_low, zero)
            )
            q = qkv_ref[rows, pair * PAIR : (pair + 1) * PAIR].astype(f32) * keep
            back[pair] += tn(q.astype(bf16), gn)
            back_sum[:, col(pair)] += jnp.sum(q * gd, axis=0, keepdims=True)

    @pl.when(step == pl.num_programs(0) - 1)
    def _():
        for pair in range(PAIRS):
            pack_state(state_out, pair, back[pair], back_sum[:, col(pair)])


def run_mid(placing, restart, opened, x, qkv, cot, inc, w_out, w_up, w_down, vectors):
    count, width = x.shape
    ff = w_up.shape[1]
    stretches = count // STRETCH
    chunks = count // CHUNK
    b_out, gain, shift, b_up, b_down = vectors
    return pl.pallas_call(
        mid_kernel,
        name="middle",
        grid_spec=pltpu.PrefetchScalarGridSpec(
            num_scalar_prefetch=3,
            grid=(count // TILE,),
            in_specs=[
                tiled(width),
                tiled(3 * MODEL),
                fixed(cot.shape),
                fixed(inc.shape),
                fixed(w_out.shape),
                fixed(w_up.shape),
                fixed(w_down.shape),
                fixed(b_out.shape),
                fixed(gain.shape),
                fixed(shift.shape),
                fixed(b_up.shape),
                fixed(b_down.shape),
            ],
            out_specs=[
                whole((stretches, STRETCH, width)),
                tiled(ff),
                tiled(ff),
                tiled(width),
                tiled(MODEL),
                tiled(width),
                tiled(MODEL),
                tiled(MODEL),
                tiled(width),
                pl.BlockSpec((TILE // CHUNK, MODEL, 3 * PAIR), lambda i, *_: (i, 0, 0)),
                whole((HEAD_DIM + 8, MODEL)),
                whole((8, ff)),
                tiled(width),
            ],
            scratch_shapes=[
                pltpu.VMEM((PAIRS, PAIR, 2 * PAIR), f32),
                pltpu.VMEM((PAIRS, PAIR, PAIR), f32),
                pltpu.VMEM((1, MODEL), f32),
                pltpu.VMEM((TILE, ff), bf16),
                pltpu.VMEM((TILE, MODEL), f32),
                pltpu.VMEM((TILE, MODEL), f32),
            ],
        ),
        out_shape=[
            jax.ShapeDtypeStruct((stretches, STRETCH, width), bf16),
            jax.ShapeDtypeStruct((count, ff), bf16),
            jax.ShapeDtypeStruct((count, ff), bf16),
            jax.ShapeDtypeStruct((count, width), bf16),
            jax.ShapeDtypeStruct((count, MODEL), bf16),
            jax.ShapeDtypeStruct((count, width), bf16),
            jax.ShapeDtypeStruct((count, MODEL), bf16),
            jax.ShapeDtypeStruct((count, MODEL), bf16),
            jax.ShapeDtypeStruct((count, width), f32),
            jax.ShapeDtypeStruct((chunks, MODEL, 3 * PAIR), bf16),
            jax.ShapeDtypeStruct((HEAD_DIM + 8, MODEL), f32),
            jax.ShapeDtypeStruct((8, ff), f32),
            jax.ShapeDtypeStruct((count, width), bf16),
        ],
        compiler_params=params(),
        cost_estimate=pl.CostEstimate(
            flops=2 * count * width * (2 * MODEL + 4 * ff) + (4 << 30),
            bytes_accessed=28 << 20,
            transcendentals=count * ff,
        ),
    )(placing, restart, opened, x, qkv, cot, inc, w_out, w_up, w_down, b_out, gain, shift, b_up, b_down)


def back_kernel(
    placing,
    restart,
    x_ref,
    qkv_ref,
    gn_ref,
    gd_ref,
    middle_ref,
    states_ref,
    inc_ref,
    weight,
    gain,
    grad_rows,
    mixed_out,
    vec_out,
    carry,
):
    step = pl.program_id(0)
    per = TILE // STRETCH
    tile = pl.num_programs(0) - 1 - step

    @pl.when(step == 0)
    def _():
        for pair in range(PAIRS):
            carry[pair] = unpack_state(inc_ref[...], pair)
        vec_out[...] = jnp.zeros_like(vec_out)

    block = same_head()
    wide_block = jnp.concatenate([block, block], axis=1)
    upper = sublanes(CHUNK, PAIR) < STRETCH
    lane = lanes(CHUNK, PAIR)
    inner = lane % HEAD_DIM
    marks = jnp.where(inner < 2, 1.0, 0.0).astype(bf16)
    mark_low = jnp.where(lane < 2, 1.0, 0.0).astype(bf16)
    mark_high = jnp.where((lane == HEAD_DIM) | (lane == HEAD_DIM + 1), 1.0, 0.0).astype(bf16)
    marks_both = jnp.concatenate([mark_low, mark_high], axis=0)
    ones_head = jnp.where(block, 1.0, 0.0).astype(bf16)

    for chunk in reversed(range(TILE // CHUNK)):
        rows = slice(chunk * CHUNK, (chunk + 1) * CHUNK)
        r0 = flag(restart[tile * per + 2 * chunk])
        r1 = flag(restart[tile * per + 2 * chunk + 1])
        r2 = flag(restart[tile * per + 2 * chunk + 2])
        mask = causal(r1, False)
        mask_t = causal(r1, True)
        keep_low = jnp.where(upper, 1.0, 1.0 - r1)
        keep_key = jnp.where(upper, 1.0 - r1, 1.0)
        for pair in range(PAIRS):
            q = qkv_ref[rows, pair * PAIR : (pair + 1) * PAIR]
            k = qkv_ref[rows, MODEL + pair * PAIR : MODEL + (pair + 1) * PAIR]
            v = qkv_ref[rows, 2 * MODEL + pair * PAIR : 2 * MODEL + (pair + 1) * PAIR]
            gn = gn_ref[rows, col(pair)]
            gdx = gd_ref[rows, col(pair)]
            state = states_ref[chunk, pair * PAIR : (pair + 1) * PAIR, :]
            grown = carry[pair] * (1.0 - r2)
            grown_s = grown[:, :PAIR].astype(bf16)
            grown_low = (grown[:, :PAIR] - grown_s.astype(f32)).astype(bf16)
            grown_z = grown[:, PAIR:]
            z_high = grown_z.astype(bf16)
            z_low = (grown_z - z_high.astype(f32)).astype(bf16)
            zero = jnp.zeros_like(z_high)
            grown_z = jnp.where(inner == 0, z_high, jnp.where(inner == 1, z_low, zero))
            k2 = by_head(k, CHUNK)
            q2 = by_head(q, CHUNK)
            v2 = by_head(v, CHUNK)
            gn2 = by_head(gn, CHUNK)
            gd2 = by_head(gdx, CHUNK)
            both = jnp.concatenate([gn, gdx], axis=1)
            mixing_t = (nt(k, q2) * mask_t).astype(bf16)
            g_mix = (nt(both, jnp.concatenate([v2, marks_both], axis=1)) * mask).astype(bf16)
            v_marks = jnp.concatenate([v, marks], axis=1)
            g_mix_t = (nt(v_marks, jnp.concatenate([gn2, gd2], axis=1)) * mask_t).astype(bf16)
            dq = nn(g_mix, k2) + (nt(both, state[:, : 2 * PAIR]) + nt(gn, state[:, 2 * PAIR :])) * keep_low
            grown_x = jnp.concatenate([grown_s, grown_z], axis=1)
            dk = nn(g_mix_t, q2) + (nt(v_marks, grown_x) + nt(v, grown_low)) * keep_key
            dv = nn(mixing_t, gn2) + nn(k, grown_s) * keep_key
            q_keep = (q.astype(f32) * keep_low).astype(bf16)
            added_s = tn(q_keep, gn)
            gd_all = nn(gdx * marks, ones_head)
            added_z = jnp.sum(q.astype(f32) * keep_low * gd_all, axis=0, keepdims=True)
            eye = sublanes(PAIR, PAIR) == lane
            diagonal = jnp.where(eye, added_z, 0.0)
            d_high = diagonal.astype(bf16)
            d_low = (diagonal - d_high.astype(f32)).astype(bf16)
            added_z = nn(d_high, ones_head) + nn(d_low, ones_head)
            added = jnp.concatenate([jnp.where(block, added_s, 0.0), added_z], axis=1)
            carry[pair] = (grown * (1.0 - r1) + added) * (1.0 - r0)
            mixed_out[rows, pair * PAIR : (pair + 1) * PAIR] = (
                dq * jnp.minimum(q.astype(f32), 1.0)
            ).astype(bf16)
            mixed_out[rows, MODEL + pair * PAIR : MODEL + (pair + 1) * PAIR] = (
                dk * jnp.minimum(k.astype(f32), 1.0)
            ).astype(bf16)
            mixed_out[rows, 2 * MODEL + pair * PAIR : 2 * MODEL + (pair + 1) * PAIR] = dv.astype(bf16)

    mixed = mixed_out[...]
    vec_out[0:1, :] += jnp.sum(mixed.astype(f32), axis=0, keepdims=True)
    upstream = nt(mixed, weight[...])
    n, scale = standardize(x_ref[...].astype(f32))
    vec_out[1:2, :MODEL] += jnp.sum(upstream * n, axis=0, keepdims=True)
    vec_out[1:2, MODEL : 2 * MODEL] += jnp.sum(upstream, axis=0, keepdims=True)
    total = (middle_ref[...] + norm_back(upstream, gain[...], n, scale)).astype(bf16)
    for i in range(per):
        grad_rows[placing[tile * per + i]] = total[i * STRETCH : (i + 1) * STRETCH, :]


def run_back(placing, restart, x, qkv, gn, gd, middle, states, inc, weight, gain):
    count, width = x.shape
    stretches = count // STRETCH
    steps = count // TILE
    return pl.pallas_call(
        back_kernel,
        name="back",
        grid_spec=pltpu.PrefetchScalarGridSpec(
            num_scalar_prefetch=2,
            grid=(steps,),
            in_specs=[
                tiled(width, steps),
                tiled(3 * MODEL, steps),
                tiled(MODEL, steps),
                tiled(MODEL, steps),
                tiled(width, steps),
                pl.BlockSpec(
                    (TILE // CHUNK, MODEL, 3 * PAIR), lambda i, *_: (steps - 1 - i, 0, 0)
                ),
                fixed(inc.shape),
                fixed(weight.shape),
                fixed(gain.shape),
            ],
            out_specs=[
                whole((stretches, STRETCH, width)),
                tiled(3 * MODEL, steps),
                whole((8, 3 * MODEL)),
            ],
            scratch_shapes=[pltpu.VMEM((PAIRS, PAIR, 2 * PAIR), f32)],
        ),
        out_shape=[
            jax.ShapeDtypeStruct((stretches, STRETCH, width), bf16),
            jax.ShapeDtypeStruct((count, 3 * MODEL), bf16),
            jax.ShapeDtypeStruct((8, 3 * MODEL), f32),
        ],
        compiler_params=params(),
        cost_estimate=pl.CostEstimate(
            flops=2 * count * width * 3 * MODEL + (6 << 30), bytes_accessed=14 << 20, transcendentals=0
        ),
    )(placing, restart, x, qkv, gn, gd, middle, states, inc, weight, gain)


def permute_kernel(slot, source, target, *, inverse):
    group = pl.program_id(0)
    for i in range(source.shape[1]):
        place = slot[group, i]
        if inverse:
            target[0, i] = source[0, place]
        else:
            target[0, place] = source[0, i]


def run_permute(slot, blocks, inverse):
    shape = (1,) + blocks.shape[1:]
    spec = pl.BlockSpec(shape, lambda i, *_: (i, 0, 0, 0))
    return pl.pallas_call(
        functools.partial(permute_kernel, inverse=inverse),
        name="permute",
        grid_spec=pltpu.PrefetchScalarGridSpec(
            num_scalar_prefetch=1,
            grid=(blocks.shape[0],),
            in_specs=[spec],
            out_specs=spec,
        ),
        out_shape=jax.ShapeDtypeStruct(blocks.shape, blocks.dtype),
        compiler_params=params(),
        cost_estimate=pl.CostEstimate(
            flops=0, bytes_accessed=2 * blocks.size * 2, transcendentals=0
        ),
    )(slot, blocks)


def index_tables(lengths, stretch_order, count):
    fsdp = lax.axis_size("fsdp")
    groups = lax.axis_size("dp")
    device = lax.axis_index(BOTH)
    base = device * count
    within = jnp.arange(count, dtype=jnp.int32)
    mine = base + within
    place = jnp.arange(stretch_order.shape[1], dtype=jnp.int32)
    here = place[None, None, :]
    landing = jnp.sum(
        jnp.where(stretch_order[:, None, :] == mine[None, :, None], here, 0), axis=-1
    )
    slot = jnp.sum((landing[:, None, :] < landing[:, :, None]).astype(jnp.int32), axis=-1)
    arrival = jnp.sum(
        jnp.where(here == mine[None, :, None], stretch_order[:, None, :], 0), axis=-1
    )
    source = arrival // count // fsdp
    ahead = (source[:, None, :] == source[:, :, None]) & (
        within[None, None, :] < within[None, :, None]
    )
    placing = source * (count // groups) + jnp.sum(ahead.astype(jnp.int32), axis=-1)
    index = jnp.arange(lengths.shape[1], dtype=jnp.int32)
    starts = jnp.sum(
        jnp.where(index[None, None, :] < index[None, :, None], lengths[:, None, :], 0), axis=-1
    )
    edge = base + jnp.arange(count + 1, dtype=jnp.int32)
    restart = jnp.any(starts[:, None, :] == edge[None, :, None], axis=-1).astype(jnp.int32)
    restart = jnp.where(edge[None, :] == stretch_order.shape[1], 1, restart)
    opened = 1 - jnp.any(
        (starts[:, None, :] >= base) & (starts[:, None, :] <= mine[None, :, None]), axis=-1
    ).astype(jnp.int32)
    last = base + count - 1
    closing = 1 - jnp.any(
        (starts[:, None, :] > mine[None, :, None]) & (starts[:, None, :] <= last), axis=-1
    ).astype(jnp.int32)
    hops = -(-(LONGEST - 1) // count)
    hop = jnp.arange(hops, dtype=jnp.int32)
    reach_back = base - 1 - hop * count
    from_before = 1.0 - jnp.any(
        (starts[:, None, :] > reach_back[None, :, None]) & (starts[:, None, :] <= base), axis=-1
    ).astype(f32)
    reach_on = base + (hop + 1) * count
    from_after = 1.0 - jnp.any(
        (starts[:, None, :] > last) & (starts[:, None, :] <= reach_on[None, :, None]), axis=-1
    ).astype(f32)
    return slot, placing, restart, opened, closing, from_before, from_after


def exchange(states, weights, forward):
    size = lax.axis_size("fsdp")
    total = None
    for hop in range(weights.shape[1]):
        step = hop + 1
        pairs = [
            (i, i + step) if forward else (i + step, i) for i in range(size - step)
        ]
        if not pairs:
            continue
        got = lax.ppermute(states, "fsdp", pairs).astype(f32) * weights[:, hop, None, None]
        total = got if total is None else total + got
    if total is None:
        total = jnp.zeros(states.shape, f32)
    return total


def halving_stages():
    stages = []
    dp, fsdp = lax.axis_size("dp"), lax.axis_size("fsdp")
    if dp > 1:
        stages.append(("dp", 1))
    bit = 1
    while bit < fsdp:
        stages.append(("fsdp", bit))
        bit *= 2
    bit = 2
    while bit < dp:
        stages.append(("dp", bit))
        bit *= 2
    return stages


def bit_dims():
    dims = []
    for axis in BOTH:
        bit = lax.axis_size(axis) // 2
        while bit:
            dims.append((axis, bit))
            bit //= 2
    return dims


def scatter_sum(x):
    dims = bit_dims()
    x = x.reshape((2,) * len(dims) + x.shape[1:])
    for axis, bit in halving_stages():
        dim = dims.index((axis, bit))
        size = lax.axis_size(axis)
        mine = (lax.axis_index(axis) // bit) % 2
        send = lax.dynamic_index_in_dim(x, 1 - mine, dim, True)
        keep = lax.dynamic_index_in_dim(x, mine, dim, True)
        got = lax.ppermute(send, axis, [(i, i ^ bit) for i in range(size)])
        x = (keep.astype(f32) + got.astype(f32)).astype(x.dtype)
    return x.reshape(x.shape[len(dims) :]).astype(f32)


def gather_all(x):
    dims = bit_dims()
    x = x.reshape((1,) * len(dims) + x.shape)
    for axis, bit in reversed(halving_stages()):
        dim = dims.index((axis, bit))
        size = lax.axis_size(axis)
        mine = (lax.axis_index(axis) // bit) % 2
        got = lax.ppermute(x, axis, [(i, i ^ bit) for i in range(size)])
        first = jnp.where(mine == 0, x, got)
        second = jnp.where(mine == 0, got, x)
        x = jnp.concatenate([first, second], axis=dim)
    return x.reshape((-1,) + x.shape[len(dims) + 1 :])


def scatter_all(x):
    return lax.psum_scatter(x, BOTH, scatter_dimension=0, tiled=True)


def to_dp(blocks):
    return lax.all_to_all(blocks, "dp", split_axis=0, concat_axis=0, tiled=True)


def body(
    tokens,
    cotangent,
    lengths,
    stretch_order,
    ln1_gain,
    ln1_bias,
    w_qkv,
    b_qkv,
    w_out,
    b_out,
    ln2_gain,
    ln2_bias,
    w_up,
    b_up,
    w_down,
    b_down,
):
    micro, rows, width = tokens.shape
    count = rows // STRETCH
    devices = lax.axis_size(BOTH)
    slot, placing, restart, opened, closing, from_before, from_after = index_tables(
        lengths, stretch_order, count
    )
    sent_rows = run_permute(slot, tokens.reshape(micro, count, STRETCH, width), False)
    sent_grads = run_permute(slot, cotangent.reshape(micro, count, STRETCH, width), False)
    moved = [to_dp(sent_rows[m]) for m in range(micro)]
    cots = [to_dp(sent_grads[m]) for m in range(micro)]
    small = (ln1_gain, ln1_bias, b_qkv, b_out, ln2_gain, ln2_bias, b_up, b_down)
    packed = gather_all(jnp.concatenate(small).reshape(1, -1))
    vectors, at = [], 0
    for item in small:
        size = item.shape[0]
        vectors.append(packed[:, at : at + size].reshape(1, -1).astype(f32))
        at += size
    gain_one, shift_one, bias_qkv, bias_out, gain_two, shift_two, bias_up, bias_down = vectors
    qkv_all = gather_all(w_qkv)
    out_all = gather_all(w_out)
    up_all = gather_all(w_up)
    down_all = gather_all(w_down)

    firsts = [
        run_qkv(placing[m], closing[m], moved[m], qkv_all, bias_qkv, gain_one, shift_one)
        for m in range(micro)
    ]
    incoming = exchange(jnp.stack([f[3] for f in firsts]), from_before, True)
    mids = [
        run_mid(
            placing[m],
            restart[m],
            opened[m],
            firsts[m][0],
            firsts[m][2],
            cots[m],
            incoming[m],
            out_all,
            up_all,
            down_all,
            (bias_out, gain_two, shift_two, bias_up, bias_down),
        )
        for m in range(micro)
    ]
    outgoing = exchange(jnp.stack([f[10] for f in mids]), from_after, False)
    backs = [
        run_back(
            placing[m],
            restart[m],
            firsts[m][0],
            firsts[m][2],
            mids[m][6],
            mids[m][7],
            mids[m][8],
            mids[m][9],
            outgoing[m],
            qkv_all,
            gain_one,
        )
        for m in range(micro)
    ]
    home = jnp.stack([to_dp(mids[m][0]) for m in range(micro)])
    home_grad = jnp.stack([to_dp(backs[m][0]) for m in range(micro)])
    result = run_permute(slot, home, True).reshape(micro, rows, width)
    input_grad = run_permute(slot, home_grad, True).reshape(micro, rows, width)

    def summed(pairs):
        total = None
        for left, right in pairs:
            part = tn(left, right)
            total = part if total is None else total + part
        return total

    def owned(total):
        return scatter_sum(total.astype(bf16).reshape(devices, -1, total.shape[1]))

    grad_up = owned(summed([(mids[m][3], mids[m][2]) for m in range(micro)]))
    grad_down = owned(summed([(mids[m][1], mids[m][12]) for m in range(micro)]))
    grad_out = owned(summed([(mids[m][4], mids[m][5]) for m in range(micro)]))
    grad_qkv = owned(summed([(firsts[m][1], backs[m][1]) for m in range(micro)]))
    vec_mid = sum(mids[m][11] for m in range(micro))
    vec_back = sum(backs[m][2] for m in range(micro))
    vec = (
        vec_back[1, :MODEL],
        vec_back[1, MODEL : 2 * MODEL],
        vec_back[0, : 2 * MODEL],
        vec_back[0, 2 * MODEL :],
        vec_mid[1, 2 * MODEL : 3 * MODEL],
        vec_mid[1, :MODEL],
        vec_mid[1, MODEL : 2 * MODEL],
        vec_mid[0],
        vec_mid[1, 3 * MODEL :],
    )
    bundle = scatter_all(
        jnp.concatenate([item.reshape(devices, -1) for item in vec], axis=1)
    ).reshape(-1)
    owned_vec, at = [], 0
    for item in vec:
        size = item.shape[0] // devices
        owned_vec.append(bundle[at : at + size])
        at += size
    g_gain1, g_bias1, g_qk, g_value, g_bout, g_gain2, g_bias2, g_bup, g_bdown = owned_vec
    return (
        result,
        input_grad,
        g_gain1,
        g_bias1,
        grad_qkv,
        g_qk,
        g_value,
        grad_out,
        g_bout,
        g_gain2,
        g_bias2,
        grad_up,
        g_bup,
        grad_down,
        g_bdown,
    )


def solution(mesh):
    rows = P(None, BOTH, None)
    vector = P(BOTH)
    matrix = P(BOTH, None)
    in_specs = (
        rows, rows, P(), P(), vector, vector, matrix, vector, matrix, vector, vector, vector,
        matrix, vector, matrix, vector,
    )
    out_specs = (
        rows, rows, vector, vector, matrix, vector, vector, matrix, vector, vector, vector,
        matrix, vector, matrix, vector,
    )
    return jax.shard_map(body, mesh=mesh, in_specs=in_specs, out_specs=out_specs, check_vma=False)
```

```python
import functools

import jax
import jax.numpy as jnp
from jax import lax
from jax.experimental import pallas as pl
from jax.experimental.pallas import tpu as pltpu
from jax.sharding import PartitionSpec as P

HEADS = 8
HEAD_DIM = 64
STRETCH = 64
LONGEST = 48
CHUNK = 2 * STRETCH
TILE = 4 * CHUNK
PAIRS = HEADS // 2
PAIR = 2 * HEAD_DIM
MODEL = HEADS * HEAD_DIM
BOTH = ("dp", "fsdp")
EPS = 1e-05
VMEM_LIMIT = 60 * 1024 * 1024

f32 = jnp.float32
bf16 = jnp.bfloat16


def nn(a, b):
    return lax.dot_general(a, b, (((1,), (0,)), ((), ())), preferred_element_type=f32)


def nt(a, b):
    return lax.dot_general(a, b, (((1,), (1,)), ((), ())), preferred_element_type=f32)


def tn(a, b):
    return lax.dot_general(a, b, (((0,), (0,)), ((), ())), preferred_element_type=f32)


def lanes(rows, width):
    return lax.broadcasted_iota(jnp.int32, (rows, width), 1)


def sublanes(rows, width):
    return lax.broadcasted_iota(jnp.int32, (rows, width), 0)


def first_head(rows):
    return lanes(rows, PAIR) < HEAD_DIM


def same_head():
    return (sublanes(PAIR, PAIR) // HEAD_DIM) == (lanes(PAIR, PAIR) // HEAD_DIM)


def by_head(x, rows):
    low = first_head(rows)
    zero = jnp.zeros_like(x)
    return jnp.concatenate([jnp.where(low, x, zero), jnp.where(low, zero, x)], axis=0)


def flag(value):
    return value.astype(f32)


def col(pair):
    return slice(pair * PAIR, (pair + 1) * PAIR)


def standardize(x):
    centre = jnp.mean(x, axis=-1, keepdims=True)
    centred = x - centre
    spread = jnp.mean(centred * centred, axis=-1, keepdims=True)
    scale = lax.rsqrt(spread + EPS)
    return centred * scale, scale


def norm_back(upstream, gain, n, scale):
    ug = upstream * gain
    return scale * (
        ug
        - jnp.mean(ug, axis=-1, keepdims=True)
        - n * jnp.mean(ug * n, axis=-1, keepdims=True)
    )


def unpack_state(block, pair):
    part = block[:HEAD_DIM, col(pair)]
    low = first_head(HEAD_DIM)
    zero = jnp.zeros_like(part)
    state = jnp.concatenate([jnp.where(low, part, zero), jnp.where(low, zero, part)], axis=0)
    row = block[HEAD_DIM : HEAD_DIM + 1, col(pair)]
    eye = sublanes(PAIR, PAIR) == lanes(PAIR, PAIR)
    diagonal = jnp.where(eye, row, 0.0)
    ones = jnp.where(same_head(), 1.0, 0.0).astype(bf16)
    high = diagonal.astype(bf16)
    low_part = (diagonal - high.astype(f32)).astype(bf16)
    sums = nn(high, ones) + nn(low_part, ones)
    return jnp.concatenate([state, sums], axis=1)


def pack_state(ref, pair, state, row):
    low = first_head(HEAD_DIM)
    ref[0, :HEAD_DIM, col(pair)] = jnp.where(low, state[:HEAD_DIM], state[HEAD_DIM:])
    ref[0, HEAD_DIM : HEAD_DIM + 1, col(pair)] = row
    ref[0, HEAD_DIM + 1 :, col(pair)] = jnp.zeros((7, PAIR), f32)


def pick(ref, place):
    per = ref.shape[2]
    return ref[lax.div(place, per), 0, lax.rem(place, per)]


def put(ref, place, value):
    per = ref.shape[2]
    ref[lax.div(place, per), 0, lax.rem(place, per)] = value


def group_spec(shape, first):
    block = (shape[0], 1) + tuple(shape[2:])
    return pl.BlockSpec(block, lambda i, *_: (0, first + i, 0, 0, 0))


def fixed(shape):
    zeros = (0,) * len(shape)
    return pl.BlockSpec(tuple(shape), lambda *_: zeros, pipeline_mode=pl.Buffered(1))


def member_spec(first=0):
    return pl.BlockSpec((1, HEAD_DIM + 8, MODEL), lambda i, *_: (first + i, 0, 0))


def tile_spec(width, tiles, reverse=False):
    if reverse:
        return pl.BlockSpec((TILE, width), lambda i, t, *_: (i * tiles + tiles - 1 - t, 0))
    return pl.BlockSpec((TILE, width), lambda i, t, *_: (i * tiles + t, 0))


def states_spec(tiles, reverse=False):
    block = (TILE // CHUNK, MODEL, 3 * PAIR)
    if reverse:
        return pl.BlockSpec(block, lambda i, t, *_: (i * tiles + tiles - 1 - t, 0, 0))
    return pl.BlockSpec(block, lambda i, t, *_: (i * tiles + t, 0, 0))


def params():
    return pltpu.CompilerParams(
        dimension_semantics=("arbitrary", "arbitrary"), vmem_limit_bytes=VMEM_LIMIT
    )


ANYWHERE = pl.BlockSpec(memory_space=pl.ANY)


def featured(mixed):
    return jnp.where(mixed > 0, mixed + 1.0, jnp.exp(jnp.minimum(mixed, 0.0))).astype(bf16)


def state_kernel(placing, closing, rows, weight, bias, gain, shift, state_out, x_scr, acc, sums):
    micro, step = pl.program_id(0), pl.program_id(1)
    per = TILE // STRETCH

    @pl.when(step == 0)
    def _():
        acc[...] = jnp.zeros_like(acc)
        sums[...] = jnp.zeros_like(sums)

    for i in range(per):
        x_scr[i * STRETCH : (i + 1) * STRETCH, :] = pick(rows, placing[micro, step * per + i])
    n, _ = standardize(x_scr[...].astype(f32))
    normed = (n * gain[...] + shift[...]).astype(bf16)
    keep = jnp.concatenate(
        [jnp.full((STRETCH, 1), flag(closing[micro, step * per + i]), f32) for i in range(per)],
        axis=0,
    )
    at = slice(MODEL, 2 * MODEL)
    keys = featured(nn(normed, weight[:, at]) + bias[:, at]).astype(f32) * keep
    sums[...] += jnp.sum(keys, axis=0, keepdims=True)
    keys = keys.astype(bf16)
    at = slice(2 * MODEL, 3 * MODEL)
    values = (nn(normed, weight[:, at]) + bias[:, at]).astype(bf16)
    for pair in range(PAIRS):
        acc[pair] += tn(keys[:, col(pair)], values[:, col(pair)])

    @pl.when(step == pl.num_programs(1) - 1)
    def _():
        for pair in range(PAIRS):
            pack_state(state_out, pair, acc[pair], sums[:, col(pair)])


def run_state(placing, closing, rows, weight, bias, gain, shift):
    micro, count = placing.shape
    width = rows.shape[-1]
    tiles = count * STRETCH // TILE
    return pl.pallas_call(
        state_kernel,
        name="end_state",
        grid_spec=pltpu.PrefetchScalarGridSpec(
            num_scalar_prefetch=2,
            grid=(micro, tiles),
            in_specs=[
                group_spec(rows.shape, 0),
                fixed(weight.shape),
                fixed(bias.shape),
                fixed(gain.shape),
                fixed(shift.shape),
            ],
            out_specs=member_spec(),
            scratch_shapes=[
                pltpu.VMEM((TILE, width), bf16),
                pltpu.VMEM((PAIRS, PAIR, PAIR), f32),
                pltpu.VMEM((1, MODEL), f32),
            ],
        ),
        out_shape=jax.ShapeDtypeStruct((micro, HEAD_DIM + 8, MODEL), f32),
        compiler_params=params(),
        cost_estimate=pl.CostEstimate(
            flops=4 * micro * count * STRETCH * width * MODEL,
            bytes_accessed=5 << 20,
            transcendentals=micro * count * STRETCH * MODEL,
        ),
    )(placing, closing, rows, weight, bias, gain, shift)


def causal(second, transposed):
    i = sublanes(CHUNK, 2 * CHUNK)
    j = lanes(CHUNK, 2 * CHUNK) % CHUNK
    if transposed:
        i, j = j, i
    crosses = (i >= STRETCH) & (j < STRETCH)
    return jnp.where(crosses, 1.0 - second, jnp.where(j <= i, 1.0, 0.0))


def mid_kernel(
    placing,
    restart,
    opened,
    owner,
    _,
    rows_ref,
    cot_ref,
    inc_ref,
    w_qkv,
    w_out,
    w_up,
    w_down,
    b_qkv,
    gain_one,
    shift_one,
    b_out,
    gain,
    shift,
    b_up,
    b_down,
    *refs,
    first,
    resumes,
    final,
):
    before, refs = (refs[:3], refs[3:]) if resumes else ((), refs)
    result, qkv_ref, branch_out, gn_out, gd_out, states_out, state_out, vec_out = refs[:8]
    refs = refs[8:]
    if final:
        keep_out, send_out, acc_up, acc_down, acc_out, turned = refs[:6]
        refs = refs[6:]
    else:
        acc_up, acc_down, acc_out = refs[:3]
        refs = refs[3:]
    carry, back, back_sum, att_scr, inv_scr, att_b, x_scr, cot_scr = refs[:8]
    sems = refs[8] if resumes else None
    member, step = pl.program_id(0), pl.program_id(1)
    micro = first + member
    per = TILE // STRETCH
    opening = (member == 0) & (step == 0)

    @pl.when(opening)
    def _():
        vec_out[...] = jnp.zeros_like(vec_out)
        if resumes:
            for n, (source, target) in enumerate(zip(before, (acc_up, acc_down, acc_out))):
                pltpu.make_async_copy(source, target, sems.at[n]).start()
        else:
            acc_up[...] = jnp.zeros_like(acc_up)
            acc_down[...] = jnp.zeros_like(acc_down)
            acc_out[...] = jnp.zeros_like(acc_out)

    @pl.when(step == 0)
    def _():
        for pair in range(PAIRS):
            carry[pair] = unpack_state(inc_ref[0], pair)
        back[...] = jnp.zeros_like(back)
        back_sum[...] = jnp.zeros_like(back_sum)

    block = same_head()
    ones_head = jnp.where(block, 1.0, 0.0).astype(bf16)
    ones_twice = jnp.concatenate([ones_head, ones_head], axis=0)
    low = first_head(CHUNK)
    one_low = jnp.where(low, 1.0, 0.0).astype(bf16)
    one_high = jnp.where(low, 0.0, 1.0).astype(bf16)
    ones_both = jnp.concatenate([one_low, one_high], axis=0)
    ones_all = jnp.ones((CHUNK, PAIR), bf16)
    wide_block = jnp.concatenate([block, block], axis=1)
    upper = sublanes(CHUNK, PAIR) < STRETCH
    inner = lanes(PAIR, PAIR) % HEAD_DIM
    zero_s = jnp.zeros((PAIR, PAIR), bf16)
    for i in range(per):
        x_scr[i * STRETCH : (i + 1) * STRETCH, :] = pick(rows_ref, placing[micro, step * per + i])
        cot_scr[i * STRETCH : (i + 1) * STRETCH, :] = pick(cot_ref, placing[micro, step * per + i])

    x = x_scr[...].astype(f32)
    n, _ = standardize(x)
    normed = (n * gain_one[...] + shift_one[...]).astype(bf16)
    for part in range(2):
        at = slice(part * MODEL, (part + 1) * MODEL)
        qkv_ref[:, at] = featured(nn(normed, w_qkv[:, at]) + b_qkv[:, at])
    at = slice(2 * MODEL, 3 * MODEL)
    qkv_ref[:, at] = (nn(normed, w_qkv[:, at]) + b_qkv[:, at]).astype(bf16)

    for chunk in range(TILE // CHUNK):
        rows = slice(chunk * CHUNK, (chunk + 1) * CHUNK)
        r0 = flag(restart[micro, step * per + 2 * chunk])
        r1 = flag(restart[micro, step * per + 2 * chunk + 1])
        mask = causal(r1, False)
        keep_low = jnp.where(upper, 1.0, 1.0 - r1)
        keep_key = jnp.where(upper, 1.0 - r1, 1.0)
        for pair in range(PAIRS):
            q = qkv_ref[rows, pair * PAIR : (pair + 1) * PAIR]
            k = qkv_ref[rows, MODEL + pair * PAIR : MODEL + (pair + 1) * PAIR]
            v = qkv_ref[rows, 2 * MODEL + pair * PAIR : 2 * MODEL + (pair + 1) * PAIR]
            state = carry[pair] * (1.0 - r0)
            state_b = state.astype(bf16)
            state_low = (state - state_b.astype(f32)).astype(bf16)
            states_out[chunk, pair * PAIR : (pair + 1) * PAIR, :] = jnp.concatenate(
                [
                    state_b[:, :PAIR],
                    jnp.where(
                        inner < 2, state_b[:, PAIR:], jnp.where(inner == 2, state_low[:, PAIR:], zero_s)
                    ),
                    state_low[:, :PAIR],
                ],
                axis=1,
            )
            mixing = nt(q, by_head(k, CHUNK)) * mask
            values = jnp.concatenate([by_head(v, CHUNK), ones_both], axis=1)
            out = nn(mixing.astype(bf16), values)
            out = out + nn((q.astype(f32) * keep_low).astype(bf16), state_b)
            inv = 1.0 / out[:, PAIR:]
            att = out[:, :PAIR] * inv
            att_scr[rows, col(pair)] = att
            inv_scr[rows, col(pair)] = inv
            att_b[rows, col(pair)] = att.astype(bf16)
            k_keep = (k.astype(f32) * keep_key).astype(bf16)
            added = tn(k_keep, jnp.concatenate([v, ones_all], axis=1))
            carry[pair] = state * (1.0 - r1) + jnp.where(wide_block, added, 0.0)

    middle = x_scr[...].astype(f32) + nn(att_b[...], w_out[...]) + b_out[...]
    n, scale = standardize(middle)
    normed = (n * gain[...] + shift[...]).astype(bf16)
    normed_t = normed.T
    cot = cot_scr[...]
    cot_t = cot.T
    ff = w_up.shape[1]
    total = middle + b_down[...]
    up_grad = jnp.zeros((TILE, MODEL), f32)
    if resumes:

        @pl.when(opening)
        def _():
            for n_, (source, target) in enumerate(zip(before, (acc_up, acc_down, acc_out))):
                pltpu.make_async_copy(source, target, sems.at[n_]).wait()

    for part in range(ff // MODEL):
        at = slice(part * MODEL, (part + 1) * MODEL)
        u = nn(normed, w_up[:, at]) + b_up[:, at]
        u2 = u * u
        t = jnp.tanh(u * (0.7978845608028654 + 0.035677408136300125 * u2))
        half = 0.5 + 0.5 * t
        act = (u * half).astype(bf16)
        rise = 0.7978845608028654 + 0.10703222440890037 * u2
        slope = half + 0.5 * u * (1.0 - t * t) * rise
        g = (nt(cot, w_down[at, :]) * slope).astype(bf16)
        total = total + nn(act, w_down[at, :])
        acc_down[:, at] += nn(cot_t, act)
        vec_out[0:1, at] += jnp.sum(g.astype(f32), axis=0, keepdims=True)
        up_grad = up_grad + nt(g, w_up[:, at])
        acc_up[:, at] += nn(normed_t, g)
    total = total.astype(bf16)
    for i in range(per):
        put(result, placing[micro, step * per + i], total[i * STRETCH : (i + 1) * STRETCH, :])

    cot_f = cot.astype(f32)
    vec_out[1:2, :MODEL] += jnp.sum(up_grad * n, axis=0, keepdims=True)
    vec_out[1:2, MODEL : 2 * MODEL] += jnp.sum(up_grad, axis=0, keepdims=True)
    vec_out[1:2, 3 * MODEL : 4 * MODEL] += jnp.sum(cot_f, axis=0, keepdims=True)
    branch = (cot_f + norm_back(up_grad, gain[...], n, scale)).astype(bf16)
    branch_out[...] = branch
    vec_out[1:2, 2 * MODEL : 3 * MODEL] += jnp.sum(branch.astype(f32), axis=0, keepdims=True)
    grad_att = nt(branch, w_out[...])
    acc_out[...] += tn(att_b[...], branch)
    lane = lanes(CHUNK, PAIR) % HEAD_DIM
    for chunk in range(TILE // CHUNK):
        rows = slice(chunk * CHUNK, (chunk + 1) * CHUNK)
        o0 = flag(opened[micro, step * per + 2 * chunk])
        o1 = flag(opened[micro, step * per + 2 * chunk + 1])
        keep = jnp.where(upper, o0, o1)
        for pair in range(PAIRS):
            inv = inv_scr[rows, col(pair)]
            gn = (grad_att[rows, col(pair)].astype(bf16).astype(f32) * inv).astype(bf16)
            product = gn.astype(f32) * att_scr[rows, col(pair)]
            high = product.astype(bf16)
            low_part = (product - high.astype(f32)).astype(bf16)
            gd = -nn(jnp.concatenate([high, low_part], axis=1), ones_twice)
            gd_high = gd.astype(bf16)
            gd_low = (gd - gd_high.astype(f32)).astype(bf16)
            zero = jnp.zeros_like(gd_high)
            gn_out[rows, col(pair)] = gn
            gd_out[rows, col(pair)] = jnp.where(
                (lane == 0) | (lane == 2), gd_high, jnp.where(lane == 1, gd_low, zero)
            )
            q = qkv_ref[rows, pair * PAIR : (pair + 1) * PAIR].astype(f32) * keep
            back[pair] += tn(q.astype(bf16), gn)
            back_sum[:, col(pair)] += jnp.sum(q * gd, axis=0, keepdims=True)

    @pl.when(step == pl.num_programs(1) - 1)
    def _():
        for pair in range(PAIRS):
            pack_state(state_out, pair, back[pair], back_sum[:, col(pair)])

    if final:

        @pl.when((member == pl.num_programs(0) - 1) & (step == pl.num_programs(1) - 1))
        def _():
            parts = ff // MODEL
            devices = 2 * keep_out.shape[0]
            less = MODEL // devices
            more = parts * less
            for part in range(parts):
                at = slice(part * MODEL, (part + 1) * MODEL)
                turned[at, :] = acc_down[:, at].T
            for j in range(devices):
                d = owner[j]
                target = keep_out if j < devices // 2 else send_out
                seat = j % (devices // 2)
                here = pl.ds(pl.multiple_of(d * less, less), less)
                for part in range(parts):
                    target[seat, part * less : (part + 1) * less, :] = acc_up[
                        here, part * MODEL : (part + 1) * MODEL
                    ].astype(target.dtype)
                there = pl.ds(pl.multiple_of(d * more, more), more)
                target[seat, more : 2 * more, :] = turned[there, :].astype(target.dtype)
                target[seat, 2 * more :, :] = acc_out[here, :].astype(target.dtype)


def run_mid(tables, first, members, target, rows, cot, inc, weights, vectors, before, owner):
    micro, count = tables[0].shape
    width = rows.shape[-1]
    ff = weights[2].shape[1]
    count = count * STRETCH
    tiles = count // TILE
    total = members * count
    resumes, final = before is not None, owner is not None
    f32_sums = [(width, ff), (width, ff), (MODEL, width)]
    devices = lax.axis_size(BOTH) if final else 0
    if not final:
        owner = jnp.zeros((8,), jnp.int32)
    half = (devices // 2, (2 * ff + MODEL) // max(devices, 1), MODEL)
    out_specs = [
        group_spec(target.shape, 0),
        tile_spec(3 * MODEL, tiles),
        tile_spec(width, tiles),
        tile_spec(MODEL, tiles),
        tile_spec(MODEL, tiles),
        states_spec(tiles),
        member_spec(),
        fixed((8, ff)),
    ]
    out_shape = [
        jax.ShapeDtypeStruct(target.shape, bf16),
        jax.ShapeDtypeStruct((total, 3 * MODEL), bf16),
        jax.ShapeDtypeStruct((total, width), bf16),
        jax.ShapeDtypeStruct((total, MODEL), bf16),
        jax.ShapeDtypeStruct((total, MODEL), bf16),
        jax.ShapeDtypeStruct((total // CHUNK, MODEL, 3 * PAIR), bf16),
        jax.ShapeDtypeStruct((members, HEAD_DIM + 8, MODEL), f32),
        jax.ShapeDtypeStruct((8, ff), f32),
    ]
    if final:
        out_specs += [fixed(half), fixed(half)]
        out_shape += [jax.ShapeDtypeStruct(half, f32), jax.ShapeDtypeStruct(half, bf16)]
        scratch = [pltpu.VMEM(shape, f32) for shape in f32_sums] + [pltpu.VMEM((ff, width), f32)]
    else:
        out_specs += [fixed(shape) for shape in f32_sums]
        out_shape += [jax.ShapeDtypeStruct(shape, f32) for shape in f32_sums]
        scratch = []
    scratch += [
        pltpu.VMEM((PAIRS, PAIR, 2 * PAIR), f32),
        pltpu.VMEM((PAIRS, PAIR, PAIR), f32),
        pltpu.VMEM((1, MODEL), f32),
        pltpu.VMEM((TILE, MODEL), f32),
        pltpu.VMEM((TILE, MODEL), f32),
        pltpu.VMEM((TILE, MODEL), bf16),
        pltpu.VMEM((TILE, width), bf16),
        pltpu.VMEM((TILE, width), bf16),
    ]
    if resumes:
        scratch.append(pltpu.SemaphoreType.DMA((3,)))
    return pl.pallas_call(
        functools.partial(mid_kernel, first=first, resumes=resumes, final=final),
        name="middle",
        grid_spec=pltpu.PrefetchScalarGridSpec(
            num_scalar_prefetch=4,
            grid=(members, tiles),
            in_specs=[
                ANYWHERE,
                group_spec(rows.shape, first),
                group_spec(cot[0].shape, cot[1]),
                member_spec(first),
            ]
            + [fixed(item.shape) for item in weights + vectors]
            + [ANYWHERE] * (3 if resumes else 0),
            out_specs=out_specs,
            scratch_shapes=scratch,
        ),
        out_shape=out_shape,
        compiler_params=params(),
        input_output_aliases={4: 0},
        cost_estimate=pl.CostEstimate(
            flops=2 * total * width * (6 * MODEL + 6 * ff) + (members << 32),
            bytes_accessed=members * (20 << 20),
            transcendentals=total * ff,
        ),
    )(*tables, owner, target, rows, cot[0], inc, *weights, *vectors, *(before or ()))


def back_kernel(
    placing,
    restart,
    owner,
    _,
    rows_ref,
    qkv_ref,
    gn_ref,
    gd_ref,
    branch_ref,
    states_ref,
    inc_ref,
    weight,
    gain,
    shift,
    owner_col,
    *refs,
    first,
    resumes,
    final,
    widths,
    sums,
):
    before, refs = (refs[:1], refs[1:]) if resumes else ((), refs)
    vec_others, refs = refs[:sums], refs[sums:]
    grad_rows, vec_out = refs[:2]
    refs = refs[2:]
    if final:
        keep_out, send_out, acc = refs[:3]
        refs = refs[3:]
    else:
        acc = refs[0]
        refs = refs[1:]
    carry, x_scr, mixed_scr = refs[:3]
    sems = refs[3] if resumes else None
    member, step = pl.program_id(0), pl.program_id(1)
    micro = first + member
    per = TILE // STRETCH
    tile = pl.num_programs(1) - 1 - step
    opening = (member == 0) & (step == 0)
    lane = lanes(CHUNK, PAIR)
    inner = lane % HEAD_DIM

    @pl.when(opening)
    def _():
        vec_out[...] = jnp.zeros_like(vec_out)
        if resumes:
            pltpu.make_async_copy(before[0], acc, sems.at[0]).start()
        else:
            acc[...] = jnp.zeros_like(acc)

    @pl.when(step == 0)
    def _():
        only = jnp.concatenate([jnp.ones((PAIR, PAIR), f32), jnp.where(inner == 0, 1.0, 0.0)], axis=1)
        for pair in range(PAIRS):
            carry[pair] = unpack_state(inc_ref[0], pair) * only

    block = same_head()
    wide_block = jnp.concatenate([block, block], axis=1)
    upper = sublanes(CHUNK, PAIR) < STRETCH
    marks = jnp.where((inner < 2) | (inner == 3), 1.0, 0.0).astype(bf16)
    mark_low = jnp.where(lane < 2, 1.0, 0.0).astype(bf16)
    mark_high = jnp.where((lane == HEAD_DIM) | (lane == HEAD_DIM + 1), 1.0, 0.0).astype(bf16)
    marks_both = jnp.concatenate([mark_low, mark_high], axis=0)
    for i in range(per):
        x_scr[i * STRETCH : (i + 1) * STRETCH, :] = pick(rows_ref, placing[micro, tile * per + i])

    for chunk in reversed(range(TILE // CHUNK)):
        rows = slice(chunk * CHUNK, (chunk + 1) * CHUNK)
        r0 = flag(restart[micro, tile * per + 2 * chunk])
        r1 = flag(restart[micro, tile * per + 2 * chunk + 1])
        r2 = flag(restart[micro, tile * per + 2 * chunk + 2])
        mask = causal(r1, False)
        mask_t = causal(r1, True)
        keep_low = jnp.where(upper, 1.0, 1.0 - r1)
        keep_key = jnp.where(upper, 1.0 - r1, 1.0)
        for pair in range(PAIRS):
            q = qkv_ref[rows, pair * PAIR : (pair + 1) * PAIR]
            k = qkv_ref[rows, MODEL + pair * PAIR : MODEL + (pair + 1) * PAIR]
            v = qkv_ref[rows, 2 * MODEL + pair * PAIR : 2 * MODEL + (pair + 1) * PAIR]
            gn = gn_ref[rows, col(pair)]
            gdx = gd_ref[rows, col(pair)]
            state = states_ref[chunk, pair * PAIR : (pair + 1) * PAIR, :]
            grown = carry[pair] * (1.0 - r2)
            grown_b = grown.astype(bf16)
            rest = grown - grown_b.astype(f32)
            grown_low = rest[:, :PAIR].astype(bf16)
            z_low = pltpu.roll(rest[:, PAIR:], 3, 1).astype(bf16)
            z_both = jnp.where(inner < 2, grown_b[:, PAIR:], jnp.where(inner == 3, z_low, jnp.zeros_like(z_low)))
            grown_x = jnp.concatenate([grown_b[:, :PAIR], z_both], axis=1)
            k2 = by_head(k, CHUNK)
            q2 = by_head(q, CHUNK)
            v2 = by_head(v, CHUNK)
            gn2 = by_head(gn, CHUNK)
            gd2 = by_head(gdx, CHUNK)
            both = jnp.concatenate([gn, gdx], axis=1)
            mixing_t = (nt(k, q2) * mask_t).astype(bf16)
            g_mix = (nt(both, jnp.concatenate([v2, marks_both], axis=1)) * mask).astype(bf16)
            v_marks = jnp.concatenate([v, marks], axis=1)
            g_mix_t = (nt(v_marks, jnp.concatenate([gn2, gd2], axis=1)) * mask_t).astype(bf16)
            dq = nn(g_mix, k2) + (nt(both, state[:, : 2 * PAIR]) + nt(gn, state[:, 2 * PAIR :])) * keep_low
            dk = nn(g_mix_t, q2) + (nt(v_marks, grown_x) + nt(v, grown_low)) * keep_key
            dv = nn(mixing_t, gn2) + nn(k, grown_b[:, :PAIR]) * keep_key
            q_keep = (q.astype(f32) * keep_low).astype(bf16)
            added = tn(q_keep, both)
            carry[pair] = (grown * (1.0 - r1) + jnp.where(wide_block, added, 0.0)) * (1.0 - r0)
            mixed_scr[rows, pair * PAIR : (pair + 1) * PAIR] = (
                dq * jnp.minimum(q.astype(f32), 1.0)
            ).astype(bf16)
            mixed_scr[rows, MODEL + pair * PAIR : MODEL + (pair + 1) * PAIR] = (
                dk * jnp.minimum(k.astype(f32), 1.0)
            ).astype(bf16)
            mixed_scr[rows, 2 * MODEL + pair * PAIR : 2 * MODEL + (pair + 1) * PAIR] = dv.astype(bf16)

    mixed = mixed_scr[...]
    vec_out[0:1, :] += jnp.sum(mixed.astype(f32), axis=0, keepdims=True)
    upstream = nt(mixed, weight[...])
    n, scale = standardize(x_scr[...].astype(f32))
    normed_t = (n * gain[...] + shift[...]).astype(bf16).T
    if resumes:

        @pl.when(opening)
        def _():
            pltpu.make_async_copy(before[0], acc, sems.at[0]).wait()

    for part in range(3):
        at = slice(part * MODEL, (part + 1) * MODEL)
        acc[:, at] += nn(normed_t, mixed[:, at])
    vec_out[1:2, :MODEL] += jnp.sum(upstream * n, axis=0, keepdims=True)
    vec_out[1:2, MODEL : 2 * MODEL] += jnp.sum(upstream, axis=0, keepdims=True)
    total = (branch_ref[...].astype(f32) + norm_back(upstream, gain[...], n, scale)).astype(bf16)
    for i in range(per):
        put(grad_rows, placing[micro, tile * per + i], total[i * STRETCH : (i + 1) * STRETCH, :])

    if final:

        @pl.when((member == pl.num_programs(0) - 1) & (step == pl.num_programs(1) - 1))
        def _():
            half = keep_out.shape[0]
            devices = 2 * half
            less = MODEL // devices
            for j in range(devices):
                here = pl.ds(pl.multiple_of(owner[j] * less, less), less)
                target = keep_out if j < half else send_out
                for part in range(3):
                    target[j % half, part * less : (part + 1) * less, :] = acc[
                        here, part * MODEL : (part + 1) * MODEL
                    ].astype(target.dtype)
            mid = sum(ref[...] for ref in vec_others if ref.shape[1] == vec_others[0].shape[1])
            rear = vec_out[...] + sum(
                ref[...] for ref in vec_others if ref.shape[1] != vec_others[0].shape[1]
            )
            sources = (
                rear[1:2, :MODEL],
                rear[1:2, MODEL : 2 * MODEL],
                rear[0:1, : 2 * MODEL],
                rear[0:1, 2 * MODEL :],
                mid[1:2, 2 * MODEL : 3 * MODEL],
                mid[1:2, :MODEL],
                mid[1:2, MODEL : 2 * MODEL],
                mid[0:1, :],
                mid[1:2, 3 * MODEL : 4 * MODEL],
            )
            rows16 = sublanes(16, MODEL)
            pieces = []
            for source, width in zip(sources, widths, strict=True):
                size = devices * width
                mine = (lanes(devices, size) // width) == owner_col[...]
                picked = jnp.where(mine, source, 0.0)
                gather = jnp.where(
                    (sublanes(size, PAIR) % width) == lanes(size, PAIR), 1.0, 0.0
                ).astype(bf16)
                high = picked.astype(bf16)
                low = (picked - high.astype(f32)).astype(bf16)
                pieces.append(nn(high, gather) + nn(low, gather))
            rest = jnp.zeros((1, MODEL - PAIR), f32)
            for j in range(devices):
                block16 = jnp.zeros((16, MODEL), f32)
                for v, piece in enumerate(pieces):
                    row = jnp.concatenate([piece[j : j + 1, :], rest], axis=1)
                    block16 = block16 + jnp.where(rows16 == v, row, 0.0)
                target = keep_out if j < half else send_out
                target[j % half, 3 * less :, :] = block16.astype(target.dtype)


def run_back(tables, first, members, target, rows, mid, inc, weight, gain, shift, before, owner, others, widths):
    (group, seat), (saved, at) = target, mid
    micro, count = tables[0].shape
    width = rows.shape[-1]
    count = count * STRETCH
    tiles = count // TILE
    resumes, final = before is not None, owner is not None
    devices = lax.axis_size(BOTH) if final else 0
    if not final:
        owner = jnp.zeros((8,), jnp.int32)
        others = []
    half = (devices // 2, 3 * MODEL // max(devices, 1) + 16, MODEL)
    out_specs = [group_spec(group.shape, seat), fixed((8, 3 * MODEL))]
    out_shape = [
        jax.ShapeDtypeStruct(group.shape, bf16),
        jax.ShapeDtypeStruct((8, 3 * MODEL), f32),
    ]
    scratch = []
    if final:
        out_specs += [fixed(half), fixed(half)]
        out_shape += [jax.ShapeDtypeStruct(half, f32), jax.ShapeDtypeStruct(half, bf16)]
        scratch.append(pltpu.VMEM((width, 3 * MODEL), f32))
    else:
        out_specs.append(fixed((width, 3 * MODEL)))
        out_shape.append(jax.ShapeDtypeStruct((width, 3 * MODEL), f32))
    scratch += [
        pltpu.VMEM((PAIRS, PAIR, 2 * PAIR), f32),
        pltpu.VMEM((TILE, width), bf16),
        pltpu.VMEM((TILE, 3 * MODEL), bf16),
    ]
    if resumes:
        scratch.append(pltpu.SemaphoreType.DMA((1,)))

    def tile(width_):
        return pl.BlockSpec((TILE, width_), lambda i, t, *_: ((at + i) * tiles + tiles - 1 - t, 0))

    return pl.pallas_call(
        functools.partial(
            back_kernel, first=first, resumes=resumes, final=final, widths=widths, sums=len(others)
        ),
        name="back",
        grid_spec=pltpu.PrefetchScalarGridSpec(
            num_scalar_prefetch=3,
            grid=(members, tiles),
            in_specs=[
                ANYWHERE,
                group_spec(rows.shape, first),
                tile(3 * MODEL),
                tile(MODEL),
                tile(MODEL),
                tile(width),
                pl.BlockSpec(
                    (TILE // CHUNK, MODEL, 3 * PAIR),
                    lambda i, t, *_: ((at + i) * tiles + tiles - 1 - t, 0, 0),
                ),
                member_spec(at),
                fixed(weight.shape),
                fixed(gain.shape),
                fixed(shift.shape),
                fixed((owner.shape[0], 1)),
            ]
            + ([ANYWHERE] if resumes else [])
            + [fixed(item.shape) for item in others],
            out_specs=out_specs,
            scratch_shapes=scratch,
        ),
        out_shape=out_shape,
        input_output_aliases={3: 0},
        compiler_params=params(),
        cost_estimate=pl.CostEstimate(
            flops=members * (2 * count * width * 6 * MODEL + (8 << 30)),
            bytes_accessed=members * (14 << 20),
            transcendentals=0,
        ),
    )(
        tables[0],
        tables[1],
        owner,
        group,
        rows,
        saved[1],
        saved[3],
        saved[4],
        saved[2],
        saved[5],
        inc,
        weight,
        gain,
        shift,
        owner[:, None],
        *(() if before is None else (before,)),
        *others,
    )


def send_kernel(slot, source, target):
    micro = pl.program_id(0)
    for i in range(source.shape[1]):
        put(target, slot[micro, i], source[0, i])


def run_send(slot, rows, first, members):
    micro, count, width = rows.shape
    stretches = count // STRETCH
    groups = lax.axis_size("dp")
    shape = (groups, members, stretches // groups, STRETCH, width)
    return pl.pallas_call(
        send_kernel,
        name="send",
        grid_spec=pltpu.PrefetchScalarGridSpec(
            num_scalar_prefetch=1,
            grid=(members,),
            in_specs=[
                pl.BlockSpec((1, stretches, STRETCH, width), lambda i, *_: (first + i, 0, 0, 0))
            ],
            out_specs=pl.BlockSpec((groups, 1) + shape[2:], lambda i, *_: (0, i, 0, 0, 0)),
        ),
        out_shape=jax.ShapeDtypeStruct(shape, rows.dtype),
        compiler_params=pltpu.CompilerParams(vmem_limit_bytes=VMEM_LIMIT),
        cost_estimate=pl.CostEstimate(
            flops=0, bytes_accessed=4 * members * count * width, transcendentals=0
        ),
    )(slot[first : first + members], rows.reshape(micro, stretches, STRETCH, width))


def land_kernel(slot, _, source, target):
    micro = pl.program_id(0)
    for i in range(target.shape[1]):
        target[0, i] = pick(source, slot[micro, i])


def run_land(slot, landed, output, first):
    members = landed.shape[1]
    shape = output.shape
    block = (landed.shape[0], 1) + landed.shape[2:]
    return pl.pallas_call(
        land_kernel,
        name="land",
        grid_spec=pltpu.PrefetchScalarGridSpec(
            num_scalar_prefetch=1,
            grid=(members,),
            in_specs=[
                pl.BlockSpec(memory_space=pl.ANY),
                pl.BlockSpec(block, lambda i, *_: (0, i, 0, 0, 0)),
            ],
            out_specs=pl.BlockSpec((1,) + shape[1:], lambda i, *_: (first + i, 0, 0, 0)),
        ),
        out_shape=jax.ShapeDtypeStruct(shape, output.dtype),
        input_output_aliases={1: 0},
        compiler_params=pltpu.CompilerParams(vmem_limit_bytes=VMEM_LIMIT),
        cost_estimate=pl.CostEstimate(flops=0, bytes_accessed=4 * landed.size, transcendentals=0),
    )(slot[first : first + members], output, landed)


def blank(shape):
    return pl.pallas_call(
        lambda ref: None,
        name="blank",
        out_specs=pl.BlockSpec(memory_space=pl.ANY),
        out_shape=jax.ShapeDtypeStruct(shape, bf16),
    )()


def index_tables(lengths, stretch_order, count):
    fsdp = lax.axis_size("fsdp")
    groups = lax.axis_size("dp")
    device = lax.axis_index(BOTH)
    base = device * count
    within = jnp.arange(count, dtype=jnp.int32)
    mine = base + within
    place = jnp.arange(stretch_order.shape[1], dtype=jnp.int32)
    here = place[None, None, :]
    landing = jnp.sum(
        jnp.where(stretch_order[:, None, :] == mine[None, :, None], here, 0), axis=-1
    )
    slot = jnp.sum((landing[:, None, :] < landing[:, :, None]).astype(jnp.int32), axis=-1)
    arrival = jnp.sum(
        jnp.where(here == mine[None, :, None], stretch_order[:, None, :], 0), axis=-1
    )
    source = arrival // count // fsdp
    ahead = (source[:, None, :] == source[:, :, None]) & (
        within[None, None, :] < within[None, :, None]
    )
    placing = source * (count // groups) + jnp.sum(ahead.astype(jnp.int32), axis=-1)
    index = jnp.arange(lengths.shape[1], dtype=jnp.int32)
    starts = jnp.sum(
        jnp.where(index[None, None, :] < index[None, :, None], lengths[:, None, :], 0), axis=-1
    )
    edge = base + jnp.arange(count + 1, dtype=jnp.int32)
    restart = jnp.any(starts[:, None, :] == edge[None, :, None], axis=-1).astype(jnp.int32)
    restart = jnp.where(edge[None, :] == stretch_order.shape[1], 1, restart)
    opened = 1 - jnp.any(
        (starts[:, None, :] >= base) & (starts[:, None, :] <= mine[None, :, None]), axis=-1
    ).astype(jnp.int32)
    last = base + count - 1
    closing = 1 - jnp.any(
        (starts[:, None, :] > mine[None, :, None]) & (starts[:, None, :] <= last), axis=-1
    ).astype(jnp.int32)
    hops = -(-(LONGEST - 1) // count)
    hop = jnp.arange(hops, dtype=jnp.int32)
    reach_back = base - 1 - hop * count
    from_before = 1.0 - jnp.any(
        (starts[:, None, :] > reach_back[None, :, None]) & (starts[:, None, :] <= base), axis=-1
    ).astype(f32)
    reach_on = base + (hop + 1) * count
    from_after = 1.0 - jnp.any(
        (starts[:, None, :] > last) & (starts[:, None, :] <= reach_on[None, :, None]), axis=-1
    ).astype(f32)
    return slot, placing, restart, opened, closing, from_before, from_after


def exchange(states, hops, forward):
    size = lax.axis_size("fsdp")
    got = []
    for hop in range(min(hops, size - 1)):
        step = hop + 1
        pairs = [(i, i + step) if forward else (i + step, i) for i in range(size - step)]
        got.append(lax.ppermute(states, "fsdp", pairs))
    return got


def joined(got, weights, *others):
    got = after(got, *others)
    return sum(item * weights[:, hop, None, None] for hop, item in enumerate(got))


def halving_stages():
    stages = []
    dp, fsdp = lax.axis_size("dp"), lax.axis_size("fsdp")
    if dp > 1:
        stages.append(("dp", 1))
    bit = 1
    while bit < fsdp:
        stages.append(("fsdp", bit))
        bit *= 2
    bit = 2
    while bit < dp:
        stages.append(("dp", bit))
        bit *= 2
    return stages


def order_tables():
    stages = halving_stages()
    fsdp = lax.axis_size("fsdp")
    devices = lax.axis_size(BOTH)
    me = lax.axis_index(BOTH)
    index = jnp.arange(devices, dtype=jnp.int32)
    bits = [bit * (fsdp if axis == "dp" else 1) for axis, bit in stages]
    place = jnp.zeros((devices,), jnp.int32)
    owner = jnp.zeros((devices,), jnp.int32)
    for s, bit in enumerate(bits):
        rank = len(bits) - 1 - s
        place = place + jnp.where(((index ^ me) & bit) != 0, 1 << rank, 0)
        owner = owner + jnp.where(((index >> rank) & 1) != 0, bit, 0)
    return place, owner ^ me


def after(x, *others):
    return lax.optimization_barrier((x, others))[0]


def swap(x, axis, bit):
    return lax.ppermute(x, axis, [(i, i ^ bit) for i in range(lax.axis_size(axis))])


def gather_halves(parts):
    stages = list(reversed(halving_stages()))
    done, steps = [], []
    for n, x in enumerate(parts):
        own = []
        for s, (axis, bit) in enumerate(stages):
            if n:
                x = after(x, done[s])
            got = swap(x, axis, bit)
            if s == len(stages) - 1:
                own.append(got)
                steps.append((x, got))
            else:
                x = jnp.concatenate([x, got], axis=0)
                own.append(x)
        done = own
        if n == 0:
            first = own
    return steps, first


def scatter_stages():
    return len(halving_stages())


def scatter_step(keep, send, s, between=None):
    stages = halving_stages()
    got = swap(send, *stages[s])
    if between is not None:
        beside = between()
        got = after(got, beside[1])
        return (*scatter_join(keep, got, s == len(stages) - 1), beside)
    return scatter_join(keep, got, s == len(stages) - 1)


def scatter_join(keep, got, last):
    if last:
        return keep[0] + got[0].astype(f32), None
    half = keep.shape[0] // 2
    send = (keep[half:] + got[half:].astype(f32)).astype(bf16)
    return keep[:half] + got[:half].astype(f32), send


def pack_kernel(qkv, out, up, down, *refs):
    *small, first, second = refs
    rows = qkv.shape[0]
    for c in range(3):
        first[0, c * rows : (c + 1) * rows, :] = qkv[:, c * MODEL : (c + 1) * MODEL]
    row = sublanes(16, PAIR)
    side = jnp.zeros((16, PAIR), f32)
    for v, item in enumerate(small):
        width = item.shape[1]
        spread = jnp.where(sublanes(width, PAIR) == lanes(width, PAIR), 1.0, 0.0).astype(bf16)
        tall = jnp.broadcast_to(item[...].astype(f32), (16, width)).astype(bf16)
        side = side + jnp.where(row == v, nn(tall, spread), 0.0)
    side = jnp.concatenate([side, jnp.zeros((16, MODEL - PAIR), f32)], axis=1)
    first[0, 3 * rows : 3 * rows + 16, :] = side.astype(bf16)
    parts = up.shape[1] // MODEL
    for c in range(parts):
        second[0, c * rows : (c + 1) * rows, :] = up[:, c * MODEL : (c + 1) * MODEL]
    second[0, parts * rows : 2 * parts * rows, :] = down[...]
    second[0, 2 * parts * rows :, :] = out[...]


def run_pack(qkv, out, up, down, small):
    rows = qkv.shape[0]
    parts = up.shape[1] // MODEL
    return pl.pallas_call(
        pack_kernel,
        name="pack",
        out_shape=[
            jax.ShapeDtypeStruct((1, 3 * rows + 16, MODEL), bf16),
            jax.ShapeDtypeStruct((1, (2 * parts + 1) * rows, MODEL), bf16),
        ],
    )(qkv, out, up, down, *(item[None] for item in small))


def sort_first_kernel(place, own, got, owner, qkv, vectors, *, widths):
    half, total, _ = own.shape
    rows = total // 4

    def part(d):
        p = place[d]
        q = lax.rem(p, half)
        return jnp.where(p < half, own[q, : 3 * rows, :], got[q, : 3 * rows, :])

    for d in range(2 * half):
        block = part(d)
        for c in range(3):
            qkv[d * rows : (d + 1) * rows, c * MODEL : (c + 1) * MODEL] = block[
                c * rows : (c + 1) * rows, :
            ]
    small = jnp.concatenate(
        [own[:, 3 * rows :, :PAIR].astype(f32), got[:, 3 * rows :, :PAIR].astype(f32)], axis=0
    )
    row = lax.broadcasted_iota(jnp.int32, small.shape, 1)
    vectors[...] = jnp.zeros_like(vectors)
    for v, width in enumerate(widths):
        values = jnp.sum(jnp.where(row == v, small, 0.0), axis=1)
        size = 2 * half * width
        lane = lanes(PAIR, size) % width
        spread = jnp.where(lane == sublanes(PAIR, size), 1.0, 0.0).astype(bf16)
        wide = nn(values.astype(bf16), spread)
        mine = (lanes(2 * half, size) // width) == owner[...]
        vectors[v : v + 1, :size] = jnp.sum(jnp.where(mine, wide, 0.0), axis=0, keepdims=True)


def run_sort_first(place, owner, own, got, widths):
    devices = place.shape[0]
    rows = own.shape[1] // 4
    vmem = pl.BlockSpec(memory_space=pltpu.VMEM)
    return pl.pallas_call(
        functools.partial(sort_first_kernel, widths=widths),
        name="sort_first",
        in_specs=[pl.BlockSpec(memory_space=pltpu.SMEM), vmem, vmem, vmem],
        out_specs=[vmem, vmem],
        out_shape=[
            jax.ShapeDtypeStruct((devices * rows, 3 * MODEL), bf16),
            jax.ShapeDtypeStruct((8, devices * max(widths)), f32),
        ],
        compiler_params=pltpu.CompilerParams(vmem_limit_bytes=VMEM_LIMIT),
    )(place, own, got, owner[:, None])


def sort_second_kernel(gathered, up, down, out):
    devices, total, _ = gathered.shape
    parts = up.shape[1] // MODEL
    rows = total // (2 * parts + 1)
    tall = parts * rows
    for d in range(devices):
        for c in range(parts):
            up[d * rows : (d + 1) * rows, c * MODEL : (c + 1) * MODEL] = gathered[
                d, c * rows : (c + 1) * rows, :
            ]
        down[d * tall : (d + 1) * tall, :] = gathered[d, tall : 2 * tall, :]
        out[d * rows : (d + 1) * rows, :] = gathered[d, 2 * tall :, :]


def run_sort_second(gathered, ff):
    devices = gathered.shape[0]
    rows = gathered.shape[1] // (2 * (ff // MODEL) + 1)
    vmem = pl.BlockSpec(memory_space=pltpu.VMEM)
    return pl.pallas_call(
        sort_second_kernel,
        name="sort_second",
        in_specs=[vmem],
        out_specs=[vmem, vmem, vmem],
        out_shape=[
            jax.ShapeDtypeStruct((devices * rows, ff), bf16),
            jax.ShapeDtypeStruct((ff, MODEL), bf16),
            jax.ShapeDtypeStruct((devices * rows, MODEL), bf16),
        ],
        compiler_params=pltpu.CompilerParams(vmem_limit_bytes=VMEM_LIMIT),
    )(gathered)


def gather_all(x):
    return lax.all_gather(x, BOTH, axis=0, tiled=True)


def scatter_all(x):
    return lax.psum_scatter(x, BOTH, scatter_dimension=0, tiled=True)


def to_dp(group):
    return lax.all_to_all(group, "dp", split_axis=0, concat_axis=0, tiled=True)


def groups_of(micro):
    return [(0, micro - 1), (micro - 1, 1)] if micro > 1 else [(0, 1)]


def find(groups, m):
    for g, (first, members) in enumerate(groups):
        if first <= m < first + members:
            return g, m - first


def body(
    tokens,
    cotangent,
    lengths,
    stretch_order,
    ln1_gain,
    ln1_bias,
    w_qkv,
    b_qkv,
    w_out,
    b_out,
    ln2_gain,
    ln2_bias,
    w_up,
    b_up,
    w_down,
    b_down,
):
    micro, rows, width = tokens.shape
    count = rows // STRETCH
    devices = lax.axis_size(BOTH)
    ff = w_up.shape[1]
    dp = lax.axis_size("dp")
    slot, placing, restart, opened, closing, from_before, from_after = index_tables(
        lengths, stretch_order, count
    )
    small = (ln1_gain, ln1_bias, b_qkv, b_out, ln2_gain, ln2_bias, b_up, b_down)
    in_parts = (width // devices) % 16 == 0
    groups = groups_of(micro)
    sent = run_send(slot, tokens, 0, micro)
    moved = to_dp(sent)
    if in_parts:
        place, owner = order_tables()
        first_part, second_part = run_pack(w_qkv, w_out, w_up, w_down, small)
        halves, _ = gather_halves([after(first_part, sent)])
        qkv_all, vectors = run_sort_first(
            place, owner, *halves[0], [item.shape[0] for item in small]
        )
        second_part = gather_all(second_part)
        vectors = [
            vectors[v : v + 1, : devices * item.shape[0]] for v, item in enumerate(small)
        ]
    else:
        owner = None
        qkv_all, out_all = gather_all(w_qkv), gather_all(w_out)
        up_all, down_all = gather_all(w_up), gather_all(w_down)
        vectors = [gather_all(item).astype(f32)[None] for item in small]
    gain_one, shift_one, bias_qkv, bias_out, gain_two, shift_two, bias_up, bias_down = vectors
    tables = (placing, restart, opened)
    vectors = [bias_qkv, gain_one, shift_one, bias_out, gain_two, shift_two, bias_up, bias_down]

    hops = from_before.shape[1]
    states = run_state(placing, closing, moved, qkv_all, bias_qkv, gain_one, shift_one)
    incoming = exchange(states, hops, True)
    cots = [
        to_dp(run_send(slot, after(cotangent, states), first, members))
        for first, members in groups
    ]
    if in_parts:
        up_all, down_all, out_all = run_sort_second(after(second_part, states), ff)
    incoming = joined(incoming, from_before, out_all)
    weights = [qkv_all, out_all, up_all, down_all]
    mids, sums = [], None
    for g, (first, members) in enumerate(groups):
        target = blank((dp, members, count // dp, STRETCH, width))
        out = run_mid(
            tables,
            first,
            members,
            target,
            moved,
            (cots[g], 0),
            incoming,
            weights,
            vectors,
            sums,
            owner if g == len(groups) - 1 else None,
        )
        sums = out[8:]
        mids.append(out)
    outgoing = [exchange(out[6], hops, False) for out in mids]
    reach = [from_after[first : first + members] for first, members in groups]
    homes = [to_dp(out[0]) for out in mids]
    sizes = [MODEL, MODEL, 2 * MODEL, MODEL, MODEL, MODEL, MODEL, ff, MODEL]
    widths = [size // devices for size in sizes]
    last = scatter_stages() - 1
    late = len(groups) - 1
    outgoing[0] = joined(outgoing[0], reach[0], *([mids[-1][7]] if late else []))
    if in_parts:
        done = 0
        keep, send = sums
        if late:
            send = after(send, outgoing[0], homes[0])
        keep, send = scatter_step(keep, send, done)
    vec_mid = [f[7] for f in mids]
    vec_back, total = [], None
    grad_rows = [blank((dp, members, count // dp, STRETCH, width)) for _, members in groups]
    for m in range(micro):
        g, seat = find(groups, m)
        saved = list(mids[g])
        if late and g == late:
            outgoing[g] = joined(outgoing[g], reach[g], vec_back[0])

        def run(m=m, g=g, seat=seat, saved=saved, total=total, vec_back=tuple(vec_back)):
            return run_back(
                tables,
                m,
                1,
                (grad_rows[g], seat),
                moved,
                (saved, seat),
                outgoing[g],
                qkv_all,
                gain_one,
                shift_one,
                total,
                owner if m == micro - 1 else None,
                vec_mid + list(vec_back),
                widths,
            )

        if in_parts and done < last - 1:
            done += 1
            saved[2], keep, send = lax.optimization_barrier((saved[2], keep, send))
            keep, send, out = scatter_step(keep, send, done, run)
        else:
            out = run()
        grad_rows[g] = out[0]
        vec_back.append(out[1])
        total = out[2]
        if m == 0 and late:
            homes[late] = after(homes[late], out[1])
    narrow = out[2:]
    result = blank((micro, count, STRETCH, width))
    input_grad = blank((micro, count, STRETCH, width))
    for (first, _), home in zip(groups, homes, strict=True):
        result = run_land(slot, home, result, first)
    grad_homes = [to_dp(group) for group in grad_rows]
    for (first, _), home in zip(groups, grad_homes, strict=True):
        input_grad = run_land(slot, home, input_grad, first)
    result = result.reshape(micro, rows, width)
    input_grad = input_grad.reshape(micro, rows, width)
    if in_parts:
        part = width // devices
        narrow_keep, narrow_send = narrow
        if len(groups) > 1:
            narrow_send = after(narrow_send, grad_homes[0])
        while done < last:
            done += 1
            narrow_send = after(narrow_send, keep, send)
            keep, send = scatter_step(keep, send, done)
        parts = ff // MODEL
        grad_up = jnp.concatenate([keep[c * part : (c + 1) * part] for c in range(parts)], axis=1)
        grad_down = keep[parts * part : 2 * parts * part]
        grad_out = keep[2 * parts * part :]
        keep, send = narrow_keep, narrow_send
        for step in range(last + 1):
            keep, send = scatter_step(keep, send, step)
        grad_qkv = jnp.concatenate([keep[c * part : (c + 1) * part] for c in range(3)], axis=1)
        owned_vec = [keep[3 * part + v, :size] for v, size in enumerate(widths)]
    else:
        grad_up, grad_down, grad_out = (scatter_all(x) for x in (sums[0], sums[1].T, sums[2]))
        grad_qkv = scatter_all(total)
        mid, back = sum(vec_mid), sum(vec_back)
        vec = (
            back[1, :MODEL],
            back[1, MODEL : 2 * MODEL],
            back[0, : 2 * MODEL],
            back[0, 2 * MODEL :],
            mid[1, 2 * MODEL : 3 * MODEL],
            mid[1, :MODEL],
            mid[1, MODEL : 2 * MODEL],
            mid[0],
            mid[1, 3 * MODEL :],
        )
        owned_vec = [scatter_all(item) for item in vec]
    g_gain1, g_bias1, g_qk, g_value, g_bout, g_gain2, g_bias2, g_bup, g_bdown = owned_vec
    return (
        result,
        input_grad,
        g_gain1,
        g_bias1,
        grad_qkv,
        g_qk,
        g_value,
        grad_out,
        g_bout,
        g_gain2,
        g_bias2,
        grad_up,
        g_bup,
        grad_down,
        g_bdown,
    )


def solution(mesh):
    rows = P(None, BOTH, None)
    vector = P(BOTH)
    matrix = P(BOTH, None)
    in_specs = (
        rows, rows, P(), P(), vector, vector, matrix, vector, matrix, vector, vector, vector,
        matrix, vector, matrix, vector,
    )
    out_specs = (
        rows, rows, vector, vector, matrix, vector, vector, matrix, vector, vector, vector,
        matrix, vector, matrix, vector,
    )
    return jax.shard_map(body, mesh=mesh, in_specs=in_specs, out_specs=out_specs, check_vma=False)
```

```python
import functools

import jax
import jax.numpy as jnp
from jax import lax
from jax.experimental import pallas as pl
from jax.experimental.pallas import tpu as pltpu
from jax.sharding import PartitionSpec as P

HEADS = 8
HEAD_DIM = 64
STRETCH = 64
LONGEST = 48
CHUNK = 2 * STRETCH
TILE = 4 * CHUNK
PAIRS = HEADS // 2
PAIR = 2 * HEAD_DIM
MODEL = HEADS * HEAD_DIM
BOTH = ("dp", "fsdp")
EPS = 1e-05
VMEM_LIMIT = 60 * 1024 * 1024

f32 = jnp.float32
bf16 = jnp.bfloat16


def nn(a, b):
    return lax.dot_general(a, b, (((1,), (0,)), ((), ())), preferred_element_type=f32)


def nt(a, b):
    return lax.dot_general(a, b, (((1,), (1,)), ((), ())), preferred_element_type=f32)


def tn(a, b):
    return lax.dot_general(a, b, (((0,), (0,)), ((), ())), preferred_element_type=f32)


def lanes(rows, width):
    return lax.broadcasted_iota(jnp.int32, (rows, width), 1)


def sublanes(rows, width):
    return lax.broadcasted_iota(jnp.int32, (rows, width), 0)


def first_head(rows):
    return lanes(rows, PAIR) < HEAD_DIM


def same_head():
    return (sublanes(PAIR, PAIR) // HEAD_DIM) == (lanes(PAIR, PAIR) // HEAD_DIM)


def by_head(x, rows):
    low = first_head(rows)
    zero = jnp.zeros_like(x)
    return jnp.concatenate([jnp.where(low, x, zero), jnp.where(low, zero, x)], axis=0)


def flag(value):
    return value.astype(f32)


def col(pair):
    return slice(pair * PAIR, (pair + 1) * PAIR)


def standardize(x):
    centre = jnp.mean(x, axis=-1, keepdims=True)
    centred = x - centre
    spread = jnp.mean(centred * centred, axis=-1, keepdims=True)
    scale = lax.rsqrt(spread + EPS)
    return centred * scale, scale


def norm_back(upstream, gain, n, scale):
    ug = upstream * gain
    return scale * (
        ug
        - jnp.mean(ug, axis=-1, keepdims=True)
        - n * jnp.mean(ug * n, axis=-1, keepdims=True)
    )


def unpack_state(block, pair):
    part = block[:HEAD_DIM, col(pair)]
    low = first_head(HEAD_DIM)
    zero = jnp.zeros_like(part)
    state = jnp.concatenate([jnp.where(low, part, zero), jnp.where(low, zero, part)], axis=0)
    row = block[HEAD_DIM : HEAD_DIM + 1, col(pair)]
    eye = sublanes(PAIR, PAIR) == lanes(PAIR, PAIR)
    diagonal = jnp.where(eye, row, 0.0)
    ones = jnp.where(same_head(), 1.0, 0.0).astype(bf16)
    high = diagonal.astype(bf16)
    low_part = (diagonal - high.astype(f32)).astype(bf16)
    sums = nn(high, ones) + nn(low_part, ones)
    return jnp.concatenate([state, sums], axis=1)


def pack_state(ref, pair, state, row):
    low = first_head(HEAD_DIM)
    ref[0, :HEAD_DIM, col(pair)] = jnp.where(low, state[:HEAD_DIM], state[HEAD_DIM:])
    ref[0, HEAD_DIM : HEAD_DIM + 1, col(pair)] = row
    ref[0, HEAD_DIM + 1 :, col(pair)] = jnp.zeros((7, PAIR), f32)


def pick(ref, place):
    per = ref.shape[2]
    return ref[lax.div(place, per), 0, lax.rem(place, per)]


def put(ref, place, value):
    per = ref.shape[2]
    ref[lax.div(place, per), 0, lax.rem(place, per)] = value


def group_spec(shape, first):
    block = (shape[0], 1) + tuple(shape[2:])
    return pl.BlockSpec(block, lambda i, *_: (0, first + i, 0, 0, 0))


def fixed(shape):
    zeros = (0,) * len(shape)
    return pl.BlockSpec(tuple(shape), lambda *_: zeros, pipeline_mode=pl.Buffered(1))


def member_spec(first=0):
    return pl.BlockSpec((1, HEAD_DIM + 8, MODEL), lambda i, *_: (first + i, 0, 0))


def tile_spec(width, tiles, reverse=False):
    if reverse:
        return pl.BlockSpec((TILE, width), lambda i, t, *_: (i * tiles + tiles - 1 - t, 0))
    return pl.BlockSpec((TILE, width), lambda i, t, *_: (i * tiles + t, 0))


def states_spec(tiles, reverse=False):
    block = (TILE // CHUNK, MODEL, 3 * PAIR)
    if reverse:
        return pl.BlockSpec(block, lambda i, t, *_: (i * tiles + tiles - 1 - t, 0, 0))
    return pl.BlockSpec(block, lambda i, t, *_: (i * tiles + t, 0, 0))


def params():
    return pltpu.CompilerParams(
        dimension_semantics=("arbitrary", "arbitrary"), vmem_limit_bytes=VMEM_LIMIT
    )


ANYWHERE = pl.BlockSpec(memory_space=pl.ANY)


GAIN_ONE, SHIFT_ONE, BIAS_QKV, BIAS_OUT, GAIN_TWO, SHIFT_TWO, BIAS_UP, BIAS_DOWN = range(8)


def vector(ref, row):
    width = 3 * MODEL if row == BIAS_QKV else ref.shape[1] if row == BIAS_UP else MODEL
    return ref[row : row + 1, :width]


def featured(mixed):
    return jnp.where(mixed > 0, mixed + 1.0, jnp.exp(jnp.minimum(mixed, 0.0))).astype(bf16)


def state_kernel(placing, closing, rows, weight, vec, state_out, x_scr, acc, sums):
    gain, shift, bias = vector(vec, GAIN_ONE), vector(vec, SHIFT_ONE), vector(vec, BIAS_QKV)
    micro, step = pl.program_id(0), pl.program_id(1)
    per = TILE // STRETCH

    @pl.when(step == 0)
    def _():
        acc[...] = jnp.zeros_like(acc)
        sums[...] = jnp.zeros_like(sums)

    for i in range(per):
        x_scr[i * STRETCH : (i + 1) * STRETCH, :] = pick(rows, placing[micro, step * per + i])
    n, _ = standardize(x_scr[...].astype(f32))
    normed = (n * gain + shift).astype(bf16)
    keep = jnp.concatenate(
        [jnp.full((STRETCH, 1), flag(closing[micro, step * per + i]), f32) for i in range(per)],
        axis=0,
    )
    at = slice(MODEL, 2 * MODEL)
    keys = featured(nn(normed, weight[:, at]) + bias[:, at]).astype(f32) * keep
    sums[...] += jnp.sum(keys, axis=0, keepdims=True)
    keys = keys.astype(bf16)
    at = slice(2 * MODEL, 3 * MODEL)
    values = (nn(normed, weight[:, at]) + bias[:, at]).astype(bf16)
    for pair in range(PAIRS):
        acc[pair] += tn(keys[:, col(pair)], values[:, col(pair)])

    @pl.when(step == pl.num_programs(1) - 1)
    def _():
        for pair in range(PAIRS):
            pack_state(state_out, pair, acc[pair], sums[:, col(pair)])


def run_state(placing, closing, rows, weight, vec):
    micro, count = placing.shape
    width = rows.shape[-1]
    tiles = count * STRETCH // TILE
    return pl.pallas_call(
        state_kernel,
        name="end_state",
        grid_spec=pltpu.PrefetchScalarGridSpec(
            num_scalar_prefetch=2,
            grid=(micro, tiles),
            in_specs=[
                group_spec(rows.shape, 0),
                fixed(weight.shape),
                fixed(vec.shape),
            ],
            out_specs=member_spec(),
            scratch_shapes=[
                pltpu.VMEM((TILE, width), bf16),
                pltpu.VMEM((PAIRS, PAIR, PAIR), f32),
                pltpu.VMEM((1, MODEL), f32),
            ],
        ),
        out_shape=jax.ShapeDtypeStruct((micro, HEAD_DIM + 8, MODEL), f32),
        compiler_params=params(),
        cost_estimate=pl.CostEstimate(
            flops=11 << 30, bytes_accessed=5 << 20, transcendentals=0
        ),
    )(placing, closing, rows, weight, vec)


def causal(second, transposed):
    i = sublanes(CHUNK, 2 * CHUNK)
    j = lanes(CHUNK, 2 * CHUNK) % CHUNK
    if transposed:
        i, j = j, i
    crosses = (i >= STRETCH) & (j < STRETCH)
    return jnp.where(crosses, 1.0 - second, jnp.where(j <= i, 1.0, 0.0))


def start_all(when, copies):
    @pl.when(when)
    def _():
        for copy in copies:
            copy.start()


def mid_kernel(
    placing,
    restart,
    opened,
    owner,
    _,
    rows_ref,
    cot_ref,
    inc_ref,
    w_qkv,
    vec,
    w_out_far,
    w_up_far,
    w_down_far,
    *refs,
    first,
    resumes,
    final,
):
    gain_one, shift_one, b_qkv = vector(vec, GAIN_ONE), vector(vec, SHIFT_ONE), vector(vec, BIAS_QKV)
    gain, shift = vector(vec, GAIN_TWO), vector(vec, SHIFT_TWO)
    b_out, b_up, b_down = vector(vec, BIAS_OUT), vector(vec, BIAS_UP), vector(vec, BIAS_DOWN)
    before, refs = (refs[:3], refs[3:]) if resumes else ((), refs)
    result, qkv_ref, branch_out, gn_out, gd_out, states_out, state_out, vec_out = refs[:8]
    refs = refs[8:]
    if final:
        keep_out, send_out, turned, acc_up, acc_down, acc_out = refs[:6]
        refs = refs[6:]
    else:
        far_up, far_down, far_out, acc_up, acc_down, acc_out = refs[:6]
        refs = refs[6:]
    carry, back, back_sum, att_scr, inv_scr, att_b, x_scr, cot_scr, w_out, w_up, w_down, sems = refs
    member, step = pl.program_id(0), pl.program_id(1)
    micro = first + member
    per = TILE // STRETCH
    opening = (member == 0) & (step == 0)
    closing = (member == pl.num_programs(0) - 1) & (step == pl.num_programs(1) - 1)
    arriving = [
        pltpu.make_async_copy(source, target, sems.at[n])
        for n, (source, target) in enumerate(
            [(w_out_far, w_out), (w_up_far, w_up), (w_down_far, w_down)]
            + list(zip(before, (acc_up, acc_down, acc_out)))
        )
    ]
    leaving = []

    @pl.when(opening)
    def _():
        vec_out[...] = jnp.zeros_like(vec_out)
        for copy in arriving:
            copy.start()
        if not resumes:
            acc_up[...] = jnp.zeros_like(acc_up)
            acc_down[...] = jnp.zeros_like(acc_down)
            acc_out[...] = jnp.zeros_like(acc_out)

    @pl.when(step == 0)
    def _():
        for pair in range(PAIRS):
            carry[pair] = unpack_state(inc_ref[0], pair)
        back[...] = jnp.zeros_like(back)
        back_sum[...] = jnp.zeros_like(back_sum)

    block = same_head()
    ones_head = jnp.where(block, 1.0, 0.0).astype(bf16)
    ones_twice = jnp.concatenate([ones_head, ones_head], axis=0)
    low = first_head(CHUNK)
    one_low = jnp.where(low, 1.0, 0.0).astype(bf16)
    one_high = jnp.where(low, 0.0, 1.0).astype(bf16)
    ones_both = jnp.concatenate([one_low, one_high], axis=0)
    ones_all = jnp.ones((CHUNK, PAIR), bf16)
    wide_block = jnp.concatenate([block, block], axis=1)
    upper = sublanes(CHUNK, PAIR) < STRETCH
    inner = lanes(PAIR, PAIR) % HEAD_DIM
    zero_s = jnp.zeros((PAIR, PAIR), bf16)
    for i in range(per):
        x_scr[i * STRETCH : (i + 1) * STRETCH, :] = pick(rows_ref, placing[micro, step * per + i])
        cot_scr[i * STRETCH : (i + 1) * STRETCH, :] = pick(cot_ref, placing[micro, step * per + i])

    x = x_scr[...].astype(f32)
    n, _ = standardize(x)
    normed = (n * gain_one + shift_one).astype(bf16)
    for part in range(2):
        at = slice(part * MODEL, (part + 1) * MODEL)
        qkv_ref[:, at] = featured(nn(normed, w_qkv[:, at]) + b_qkv[:, at])
    at = slice(2 * MODEL, 3 * MODEL)
    qkv_ref[:, at] = (nn(normed, w_qkv[:, at]) + b_qkv[:, at]).astype(bf16)

    for chunk in range(TILE // CHUNK):
        rows = slice(chunk * CHUNK, (chunk + 1) * CHUNK)
        r0 = flag(restart[micro, step * per + 2 * chunk])
        r1 = flag(restart[micro, step * per + 2 * chunk + 1])
        mask = causal(r1, False)
        keep_low = jnp.where(upper, 1.0, 1.0 - r1)
        keep_key = jnp.where(upper, 1.0 - r1, 1.0)
        for pair in range(PAIRS):
            q = qkv_ref[rows, pair * PAIR : (pair + 1) * PAIR]
            k = qkv_ref[rows, MODEL + pair * PAIR : MODEL + (pair + 1) * PAIR]
            v = qkv_ref[rows, 2 * MODEL + pair * PAIR : 2 * MODEL + (pair + 1) * PAIR]
            state = carry[pair] * (1.0 - r0)
            state_b = state.astype(bf16)
            state_low = (state - state_b.astype(f32)).astype(bf16)
            states_out[chunk, pair * PAIR : (pair + 1) * PAIR, :] = jnp.concatenate(
                [
                    state_b[:, :PAIR],
                    jnp.where(
                        inner < 2, state_b[:, PAIR:], jnp.where(inner == 2, state_low[:, PAIR:], zero_s)
                    ),
                    state_low[:, :PAIR],
                ],
                axis=1,
            )
            mixing = nt(q, by_head(k, CHUNK)) * mask
            values = jnp.concatenate([by_head(v, CHUNK), ones_both], axis=1)
            out = nn(mixing.astype(bf16), values)
            out = out + nn((q.astype(f32) * keep_low).astype(bf16), state_b)
            inv = 1.0 / out[:, PAIR:]
            att = out[:, :PAIR] * inv
            att_scr[rows, col(pair)] = att
            inv_scr[rows, col(pair)] = inv
            att_b[rows, col(pair)] = att.astype(bf16)
            k_keep = (k.astype(f32) * keep_key).astype(bf16)
            added = tn(k_keep, jnp.concatenate([v, ones_all], axis=1))
            carry[pair] = state * (1.0 - r1) + jnp.where(wide_block, added, 0.0)

    @pl.when(opening)
    def _():
        for copy in arriving:
            copy.wait()

    middle = x_scr[...].astype(f32) + nn(att_b[...], w_out[...]) + b_out
    n, scale = standardize(middle)
    normed = (n * gain + shift).astype(bf16)
    normed_t = normed.T
    cot = cot_scr[...]
    cot_t = cot.T
    ff = w_up.shape[1]
    total = middle + b_down
    up_grad = jnp.zeros((TILE, MODEL), f32)
    for part in range(ff // MODEL):
        at = slice(part * MODEL, (part + 1) * MODEL)
        u = nn(normed, w_up[:, at]) + b_up[:, at]
        u2 = u * u
        t = jnp.tanh(u * (0.7978845608028654 + 0.035677408136300125 * u2))
        half = 0.5 + 0.5 * t
        act = (u * half).astype(bf16)
        rise = 1.5957691216057308 + 0.21406444881780074 * u2
        slope = half + u * half * (1.0 - half) * rise
        g = (nt(cot, w_down[at, :]) * slope).astype(bf16)
        total = total + nn(act, w_down[at, :])
        acc_down[:, at] += nn(cot_t, act)
        vec_out[0:1, at] += jnp.sum(g.astype(f32), axis=0, keepdims=True)
        up_grad = up_grad + nt(g, w_up[:, at])
        acc_up[:, at] += nn(normed_t, g)
        if not final:
            leaving.append(pltpu.make_async_copy(acc_down.at[:, at], far_down.at[:, at], sems.at[6 + 2 * part]))
            leaving.append(pltpu.make_async_copy(acc_up.at[:, at], far_up.at[:, at], sems.at[7 + 2 * part]))
            start_all(closing, leaving[-2:])
    total = total.astype(bf16)
    for i in range(per):
        put(result, placing[micro, step * per + i], total[i * STRETCH : (i + 1) * STRETCH, :])

    cot_f = cot.astype(f32)
    vec_out[1:2, :MODEL] += jnp.sum(up_grad * n, axis=0, keepdims=True)
    vec_out[1:2, MODEL : 2 * MODEL] += jnp.sum(up_grad, axis=0, keepdims=True)
    vec_out[1:2, 3 * MODEL : 4 * MODEL] += jnp.sum(cot_f, axis=0, keepdims=True)
    branch = (cot_f + norm_back(up_grad, gain, n, scale)).astype(bf16)
    branch_out[...] = branch
    vec_out[1:2, 2 * MODEL : 3 * MODEL] += jnp.sum(branch.astype(f32), axis=0, keepdims=True)
    grad_att = nt(branch, w_out[...])
    acc_out[...] += tn(att_b[...], branch)
    if not final:
        leaving.append(pltpu.make_async_copy(acc_out, far_out, sems.at[6 + 2 * (ff // MODEL)]))
        start_all(closing, leaving[-1:])
    lane = lanes(CHUNK, PAIR) % HEAD_DIM
    for chunk in range(TILE // CHUNK):
        rows = slice(chunk * CHUNK, (chunk + 1) * CHUNK)
        o0 = flag(opened[micro, step * per + 2 * chunk])
        o1 = flag(opened[micro, step * per + 2 * chunk + 1])
        keep = jnp.where(upper, o0, o1)
        for pair in range(PAIRS):
            inv = inv_scr[rows, col(pair)]
            gn = (grad_att[rows, col(pair)].astype(bf16).astype(f32) * inv).astype(bf16)
            product = gn.astype(f32) * att_scr[rows, col(pair)]
            high = product.astype(bf16)
            low_part = (product - high.astype(f32)).astype(bf16)
            gd = -nn(jnp.concatenate([high, low_part], axis=1), ones_twice)
            gd_high = gd.astype(bf16)
            gd_low = (gd - gd_high.astype(f32)).astype(bf16)
            zero = jnp.zeros_like(gd_high)
            gn_out[rows, col(pair)] = gn
            gd_out[rows, col(pair)] = jnp.where(
                (lane == 0) | (lane == 2), gd_high, jnp.where(lane == 1, gd_low, zero)
            )
            q = qkv_ref[rows, pair * PAIR : (pair + 1) * PAIR].astype(f32) * keep
            back[pair] += tn(q.astype(bf16), gn)
            back_sum[:, col(pair)] += jnp.sum(q * gd, axis=0, keepdims=True)

    @pl.when(step == pl.num_programs(1) - 1)
    def _():
        for pair in range(PAIRS):
            pack_state(state_out, pair, back[pair], back_sum[:, col(pair)])

    if not final:

        @pl.when(closing)
        def _():
            for copy in leaving:
                copy.wait()

    else:

        @pl.when(closing)
        def _():
            parts = ff // MODEL
            devices = 2 * keep_out.shape[0]
            less = MODEL // devices
            more = parts * less
            for part in range(parts):
                at = slice(part * MODEL, (part + 1) * MODEL)
                turned[at, :] = acc_down[:, at].T
            for j in range(devices):
                d = owner[j]
                target = keep_out if j < devices // 2 else send_out
                seat = j % (devices // 2)
                here = pl.ds(pl.multiple_of(d * less, less), less)
                for part in range(parts):
                    target[seat, part * less : (part + 1) * less, :] = acc_up[
                        here, part * MODEL : (part + 1) * MODEL
                    ].astype(target.dtype)
                there = pl.ds(pl.multiple_of(d * more, more), more)
                target[seat, more : 2 * more, :] = turned[there, :].astype(target.dtype)
                target[seat, 2 * more :, :] = acc_out[here, :].astype(target.dtype)


def run_mid(tables, first, members, target, rows, cot, inc, weights, vec, before, owner):
    micro, count = tables[0].shape
    width = rows.shape[-1]
    ff = weights[2].shape[1]
    count = count * STRETCH
    tiles = count // TILE
    total = members * count
    resumes, final = before is not None, owner is not None
    f32_sums = [(width, ff), (width, ff), (MODEL, width)]
    out_specs = [
        group_spec(target.shape, 0),
        tile_spec(3 * MODEL, tiles),
        tile_spec(width, tiles),
        tile_spec(MODEL, tiles),
        tile_spec(MODEL, tiles),
        states_spec(tiles),
        member_spec(),
        fixed((8, ff)),
    ]
    out_shape = [
        jax.ShapeDtypeStruct(target.shape, bf16),
        jax.ShapeDtypeStruct((total, 3 * MODEL), bf16),
        jax.ShapeDtypeStruct((total, width), bf16),
        jax.ShapeDtypeStruct((total, MODEL), bf16),
        jax.ShapeDtypeStruct((total, MODEL), bf16),
        jax.ShapeDtypeStruct((total // CHUNK, MODEL, 3 * PAIR), bf16),
        jax.ShapeDtypeStruct((members, HEAD_DIM + 8, MODEL), f32),
        jax.ShapeDtypeStruct((8, ff), f32),
    ]
    if final:
        devices = owner.shape[0]
        half = (devices // 2, (2 * ff + MODEL) // devices, MODEL)
        out_specs += [fixed(half), fixed(half)]
        out_shape += [jax.ShapeDtypeStruct(half, f32), jax.ShapeDtypeStruct(half, bf16)]
    else:
        out_specs += [ANYWHERE] * 3
        out_shape += [jax.ShapeDtypeStruct(shape, f32) for shape in f32_sums]
    if not final:
        owner = jnp.zeros((8,), jnp.int32)
    scratch = [pltpu.VMEM((ff, width), f32)] if final else []
    scratch += [pltpu.VMEM(shape, f32) for shape in f32_sums]
    scratch += [
        pltpu.VMEM((PAIRS, PAIR, 2 * PAIR), f32),
        pltpu.VMEM((PAIRS, PAIR, PAIR), f32),
        pltpu.VMEM((1, MODEL), f32),
        pltpu.VMEM((TILE, MODEL), f32),
        pltpu.VMEM((TILE, MODEL), f32),
        pltpu.VMEM((TILE, MODEL), bf16),
        pltpu.VMEM((TILE, width), bf16),
        pltpu.VMEM((TILE, width), bf16),
    ]
    scratch += [pltpu.VMEM(item.shape, bf16) for item in weights[1:]]
    scratch.append(pltpu.SemaphoreType.DMA((7 + 2 * (ff // MODEL),)))
    return pl.pallas_call(
        functools.partial(mid_kernel, first=first, resumes=resumes, final=final),
        name="middle",
        grid_spec=pltpu.PrefetchScalarGridSpec(
            num_scalar_prefetch=4,
            grid=(members, tiles),
            in_specs=[
                ANYWHERE,
                group_spec(rows.shape, first),
                group_spec(cot[0].shape, cot[1]),
                member_spec(first),
            ]
            + [fixed(weights[0].shape), fixed(vec.shape)]
            + [ANYWHERE] * (6 if resumes else 3),
            out_specs=out_specs,
            scratch_shapes=scratch,
        ),
        out_shape=out_shape,
        compiler_params=params(),
        input_output_aliases={4: 0},
        cost_estimate=pl.CostEstimate(
            flops=members * (24 << 30), bytes_accessed=members << 24, transcendentals=0
        ),
    )(*tables, owner, target, rows, cot[0], inc, weights[0], vec, *weights[1:], *(before or ()))


def back_kernel(
    placing,
    restart,
    owner,
    _,
    rows_ref,
    qkv_ref,
    gn_ref,
    gd_ref,
    branch_ref,
    states_ref,
    inc_ref,
    weight,
    vec,
    owner_col,
    *refs,
    first,
    resumes,
    final,
    widths,
    sums,
):
    gain, shift = vector(vec, GAIN_ONE), vector(vec, SHIFT_ONE)
    before, refs = (refs[:1], refs[1:]) if resumes else ((), refs)
    vec_others, refs = refs[:sums], refs[sums:]
    grad_rows, vec_out = refs[:2]
    refs = refs[2:]
    if final:
        keep_out, send_out, acc = refs[:3]
        refs = refs[3:]
    else:
        acc = refs[0]
        refs = refs[1:]
    carry, x_scr, mixed_scr = refs[:3]
    sems = refs[3] if resumes else None
    member, step = pl.program_id(0), pl.program_id(1)
    micro = first + member
    per = TILE // STRETCH
    tile = pl.num_programs(1) - 1 - step
    opening = (member == 0) & (step == 0)
    lane = lanes(CHUNK, PAIR)
    inner = lane % HEAD_DIM

    @pl.when(opening)
    def _():
        vec_out[...] = jnp.zeros_like(vec_out)
        if resumes:
            pltpu.make_async_copy(before[0], acc, sems.at[0]).start()
        else:
            acc[...] = jnp.zeros_like(acc)

    @pl.when(step == 0)
    def _():
        only = jnp.concatenate([jnp.ones((PAIR, PAIR), f32), jnp.where(inner == 0, 1.0, 0.0)], axis=1)
        for pair in range(PAIRS):
            carry[pair] = unpack_state(inc_ref[0], pair) * only

    block = same_head()
    wide_block = jnp.concatenate([block, block], axis=1)
    upper = sublanes(CHUNK, PAIR) < STRETCH
    marks = jnp.where((inner < 2) | (inner == 3), 1.0, 0.0).astype(bf16)
    mark_low = jnp.where(lane < 2, 1.0, 0.0).astype(bf16)
    mark_high = jnp.where((lane == HEAD_DIM) | (lane == HEAD_DIM + 1), 1.0, 0.0).astype(bf16)
    marks_both = jnp.concatenate([mark_low, mark_high], axis=0)
    for i in range(per):
        x_scr[i * STRETCH : (i + 1) * STRETCH, :] = pick(rows_ref, placing[micro, tile * per + i])

    for chunk in reversed(range(TILE // CHUNK)):
        rows = slice(chunk * CHUNK, (chunk + 1) * CHUNK)
        r0 = flag(restart[micro, tile * per + 2 * chunk])
        r1 = flag(restart[micro, tile * per + 2 * chunk + 1])
        r2 = flag(restart[micro, tile * per + 2 * chunk + 2])
        mask = causal(r1, False)
        mask_t = causal(r1, True)
        keep_low = jnp.where(upper, 1.0, 1.0 - r1)
        keep_key = jnp.where(upper, 1.0 - r1, 1.0)
        for pair in range(PAIRS):
            q = qkv_ref[rows, pair * PAIR : (pair + 1) * PAIR]
            k = qkv_ref[rows, MODEL + pair * PAIR : MODEL + (pair + 1) * PAIR]
            v = qkv_ref[rows, 2 * MODEL + pair * PAIR : 2 * MODEL + (pair + 1) * PAIR]
            gn = gn_ref[rows, col(pair)]
            gdx = gd_ref[rows, col(pair)]
            state = states_ref[chunk, pair * PAIR : (pair + 1) * PAIR, :]
            grown = carry[pair] * (1.0 - r2)
            grown_b = grown.astype(bf16)
            rest = grown - grown_b.astype(f32)
            grown_low = rest[:, :PAIR].astype(bf16)
            z_low = pltpu.roll(rest[:, PAIR:], 3, 1).astype(bf16)
            z_both = jnp.where(inner < 2, grown_b[:, PAIR:], jnp.where(inner == 3, z_low, jnp.zeros_like(z_low)))
            grown_x = jnp.concatenate([grown_b[:, :PAIR], z_both], axis=1)
            k2 = by_head(k, CHUNK)
            q2 = by_head(q, CHUNK)
            v2 = by_head(v, CHUNK)
            gn2 = by_head(gn, CHUNK)
            gd2 = by_head(gdx, CHUNK)
            both = jnp.concatenate([gn, gdx], axis=1)
            mixing_t = (nt(k, q2) * mask_t).astype(bf16)
            g_mix = (nt(both, jnp.concatenate([v2, marks_both], axis=1)) * mask).astype(bf16)
            v_marks = jnp.concatenate([v, marks], axis=1)
            g_mix_t = (nt(v_marks, jnp.concatenate([gn2, gd2], axis=1)) * mask_t).astype(bf16)
            dq = nn(g_mix, k2) + (nt(both, state[:, : 2 * PAIR]) + nt(gn, state[:, 2 * PAIR :])) * keep_low
            dk = nn(g_mix_t, q2) + (nt(v_marks, grown_x) + nt(v, grown_low)) * keep_key
            dv = nn(mixing_t, gn2) + nn(k, grown_b[:, :PAIR]) * keep_key
            q_keep = (q.astype(f32) * keep_low).astype(bf16)
            added = tn(q_keep, both)
            carry[pair] = (grown * (1.0 - r1) + jnp.where(wide_block, added, 0.0)) * (1.0 - r0)
            mixed_scr[rows, pair * PAIR : (pair + 1) * PAIR] = (
                dq * jnp.minimum(q.astype(f32), 1.0)
            ).astype(bf16)
            mixed_scr[rows, MODEL + pair * PAIR : MODEL + (pair + 1) * PAIR] = (
                dk * jnp.minimum(k.astype(f32), 1.0)
            ).astype(bf16)
            mixed_scr[rows, 2 * MODEL + pair * PAIR : 2 * MODEL + (pair + 1) * PAIR] = dv.astype(bf16)

    mixed = mixed_scr[...]
    vec_out[0:1, :] += jnp.sum(mixed.astype(f32), axis=0, keepdims=True)
    upstream = nt(mixed, weight[...])
    n, scale = standardize(x_scr[...].astype(f32))
    normed_t = (n * gain + shift).astype(bf16).T
    if resumes:

        @pl.when(opening)
        def _():
            pltpu.make_async_copy(before[0], acc, sems.at[0]).wait()

    for part in range(3):
        at = slice(part * MODEL, (part + 1) * MODEL)
        acc[:, at] += nn(normed_t, mixed[:, at])
    vec_out[1:2, :MODEL] += jnp.sum(upstream * n, axis=0, keepdims=True)
    vec_out[1:2, MODEL : 2 * MODEL] += jnp.sum(upstream, axis=0, keepdims=True)
    total = (branch_ref[...].astype(f32) + norm_back(upstream, gain, n, scale)).astype(bf16)
    for i in range(per):
        put(grad_rows, placing[micro, tile * per + i], total[i * STRETCH : (i + 1) * STRETCH, :])

    if final:

        @pl.when((member == pl.num_programs(0) - 1) & (step == pl.num_programs(1) - 1))
        def _():
            half = keep_out.shape[0]
            devices = 2 * half
            less = MODEL // devices
            for j in range(devices):
                here = pl.ds(pl.multiple_of(owner[j] * less, less), less)
                target = keep_out if j < half else send_out
                for part in range(3):
                    target[j % half, part * less : (part + 1) * less, :] = acc[
                        here, part * MODEL : (part + 1) * MODEL
                    ].astype(target.dtype)
            mid = sum(ref[...] for ref in vec_others if ref.shape[1] == vec_others[0].shape[1])
            rear = vec_out[...] + sum(
                ref[...] for ref in vec_others if ref.shape[1] != vec_others[0].shape[1]
            )
            sources = (
                rear[1:2, :MODEL],
                rear[1:2, MODEL : 2 * MODEL],
                rear[0:1, : 2 * MODEL],
                rear[0:1, 2 * MODEL :],
                mid[1:2, 2 * MODEL : 3 * MODEL],
                mid[1:2, :MODEL],
                mid[1:2, MODEL : 2 * MODEL],
                mid[0:1, :],
                mid[1:2, 3 * MODEL : 4 * MODEL],
            )
            rows16 = sublanes(16, MODEL)
            pieces = []
            for source, width in zip(sources, widths, strict=True):
                size = devices * width
                mine = (lanes(devices, size) // width) == owner_col[...]
                picked = jnp.where(mine, source, 0.0)
                gather = jnp.where(
                    (sublanes(size, PAIR) % width) == lanes(size, PAIR), 1.0, 0.0
                ).astype(bf16)
                high = picked.astype(bf16)
                low = (picked - high.astype(f32)).astype(bf16)
                pieces.append(nn(high, gather) + nn(low, gather))
            rest = jnp.zeros((1, MODEL - PAIR), f32)
            for j in range(devices):
                block16 = jnp.zeros((16, MODEL), f32)
                for v, piece in enumerate(pieces):
                    row = jnp.concatenate([piece[j : j + 1, :], rest], axis=1)
                    block16 = block16 + jnp.where(rows16 == v, row, 0.0)
                target = keep_out if j < half else send_out
                target[j % half, 3 * less :, :] = block16.astype(target.dtype)


def run_back(tables, first, members, target, rows, mid, inc, weight, vec, before, owner, others, widths):
    (group, seat), (saved, at) = target, mid
    micro, count = tables[0].shape
    width = rows.shape[-1]
    count = count * STRETCH
    tiles = count // TILE
    resumes, final = before is not None, owner is not None
    devices = lax.axis_size(BOTH) if final else 0
    if not final:
        owner = jnp.zeros((8,), jnp.int32)
        others = []
    half = (devices // 2, 3 * MODEL // max(devices, 1) + 16, MODEL)
    out_specs = [group_spec(group.shape, seat), fixed((8, 3 * MODEL))]
    out_shape = [
        jax.ShapeDtypeStruct(group.shape, bf16),
        jax.ShapeDtypeStruct((8, 3 * MODEL), f32),
    ]
    scratch = []
    if final:
        out_specs += [fixed(half), fixed(half)]
        out_shape += [jax.ShapeDtypeStruct(half, f32), jax.ShapeDtypeStruct(half, bf16)]
        scratch.append(pltpu.VMEM((width, 3 * MODEL), f32))
    else:
        out_specs.append(fixed((width, 3 * MODEL)))
        out_shape.append(jax.ShapeDtypeStruct((width, 3 * MODEL), f32))
    scratch += [
        pltpu.VMEM((PAIRS, PAIR, 2 * PAIR), f32),
        pltpu.VMEM((TILE, width), bf16),
        pltpu.VMEM((TILE, 3 * MODEL), bf16),
    ]
    if resumes:
        scratch.append(pltpu.SemaphoreType.DMA((1,)))

    def tile(width_):
        return pl.BlockSpec((TILE, width_), lambda i, t, *_: ((at + i) * tiles + tiles - 1 - t, 0))

    return pl.pallas_call(
        functools.partial(
            back_kernel, first=first, resumes=resumes, final=final, widths=widths, sums=len(others)
        ),
        name="back",
        grid_spec=pltpu.PrefetchScalarGridSpec(
            num_scalar_prefetch=3,
            grid=(members, tiles),
            in_specs=[
                ANYWHERE,
                group_spec(rows.shape, first),
                tile(3 * MODEL),
                tile(MODEL),
                tile(MODEL),
                tile(width),
                pl.BlockSpec(
                    (TILE // CHUNK, MODEL, 3 * PAIR),
                    lambda i, t, *_: ((at + i) * tiles + tiles - 1 - t, 0, 0),
                ),
                member_spec(at),
                fixed(weight.shape),
                fixed(vec.shape),
                fixed((owner.shape[0], 1)),
            ]
            + ([ANYWHERE] if resumes else [])
            + [fixed(item.shape) for item in others],
            out_specs=out_specs,
            scratch_shapes=scratch,
        ),
        out_shape=out_shape,
        input_output_aliases={3: 0},
        compiler_params=params(),
        cost_estimate=pl.CostEstimate(
            flops=members * (15 << 30), bytes_accessed=members << 24, transcendentals=0
        ),
    )(
        tables[0],
        tables[1],
        owner,
        group,
        rows,
        saved[1],
        saved[3],
        saved[4],
        saved[2],
        saved[5],
        inc,
        weight,
        vec,
        owner[:, None],
        *(() if before is None else (before,)),
        *others,
    )


def send_kernel(slot, source, target):
    micro = pl.program_id(0)
    for i in range(source.shape[1]):
        put(target, slot[micro, i], source[0, i])


def run_send(slot, rows, first, members):
    micro, count, width = rows.shape
    stretches = count // STRETCH
    groups = lax.axis_size("dp")
    shape = (groups, members, stretches // groups, STRETCH, width)
    return pl.pallas_call(
        send_kernel,
        name="send",
        grid_spec=pltpu.PrefetchScalarGridSpec(
            num_scalar_prefetch=1,
            grid=(members,),
            in_specs=[
                pl.BlockSpec((1, stretches, STRETCH, width), lambda i, *_: (first + i, 0, 0, 0))
            ],
            out_specs=pl.BlockSpec((groups, 1) + shape[2:], lambda i, *_: (0, i, 0, 0, 0)),
        ),
        out_shape=jax.ShapeDtypeStruct(shape, rows.dtype),
        compiler_params=pltpu.CompilerParams(vmem_limit_bytes=VMEM_LIMIT),
        cost_estimate=pl.CostEstimate(
            flops=0, bytes_accessed=4 * members * count * width, transcendentals=0
        ),
    )(slot[first : first + members], rows.reshape(micro, stretches, STRETCH, width))


def land_kernel(slot, _, source, target):
    micro = pl.program_id(0)
    for i in range(target.shape[1]):
        target[0, i] = pick(source, slot[micro, i])


def run_land(slot, landed, output, first):
    members = landed.shape[1]
    shape = output.shape
    block = (landed.shape[0], 1) + landed.shape[2:]
    return pl.pallas_call(
        land_kernel,
        name="land",
        grid_spec=pltpu.PrefetchScalarGridSpec(
            num_scalar_prefetch=1,
            grid=(members,),
            in_specs=[
                pl.BlockSpec(memory_space=pl.ANY),
                pl.BlockSpec(block, lambda i, *_: (0, i, 0, 0, 0)),
            ],
            out_specs=pl.BlockSpec((1,) + shape[1:], lambda i, *_: (first + i, 0, 0, 0)),
        ),
        out_shape=jax.ShapeDtypeStruct(shape, output.dtype),
        input_output_aliases={1: 0},
        compiler_params=pltpu.CompilerParams(vmem_limit_bytes=VMEM_LIMIT),
        cost_estimate=pl.CostEstimate(flops=0, bytes_accessed=4 * landed.size, transcendentals=0),
    )(slot[first : first + members], output, landed)


def blank(shape):
    return pl.pallas_call(
        lambda ref: None,
        name="blank",
        out_specs=pl.BlockSpec(memory_space=pl.ANY),
        out_shape=jax.ShapeDtypeStruct(shape, bf16),
    )()


def index_tables(lengths, stretch_order, count):
    fsdp = lax.axis_size("fsdp")
    groups = lax.axis_size("dp")
    device = lax.axis_index(BOTH)
    base = device * count
    within = jnp.arange(count, dtype=jnp.int32)
    mine = base + within
    place = jnp.arange(stretch_order.shape[1], dtype=jnp.int32)
    here = place[None, None, :]
    landing = jnp.sum(
        jnp.where(stretch_order[:, None, :] == mine[None, :, None], here, 0), axis=-1
    )
    slot = jnp.sum((landing[:, None, :] < landing[:, :, None]).astype(jnp.int32), axis=-1)
    arrival = jnp.sum(
        jnp.where(here == mine[None, :, None], stretch_order[:, None, :], 0), axis=-1
    )
    source = arrival // count // fsdp
    ahead = (source[:, None, :] == source[:, :, None]) & (
        within[None, None, :] < within[None, :, None]
    )
    placing = source * (count // groups) + jnp.sum(ahead.astype(jnp.int32), axis=-1)
    index = jnp.arange(lengths.shape[1], dtype=jnp.int32)
    starts = jnp.sum(
        jnp.where(index[None, None, :] < index[None, :, None], lengths[:, None, :], 0), axis=-1
    )
    edge = base + jnp.arange(count + 1, dtype=jnp.int32)
    restart = jnp.any(starts[:, None, :] == edge[None, :, None], axis=-1).astype(jnp.int32)
    restart = jnp.where(edge[None, :] == stretch_order.shape[1], 1, restart)
    opened = 1 - jnp.any(
        (starts[:, None, :] >= base) & (starts[:, None, :] <= mine[None, :, None]), axis=-1
    ).astype(jnp.int32)
    last = base + count - 1
    closing = 1 - jnp.any(
        (starts[:, None, :] > mine[None, :, None]) & (starts[:, None, :] <= last), axis=-1
    ).astype(jnp.int32)
    hops = -(-(LONGEST - 1) // count)
    hop = jnp.arange(hops, dtype=jnp.int32)
    reach_back = base - 1 - hop * count
    from_before = 1.0 - jnp.any(
        (starts[:, None, :] > reach_back[None, :, None]) & (starts[:, None, :] <= base), axis=-1
    ).astype(f32)
    reach_on = base + (hop + 1) * count
    from_after = 1.0 - jnp.any(
        (starts[:, None, :] > last) & (starts[:, None, :] <= reach_on[None, :, None]), axis=-1
    ).astype(f32)
    first = base - hop * count
    unbroken = 1.0 - jnp.any(
        (starts[:, None, :] >= first[None, :, None]) & (starts[:, None, :] <= last), axis=-1
    ).astype(f32)
    return slot, placing, restart, opened, closing, from_before, from_after, unbroken


def exchange(states, hops, forward):
    size = lax.axis_size("fsdp")
    got = []
    for hop in range(min(hops, size - 1)):
        step = hop + 1
        pairs = [(i, i + step) if forward else (i + step, i) for i in range(size - step)]
        got.append(lax.ppermute(states, "fsdp", pairs))
    return got


def passed_on(states, weights, unbroken, beside):
    size = lax.axis_size("fsdp")
    total, own, step = jnp.zeros_like(states), states, 1
    while step <= weights.shape[1] and step < size:
        got = lax.ppermute(own, "fsdp", [(i, i + step) for i in range(size - step)])
        total = total + got * weights[:, step - 1, None, None]
        own = after(own + got * unbroken[:, step - 1, None, None], beside)
        step *= 2
    return total


def joined(got, weights, *others):
    got = after(got, *others)
    return sum(item * weights[:, hop, None, None] for hop, item in enumerate(got))


def halving_stages():
    stages = []
    dp, fsdp = lax.axis_size("dp"), lax.axis_size("fsdp")
    if dp > 1:
        stages.append(("dp", 1))
    bit = 1
    while bit < fsdp:
        stages.append(("fsdp", bit))
        bit *= 2
    bit = 2
    while bit < dp:
        stages.append(("dp", bit))
        bit *= 2
    return stages


def order_tables():
    stages = halving_stages()
    fsdp = lax.axis_size("fsdp")
    devices = lax.axis_size(BOTH)
    me = lax.axis_index(BOTH)
    index = jnp.arange(devices, dtype=jnp.int32)
    bits = [bit * (fsdp if axis == "dp" else 1) for axis, bit in stages]
    place = jnp.zeros((devices,), jnp.int32)
    owner = jnp.zeros((devices,), jnp.int32)
    for s, bit in enumerate(bits):
        rank = len(bits) - 1 - s
        place = place + jnp.where(((index ^ me) & bit) != 0, 1 << rank, 0)
        owner = owner + jnp.where(((index >> rank) & 1) != 0, bit, 0)
    return place, owner ^ me


def after(x, *others):
    return lax.optimization_barrier((x, others))[0]


def swap(x, axis, bit):
    return lax.ppermute(x, axis, [(i, i ^ bit) for i in range(lax.axis_size(axis))])


def gather_halves(x, ties):
    stages = list(reversed(halving_stages()))
    steps = []
    for s, (axis, bit) in enumerate(stages[:-1]):
        if s in ties:
            x = after(x, ties[s])
        x = jnp.concatenate([x, swap(x, axis, bit)], axis=0)
        steps.append(x)
    return (x, swap(x, *stages[-1])), steps


def scatter_step(keep, send, s):
    stages = halving_stages()
    return scatter_join(keep, swap(send, *stages[s]), s == len(stages) - 1)


def scatter_join(keep, got, last):
    if last:
        return keep[0] + got[0].astype(f32), None
    half = keep.shape[0] // 2
    send = (keep[half:] + got[half:].astype(f32)).astype(bf16)
    return keep[:half] + got[:half].astype(f32), send


def finish_kernel(keep, got, qkv, *vectors):
    total = keep[0] + got[0].astype(f32)
    rows = qkv.shape[0]
    for part in range(3):
        qkv[:, part * MODEL : (part + 1) * MODEL] = total[part * rows : (part + 1) * rows, :]
    for v, ref in enumerate(vectors):
        ref[...] = total[3 * rows + v : 3 * rows + v + 1, : ref.shape[1]]


def run_finish(keep, got, widths):
    rows = (keep.shape[1] - 16) // 3
    return pl.pallas_call(
        finish_kernel,
        name="finish",
        out_shape=[jax.ShapeDtypeStruct((rows, 3 * MODEL), f32)]
        + [jax.ShapeDtypeStruct((1, width), f32) for width in widths],
    )(keep, got)


def pack_kernel(qkv, out, up, down, *refs):
    *small, first, second = refs
    rows = qkv.shape[0]
    for c in range(3):
        first[0, c * rows : (c + 1) * rows, :] = qkv[:, c * MODEL : (c + 1) * MODEL]
    row = sublanes(16, PAIR)
    side = jnp.zeros((16, PAIR), f32)
    for v, item in enumerate(small):
        width = item.shape[1]
        spread = jnp.where(sublanes(width, PAIR) == lanes(width, PAIR), 1.0, 0.0).astype(bf16)
        tall = jnp.broadcast_to(item[...].astype(f32), (16, width)).astype(bf16)
        side = side + jnp.where(row == v, nn(tall, spread), 0.0)
    side = jnp.concatenate([side, jnp.zeros((16, MODEL - PAIR), f32)], axis=1)
    first[0, 3 * rows : 3 * rows + 16, :] = side.astype(bf16)
    parts = up.shape[1] // MODEL
    for c in range(parts):
        second[0, c * rows : (c + 1) * rows, :] = up[:, c * MODEL : (c + 1) * MODEL]
    second[0, parts * rows : 2 * parts * rows, :] = down[...]
    second[0, 2 * parts * rows :, :] = out[...]


def run_pack(qkv, out, up, down, small):
    rows = qkv.shape[0]
    parts = up.shape[1] // MODEL
    return pl.pallas_call(
        pack_kernel,
        name="pack",
        out_shape=[
            jax.ShapeDtypeStruct((1, 3 * rows + 16, MODEL), bf16),
            jax.ShapeDtypeStruct((1, (2 * parts + 1) * rows, MODEL), bf16),
        ],
    )(qkv, out, up, down, *(item[None] for item in small))


def sort_first_kernel(place, own, got, owner, qkv, vectors, *, widths):
    half, total, _ = own.shape
    rows = total // 4

    def part(d):
        p = place[d]
        q = lax.rem(p, half)
        return jnp.where(p < half, own[q, : 3 * rows, :], got[q, : 3 * rows, :])

    for d in range(2 * half):
        block = part(d)
        for c in range(3):
            qkv[d * rows : (d + 1) * rows, c * MODEL : (c + 1) * MODEL] = block[
                c * rows : (c + 1) * rows, :
            ]
    small = jnp.concatenate(
        [own[:, 3 * rows :, :PAIR].astype(f32), got[:, 3 * rows :, :PAIR].astype(f32)], axis=0
    )
    row = lax.broadcasted_iota(jnp.int32, small.shape, 1)
    vectors[...] = jnp.zeros_like(vectors)
    for v, width in enumerate(widths):
        values = jnp.sum(jnp.where(row == v, small, 0.0), axis=1)
        size = 2 * half * width
        lane = lanes(PAIR, size) % width
        spread = jnp.where(lane == sublanes(PAIR, size), 1.0, 0.0).astype(bf16)
        wide = nn(values.astype(bf16), spread)
        mine = (lanes(2 * half, size) // width) == owner[...]
        vectors[v : v + 1, :size] = jnp.sum(jnp.where(mine, wide, 0.0), axis=0, keepdims=True)


def run_sort_first(place, owner, own, got, widths):
    devices = place.shape[0]
    rows = own.shape[1] // 4
    vmem = pl.BlockSpec(memory_space=pltpu.VMEM)
    return pl.pallas_call(
        functools.partial(sort_first_kernel, widths=widths),
        name="sort_first",
        in_specs=[pl.BlockSpec(memory_space=pltpu.SMEM), vmem, vmem, vmem],
        out_specs=[vmem, vmem],
        out_shape=[
            jax.ShapeDtypeStruct((devices * rows, 3 * MODEL), bf16),
            jax.ShapeDtypeStruct((8, devices * max(widths)), f32),
        ],
        compiler_params=pltpu.CompilerParams(vmem_limit_bytes=VMEM_LIMIT),
    )(place, own, got, owner[:, None])


def sort_second_kernel(gathered, up, down, out):
    devices, total, _ = gathered.shape
    parts = up.shape[1] // MODEL
    rows = total // (2 * parts + 1)
    tall = parts * rows
    for d in range(devices):
        for c in range(parts):
            up[d * rows : (d + 1) * rows, c * MODEL : (c + 1) * MODEL] = gathered[
                d, c * rows : (c + 1) * rows, :
            ]
        down[d * tall : (d + 1) * tall, :] = gathered[d, tall : 2 * tall, :]
        out[d * rows : (d + 1) * rows, :] = gathered[d, 2 * tall :, :]


def run_sort_second(gathered, ff):
    devices = gathered.shape[0]
    rows = gathered.shape[1] // (2 * (ff // MODEL) + 1)
    vmem = pl.BlockSpec(memory_space=pltpu.VMEM)
    return pl.pallas_call(
        sort_second_kernel,
        name="sort_second",
        in_specs=[vmem],
        out_specs=[vmem, vmem, vmem],
        out_shape=[
            jax.ShapeDtypeStruct((devices * rows, ff), bf16),
            jax.ShapeDtypeStruct((ff, MODEL), bf16),
            jax.ShapeDtypeStruct((devices * rows, MODEL), bf16),
        ],
        compiler_params=pltpu.CompilerParams(vmem_limit_bytes=VMEM_LIMIT),
    )(gathered)


def gather_all(x):
    return lax.all_gather(x, BOTH, axis=0, tiled=True)


def scatter_all(x):
    return lax.psum_scatter(x, BOTH, scatter_dimension=0, tiled=True)


def to_dp(group):
    return lax.all_to_all(group, "dp", split_axis=0, concat_axis=0, tiled=True)


def groups_of(micro):
    return [(0, micro - 1), (micro - 1, 1)] if micro > 1 else [(0, 1)]


def find(groups, m):
    for g, (first, members) in enumerate(groups):
        if first <= m < first + members:
            return g, m - first


def body(
    tokens,
    cotangent,
    lengths,
    stretch_order,
    ln1_gain,
    ln1_bias,
    w_qkv,
    b_qkv,
    w_out,
    b_out,
    ln2_gain,
    ln2_bias,
    w_up,
    b_up,
    w_down,
    b_down,
):
    micro, rows, width = tokens.shape
    count = rows // STRETCH
    devices = lax.axis_size(BOTH)
    ff = w_up.shape[1]
    dp = lax.axis_size("dp")
    slot, placing, restart, opened, closing, from_before, from_after, unbroken = index_tables(
        lengths, stretch_order, count
    )
    small = (ln1_gain, ln1_bias, b_qkv, b_out, ln2_gain, ln2_bias, b_up, b_down)
    in_parts = (width // devices) % 16 == 0
    groups = groups_of(micro)
    sent = run_send(slot, tokens, 0, micro)
    if in_parts:
        place, owner = order_tables()
        first_part, second_part = run_pack(w_qkv, w_out, w_up, w_down, small)
        halves, steps = gather_halves(first_part, {1: sent})
        moved = to_dp(after(sent, steps[0]))
        qkv_all, vectors = run_sort_first(
            place, owner, *halves, [item.shape[0] for item in small]
        )
        ready = (qkv_all,)
        second_part = gather_all(second_part)
    else:
        owner, ready = None, ()
        moved = to_dp(sent)
        qkv_all, out_all = gather_all(w_qkv), gather_all(w_out)
        up_all, down_all = gather_all(w_up), gather_all(w_down)
        vectors = [gather_all(item).astype(f32) for item in small]
        vectors = jnp.stack([jnp.pad(item, (0, ff - item.shape[0])) for item in vectors])
    tables = (placing, restart, opened)

    sent_grads = run_send(slot, after(cotangent, *ready), 0, micro)
    hops = from_before.shape[1]
    states = run_state(placing, closing, moved, qkv_all, vectors)
    cots = to_dp(after(sent_grads, states))
    if in_parts:
        up_all, down_all, out_all = run_sort_second(after(second_part, states), ff)
    incoming = passed_on(states, from_before, unbroken, out_all)
    weights = [qkv_all, out_all, up_all, down_all]
    mids, sums = [], None
    for g, (first, members) in enumerate(groups):
        target = blank((dp, members, count // dp, STRETCH, width))
        out = run_mid(
            tables,
            first,
            members,
            target,
            moved,
            (cots, first),
            incoming,
            weights,
            vectors,
            sums,
            owner if g == len(groups) - 1 else None,
        )
        sums = out[8:]
        mids.append(out)
    outgoing = [exchange(out[6], hops, False) for out in mids]
    reach = [from_after[first : first + members] for first, members in groups]
    homes = [to_dp(out[0]) for out in mids]
    sizes = [MODEL, MODEL, 2 * MODEL, MODEL, MODEL, MODEL, MODEL, ff, MODEL]
    widths = [size // devices for size in sizes]
    last = len(halving_stages()) - 1
    late = len(groups) - 1
    outgoing[0] = joined(outgoing[0], reach[0], *([mids[-1][7]] if late else []))
    if in_parts:
        keep, send = sums
        if late:
            send = after(send, outgoing[0], homes[0])
        keep, send = scatter_step(keep, send, 0)
        done = 0
    vec_mid = [f[7] for f in mids]
    vec_back, total = [], None
    grad_rows = []
    for g, (first, members) in enumerate(groups):
        if g:
            outgoing[g] = joined(outgoing[g], reach[g], vec_back[0], homes[g])
            grad_rows[0] = after(grad_rows[0], outgoing[g])
        saved = list(mids[g])
        if in_parts:
            saved[2], keep, send = lax.optimization_barrier((saved[2], keep, send))
            got = swap(send, *halving_stages()[done + 1])
        out = run_back(
            tables,
            first,
            members,
            (blank((dp, members, count // dp, STRETCH, width)), 0),
            moved,
            (saved, 0),
            outgoing[g],
            qkv_all,
            vectors,
            total,
            owner if g == late else None,
            vec_mid + vec_back,
            widths,
        )
        grad_rows.append(out[0])
        vec_back.append(out[1])
        total = out[2]
        if in_parts:
            done += 1
            keep, send = scatter_join(keep, after(got, out[1]), done == last)
            if g == late:
                grad_rows[g] = after(grad_rows[g], keep)
    narrow = out[2:]
    grad_homes = [to_dp(group) for group in grad_rows]
    result = blank((micro, count, STRETCH, width))
    input_grad = blank((micro, count, STRETCH, width))

    def land(output, pieces, *others):
        for (first, _), home in zip(groups, pieces, strict=True):
            output = run_land(slot, after(home, *others), output, first)
        return output

    if in_parts:
        part = width // devices
        narrow_keep, narrow_send = narrow
        if len(groups) > 1:
            narrow_send = after(narrow_send, grad_homes[0], keep, send)
        while done < last:
            done += 1
            keep, send = scatter_step(keep, send, done)
        wide = keep
        parts = ff // MODEL
        grad_up = jnp.concatenate([wide[c * part : (c + 1) * part] for c in range(parts)], axis=1)
        grad_down = wide[parts * part : 2 * parts * part]
        grad_out = wide[2 * parts * part :]
        keep, send = narrow_keep, narrow_send
        for step in range(last):
            keep, send = scatter_step(keep, send, step)
            if step == 0:
                result = land(result, homes, send)
            if step == 1:
                send = after(send, result)
                input_grad = land(input_grad, grad_homes, send)
        send = after(send, input_grad)
        grad_qkv, *owned_vec = run_finish(keep, swap(send, *halving_stages()[last]), widths)
        owned_vec = [item[0] for item in owned_vec]
    else:
        grad_up, grad_down, grad_out = (scatter_all(x) for x in (sums[0], sums[1].T, sums[2]))
        grad_qkv = scatter_all(total)
        mid, back = sum(vec_mid), sum(vec_back)
        vec = (
            back[1, :MODEL],
            back[1, MODEL : 2 * MODEL],
            back[0, : 2 * MODEL],
            back[0, 2 * MODEL :],
            mid[1, 2 * MODEL : 3 * MODEL],
            mid[1, :MODEL],
            mid[1, MODEL : 2 * MODEL],
            mid[0],
            mid[1, 3 * MODEL :],
        )
        owned_vec = [scatter_all(item) for item in vec]
        result, input_grad = land(result, homes), land(input_grad, grad_homes)
    result = result.reshape(micro, rows, width)
    input_grad = input_grad.reshape(micro, rows, width)
    g_gain1, g_bias1, g_qk, g_value, g_bout, g_gain2, g_bias2, g_bup, g_bdown = owned_vec
    return (
        result,
        input_grad,
        g_gain1,
        g_bias1,
        grad_qkv,
        g_qk,
        g_value,
        grad_out,
        g_bout,
        g_gain2,
        g_bias2,
        grad_up,
        g_bup,
        grad_down,
        g_bdown,
    )


def solution(mesh):
    rows = P(None, BOTH, None)
    vector = P(BOTH)
    matrix = P(BOTH, None)
    in_specs = (
        rows, rows, P(), P(), vector, vector, matrix, vector, matrix, vector, vector, vector,
        matrix, vector, matrix, vector,
    )
    out_specs = (
        rows, rows, vector, vector, matrix, vector, vector, matrix, vector, vector, vector,
        matrix, vector, matrix, vector,
    )
    return jax.shard_map(body, mesh=mesh, in_specs=in_specs, out_specs=out_specs, check_vma=False)
```

```python
import functools

import jax
import jax.numpy as jnp
from jax import lax
from jax.experimental import pallas as pl
from jax.experimental.pallas import tpu as pltpu
from jax.sharding import PartitionSpec as P

HEADS = 8
HEAD_DIM = 64
STRETCH = 64
LONGEST = 48
CHUNK = 2 * STRETCH
TILE = 4 * CHUNK
PAIRS = HEADS // 2
PAIR = 2 * HEAD_DIM
MODEL = HEADS * HEAD_DIM
BOTH = ("dp", "fsdp")
EPS = 1e-05
VMEM_LIMIT = 60 * 1024 * 1024

f32 = jnp.float32
bf16 = jnp.bfloat16


def nn(a, b):
    return lax.dot_general(a, b, (((1,), (0,)), ((), ())), preferred_element_type=f32)


def nt(a, b):
    return lax.dot_general(a, b, (((1,), (1,)), ((), ())), preferred_element_type=f32)


def tn(a, b):
    return lax.dot_general(a, b, (((0,), (0,)), ((), ())), preferred_element_type=f32)


def lanes(rows, width):
    return lax.broadcasted_iota(jnp.int32, (rows, width), 1)


def sublanes(rows, width):
    return lax.broadcasted_iota(jnp.int32, (rows, width), 0)


def first_head(rows):
    return lanes(rows, PAIR) < HEAD_DIM


def same_head():
    return (sublanes(PAIR, PAIR) // HEAD_DIM) == (lanes(PAIR, PAIR) // HEAD_DIM)


def by_head(x, rows):
    low = first_head(rows)
    zero = jnp.zeros_like(x)
    return jnp.concatenate([jnp.where(low, x, zero), jnp.where(low, zero, x)], axis=0)


def flag(value):
    return value.astype(f32)


def col(pair):
    return slice(pair * PAIR, (pair + 1) * PAIR)


def standardize(x):
    centre = jnp.mean(x, axis=-1, keepdims=True)
    centred = x - centre
    spread = jnp.mean(centred * centred, axis=-1, keepdims=True)
    scale = lax.rsqrt(spread + EPS)
    return centred * scale, scale


def norm_back(upstream, gain, n, scale):
    ug = upstream * gain
    return scale * (
        ug
        - jnp.mean(ug, axis=-1, keepdims=True)
        - n * jnp.mean(ug * n, axis=-1, keepdims=True)
    )


def unpack_state(block, pair):
    part = block[:HEAD_DIM, col(pair)]
    low = first_head(HEAD_DIM)
    zero = jnp.zeros_like(part)
    state = jnp.concatenate([jnp.where(low, part, zero), jnp.where(low, zero, part)], axis=0)
    row = block[HEAD_DIM : HEAD_DIM + 1, col(pair)]
    eye = sublanes(PAIR, PAIR) == lanes(PAIR, PAIR)
    diagonal = jnp.where(eye, row, 0.0)
    ones = jnp.where(same_head(), 1.0, 0.0).astype(bf16)
    high = diagonal.astype(bf16)
    low_part = (diagonal - high.astype(f32)).astype(bf16)
    sums = nn(high, ones) + nn(low_part, ones)
    return jnp.concatenate([state, sums], axis=1)


def pack_state(ref, pair, state, row):
    low = first_head(HEAD_DIM)
    ref[0, :HEAD_DIM, col(pair)] = jnp.where(low, state[:HEAD_DIM], state[HEAD_DIM:])
    ref[0, HEAD_DIM : HEAD_DIM + 1, col(pair)] = row
    ref[0, HEAD_DIM + 1 :, col(pair)] = jnp.zeros((7, PAIR), f32)


def pick(ref, place):
    per = ref.shape[2]
    return ref[lax.div(place, per), 0, lax.rem(place, per)]


def put(ref, place, value):
    per = ref.shape[2]
    ref[lax.div(place, per), 0, lax.rem(place, per)] = value


def group_spec(shape, first):
    block = (shape[0], 1) + tuple(shape[2:])
    return pl.BlockSpec(block, lambda i, *_: (0, first + i, 0, 0, 0))


def fixed(shape):
    zeros = (0,) * len(shape)
    return pl.BlockSpec(tuple(shape), lambda *_: zeros, pipeline_mode=pl.Buffered(1))


def member_spec(first=0):
    return pl.BlockSpec((1, HEAD_DIM + 8, MODEL), lambda i, *_: (first + i, 0, 0))


def tile_spec(width, tiles, reverse=False):
    if reverse:
        return pl.BlockSpec((TILE, width), lambda i, t, *_: (i * tiles + tiles - 1 - t, 0))
    return pl.BlockSpec((TILE, width), lambda i, t, *_: (i * tiles + t, 0))


def states_spec(tiles, reverse=False):
    block = (TILE // CHUNK, MODEL, 3 * PAIR)
    if reverse:
        return pl.BlockSpec(block, lambda i, t, *_: (i * tiles + tiles - 1 - t, 0, 0))
    return pl.BlockSpec(block, lambda i, t, *_: (i * tiles + t, 0, 0))


def params():
    return pltpu.CompilerParams(
        dimension_semantics=("arbitrary", "arbitrary"), vmem_limit_bytes=VMEM_LIMIT
    )


ANYWHERE = pl.BlockSpec(memory_space=pl.ANY)


GAIN_ONE, SHIFT_ONE, BIAS_QKV, BIAS_OUT, GAIN_TWO, SHIFT_TWO, BIAS_UP, BIAS_DOWN = range(8)


def vector(ref, row):
    width = 3 * MODEL if row == BIAS_QKV else ref.shape[1] if row == BIAS_UP else MODEL
    return ref[row : row + 1, :width]


def featured(mixed):
    return jnp.where(mixed > 0, mixed + 1.0, jnp.exp(jnp.minimum(mixed, 0.0))).astype(bf16)


def state_kernel(placing, closing, rows, weight, vec, state_out, x_scr, acc, sums):
    gain, shift, bias = vector(vec, GAIN_ONE), vector(vec, SHIFT_ONE), vector(vec, BIAS_QKV)
    micro, step = pl.program_id(0), pl.program_id(1)
    per = TILE // STRETCH

    @pl.when(step == 0)
    def _():
        acc[...] = jnp.zeros_like(acc)
        sums[...] = jnp.zeros_like(sums)

    for i in range(per):
        x_scr[i * STRETCH : (i + 1) * STRETCH, :] = pick(rows, placing[micro, step * per + i])
    n, _ = standardize(x_scr[...].astype(f32))
    normed = (n * gain + shift).astype(bf16)
    keep = jnp.concatenate(
        [jnp.full((STRETCH, 1), flag(closing[micro, step * per + i]), f32) for i in range(per)],
        axis=0,
    )
    at = slice(MODEL, 2 * MODEL)
    keys = featured(nn(normed, weight[:, at]) + bias[:, at]).astype(f32) * keep
    sums[...] += jnp.sum(keys, axis=0, keepdims=True)
    keys = keys.astype(bf16)
    at = slice(2 * MODEL, 3 * MODEL)
    values = (nn(normed, weight[:, at]) + bias[:, at]).astype(bf16)
    for pair in range(PAIRS):
        acc[pair] += tn(keys[:, col(pair)], values[:, col(pair)])

    @pl.when(step == pl.num_programs(1) - 1)
    def _():
        for pair in range(PAIRS):
            pack_state(state_out, pair, acc[pair], sums[:, col(pair)])


def run_state(placing, closing, rows, weight, vec):
    micro, count = placing.shape
    width = rows.shape[-1]
    tiles = count * STRETCH // TILE
    return pl.pallas_call(
        state_kernel,
        name="end_state",
        grid_spec=pltpu.PrefetchScalarGridSpec(
            num_scalar_prefetch=2,
            grid=(micro, tiles),
            in_specs=[
                group_spec(rows.shape, 0),
                fixed(weight.shape),
                fixed(vec.shape),
            ],
            out_specs=member_spec(),
            scratch_shapes=[
                pltpu.VMEM((TILE, width), bf16),
                pltpu.VMEM((PAIRS, PAIR, PAIR), f32),
                pltpu.VMEM((1, MODEL), f32),
            ],
        ),
        out_shape=jax.ShapeDtypeStruct((micro, HEAD_DIM + 8, MODEL), f32),
        compiler_params=params(),
        cost_estimate=pl.CostEstimate(
            flops=11 << 30, bytes_accessed=5 << 20, transcendentals=0
        ),
    )(placing, closing, rows, weight, vec)


def causal(second, transposed):
    i = sublanes(CHUNK, 2 * CHUNK)
    j = lanes(CHUNK, 2 * CHUNK) % CHUNK
    if transposed:
        i, j = j, i
    crosses = (i >= STRETCH) & (j < STRETCH)
    return jnp.where(crosses, 1.0 - second, jnp.where(j <= i, 1.0, 0.0))


def start_all(when, copies):
    @pl.when(when)
    def _():
        for copy in copies:
            copy.start()


def mid_kernel(
    placing,
    restart,
    opened,
    owner,
    _,
    rows_ref,
    cot_ref,
    inc_ref,
    w_qkv,
    vec,
    w_out_far,
    w_up_far,
    w_down_far,
    *refs,
    first,
    resumes,
    final,
):
    gain_one, shift_one, b_qkv = vector(vec, GAIN_ONE), vector(vec, SHIFT_ONE), vector(vec, BIAS_QKV)
    gain, shift = vector(vec, GAIN_TWO), vector(vec, SHIFT_TWO)
    b_out, b_up, b_down = vector(vec, BIAS_OUT), vector(vec, BIAS_UP), vector(vec, BIAS_DOWN)
    before, refs = (refs[:3], refs[3:]) if resumes else ((), refs)
    result, qkv_ref, branch_out, gn_out, gd_out, states_out, state_out, vec_out = refs[:8]
    refs = refs[8:]
    if final:
        keep_out, send_out, turned, acc_up, acc_down, acc_out = refs[:6]
        refs = refs[6:]
    else:
        far_up, far_down, far_out, acc_up, acc_down, acc_out = refs[:6]
        refs = refs[6:]
    carry, back, back_sum, att_scr, inv_scr, att_b, x_scr, cot_scr, w_out, w_up, w_down, sems = refs
    member, step = pl.program_id(0), pl.program_id(1)
    micro = first + member
    per = TILE // STRETCH
    opening = (member == 0) & (step == 0)
    closing = (member == pl.num_programs(0) - 1) & (step == pl.num_programs(1) - 1)
    arriving = [
        pltpu.make_async_copy(source, target, sems.at[n])
        for n, (source, target) in enumerate(
            [(w_out_far, w_out), (w_up_far, w_up), (w_down_far, w_down)]
            + list(zip(before, (acc_up, acc_down, acc_out)))
        )
    ]
    leaving = []

    @pl.when(opening)
    def _():
        vec_out[...] = jnp.zeros_like(vec_out)
        for copy in arriving:
            copy.start()
        if not resumes:
            acc_up[...] = jnp.zeros_like(acc_up)
            acc_down[...] = jnp.zeros_like(acc_down)
            acc_out[...] = jnp.zeros_like(acc_out)

    @pl.when(step == 0)
    def _():
        for pair in range(PAIRS):
            carry[pair] = unpack_state(inc_ref[0], pair)
        back[...] = jnp.zeros_like(back)
        back_sum[...] = jnp.zeros_like(back_sum)

    block = same_head()
    ones_head = jnp.where(block, 1.0, 0.0).astype(bf16)
    ones_twice = jnp.concatenate([ones_head, ones_head], axis=0)
    low = first_head(CHUNK)
    one_low = jnp.where(low, 1.0, 0.0).astype(bf16)
    one_high = jnp.where(low, 0.0, 1.0).astype(bf16)
    ones_both = jnp.concatenate([one_low, one_high], axis=0)
    ones_all = jnp.ones((CHUNK, PAIR), bf16)
    wide_block = jnp.concatenate([block, block], axis=1)
    upper = sublanes(CHUNK, PAIR) < STRETCH
    inner = lanes(PAIR, PAIR) % HEAD_DIM
    zero_s = jnp.zeros((PAIR, PAIR), bf16)
    for i in range(per):
        x_scr[i * STRETCH : (i + 1) * STRETCH, :] = pick(rows_ref, placing[micro, step * per + i])
        cot_scr[i * STRETCH : (i + 1) * STRETCH, :] = pick(cot_ref, placing[micro, step * per + i])

    x = x_scr[...].astype(f32)
    n, _ = standardize(x)
    normed = (n * gain_one + shift_one).astype(bf16)
    for part in range(2):
        at = slice(part * MODEL, (part + 1) * MODEL)
        qkv_ref[:, at] = featured(nn(normed, w_qkv[:, at]) + b_qkv[:, at])
    at = slice(2 * MODEL, 3 * MODEL)
    qkv_ref[:, at] = (nn(normed, w_qkv[:, at]) + b_qkv[:, at]).astype(bf16)

    for chunk in range(TILE // CHUNK):
        rows = slice(chunk * CHUNK, (chunk + 1) * CHUNK)
        r0 = flag(restart[micro, step * per + 2 * chunk])
        r1 = flag(restart[micro, step * per + 2 * chunk + 1])
        mask = causal(r1, False)
        keep_low = jnp.where(upper, 1.0, 1.0 - r1)
        keep_key = jnp.where(upper, 1.0 - r1, 1.0)
        for pair in range(PAIRS):
            q = qkv_ref[rows, pair * PAIR : (pair + 1) * PAIR]
            k = qkv_ref[rows, MODEL + pair * PAIR : MODEL + (pair + 1) * PAIR]
            v = qkv_ref[rows, 2 * MODEL + pair * PAIR : 2 * MODEL + (pair + 1) * PAIR]
            state = carry[pair] * (1.0 - r0)
            state_b = state.astype(bf16)
            state_low = (state - state_b.astype(f32)).astype(bf16)
            states_out[chunk, pair * PAIR : (pair + 1) * PAIR, :] = jnp.concatenate(
                [
                    state_b[:, :PAIR],
                    jnp.where(
                        inner < 2, state_b[:, PAIR:], jnp.where(inner == 2, state_low[:, PAIR:], zero_s)
                    ),
                    state_low[:, :PAIR],
                ],
                axis=1,
            )
            mixing = nt(q, by_head(k, CHUNK)) * mask
            values = jnp.concatenate([by_head(v, CHUNK), ones_both], axis=1)
            out = nn(mixing.astype(bf16), values)
            out = out + nn((q.astype(f32) * keep_low).astype(bf16), state_b)
            inv = 1.0 / out[:, PAIR:]
            att = out[:, :PAIR] * inv
            att_scr[rows, col(pair)] = att
            inv_scr[rows, col(pair)] = inv
            att_b[rows, col(pair)] = att.astype(bf16)
            k_keep = (k.astype(f32) * keep_key).astype(bf16)
            added = tn(k_keep, jnp.concatenate([v, ones_all], axis=1))
            carry[pair] = state * (1.0 - r1) + jnp.where(wide_block, added, 0.0)

    @pl.when(opening)
    def _():
        for copy in arriving:
            copy.wait()

    middle = x_scr[...].astype(f32) + nn(att_b[...], w_out[...]) + b_out
    n, scale = standardize(middle)
    normed = (n * gain + shift).astype(bf16)
    normed_t = normed.T
    cot = cot_scr[...]
    cot_t = cot.T
    ff = w_up.shape[1]
    total = middle + b_down
    up_grad = jnp.zeros((TILE, MODEL), f32)
    for part in range(ff // MODEL):
        at = slice(part * MODEL, (part + 1) * MODEL)
        u = nn(normed, w_up[:, at]) + b_up[:, at]
        u2 = u * u
        t = jnp.tanh(u * (0.7978845608028654 + 0.035677408136300125 * u2))
        half = 0.5 + 0.5 * t
        act = (u * half).astype(bf16)
        rise = 1.5957691216057308 + 0.21406444881780074 * u2
        slope = half + u * half * (1.0 - half) * rise
        g = (nt(cot, w_down[at, :]) * slope).astype(bf16)
        total = total + nn(act, w_down[at, :])
        acc_down[:, at] += nn(cot_t, act)
        vec_out[0:1, at] += jnp.sum(g.astype(f32), axis=0, keepdims=True)
        up_grad = up_grad + nt(g, w_up[:, at])
        acc_up[:, at] += nn(normed_t, g)
        if not final:
            leaving.append(pltpu.make_async_copy(acc_down.at[:, at], far_down.at[:, at], sems.at[6 + 2 * part]))
            leaving.append(pltpu.make_async_copy(acc_up.at[:, at], far_up.at[:, at], sems.at[7 + 2 * part]))
            start_all(closing, leaving[-2:])
    total = total.astype(bf16)
    for i in range(per):
        put(result, placing[micro, step * per + i], total[i * STRETCH : (i + 1) * STRETCH, :])

    cot_f = cot.astype(f32)
    vec_out[1:2, :MODEL] += jnp.sum(up_grad * n, axis=0, keepdims=True)
    vec_out[1:2, MODEL : 2 * MODEL] += jnp.sum(up_grad, axis=0, keepdims=True)
    vec_out[1:2, 3 * MODEL : 4 * MODEL] += jnp.sum(cot_f, axis=0, keepdims=True)
    branch = (cot_f + norm_back(up_grad, gain, n, scale)).astype(bf16)
    branch_out[...] = branch
    vec_out[1:2, 2 * MODEL : 3 * MODEL] += jnp.sum(branch.astype(f32), axis=0, keepdims=True)
    grad_att = nt(branch, w_out[...])
    acc_out[...] += tn(att_b[...], branch)
    if not final:
        leaving.append(pltpu.make_async_copy(acc_out, far_out, sems.at[6 + 2 * (ff // MODEL)]))
        start_all(closing, leaving[-1:])
    lane = lanes(CHUNK, PAIR) % HEAD_DIM
    for chunk in range(TILE // CHUNK):
        rows = slice(chunk * CHUNK, (chunk + 1) * CHUNK)
        o0 = flag(opened[micro, step * per + 2 * chunk])
        o1 = flag(opened[micro, step * per + 2 * chunk + 1])
        keep = jnp.where(upper, o0, o1)
        for pair in range(PAIRS):
            inv = inv_scr[rows, col(pair)]
            gn = (grad_att[rows, col(pair)].astype(bf16).astype(f32) * inv).astype(bf16)
            product = gn.astype(f32) * att_scr[rows, col(pair)]
            high = product.astype(bf16)
            low_part = (product - high.astype(f32)).astype(bf16)
            gd = -nn(jnp.concatenate([high, low_part], axis=1), ones_twice)
            gd_high = gd.astype(bf16)
            gd_low = (gd - gd_high.astype(f32)).astype(bf16)
            zero = jnp.zeros_like(gd_high)
            gn_out[rows, col(pair)] = gn
            gd_out[rows, col(pair)] = jnp.where(
                (lane == 0) | (lane == 2), gd_high, jnp.where(lane == 1, gd_low, zero)
            )
            q = qkv_ref[rows, pair * PAIR : (pair + 1) * PAIR].astype(f32) * keep
            back[pair] += tn(q.astype(bf16), gn)
            back_sum[:, col(pair)] += jnp.sum(q * gd, axis=0, keepdims=True)

    @pl.when(step == pl.num_programs(1) - 1)
    def _():
        for pair in range(PAIRS):
            pack_state(state_out, pair, back[pair], back_sum[:, col(pair)])

    if not final:

        @pl.when(closing)
        def _():
            for copy in leaving:
                copy.wait()

    else:

        @pl.when(closing)
        def _():
            parts = ff // MODEL
            devices = 2 * keep_out.shape[0]
            less = MODEL // devices
            more = parts * less
            for part in range(parts):
                at = slice(part * MODEL, (part + 1) * MODEL)
                turned[at, :] = acc_down[:, at].T
            for j in range(devices):
                d = owner[j]
                target = keep_out if j < devices // 2 else send_out
                seat = j % (devices // 2)
                here = pl.ds(pl.multiple_of(d * less, less), less)
                for part in range(parts):
                    target[seat, part * less : (part + 1) * less, :] = acc_up[
                        here, part * MODEL : (part + 1) * MODEL
                    ].astype(target.dtype)
                there = pl.ds(pl.multiple_of(d * more, more), more)
                target[seat, more : 2 * more, :] = turned[there, :].astype(target.dtype)
                target[seat, 2 * more :, :] = acc_out[here, :].astype(target.dtype)


def run_mid(tables, first, members, target, rows, cot, inc, weights, vec, before, owner):
    micro, count = tables[0].shape
    width = rows.shape[-1]
    ff = weights[2].shape[1]
    count = count * STRETCH
    tiles = count // TILE
    total = members * count
    resumes, final = before is not None, owner is not None
    f32_sums = [(width, ff), (width, ff), (MODEL, width)]
    out_specs = [
        group_spec(target.shape, 0),
        tile_spec(3 * MODEL, tiles),
        tile_spec(width, tiles),
        tile_spec(MODEL, tiles),
        tile_spec(MODEL, tiles),
        states_spec(tiles),
        member_spec(),
        fixed((8, ff)),
    ]
    out_shape = [
        jax.ShapeDtypeStruct(target.shape, bf16),
        jax.ShapeDtypeStruct((total, 3 * MODEL), bf16),
        jax.ShapeDtypeStruct((total, width), bf16),
        jax.ShapeDtypeStruct((total, MODEL), bf16),
        jax.ShapeDtypeStruct((total, MODEL), bf16),
        jax.ShapeDtypeStruct((total // CHUNK, MODEL, 3 * PAIR), bf16),
        jax.ShapeDtypeStruct((members, HEAD_DIM + 8, MODEL), f32),
        jax.ShapeDtypeStruct((8, ff), f32),
    ]
    if final:
        devices = owner.shape[0]
        half = (devices // 2, (2 * ff + MODEL) // devices, MODEL)
        out_specs += [fixed(half), fixed(half)]
        out_shape += [jax.ShapeDtypeStruct(half, bf16)] * 2
    else:
        out_specs += [ANYWHERE] * 3
        out_shape += [jax.ShapeDtypeStruct(shape, f32) for shape in f32_sums]
    if not final:
        owner = jnp.zeros((8,), jnp.int32)
    scratch = [pltpu.VMEM((ff, width), f32)] if final else []
    scratch += [pltpu.VMEM(shape, f32) for shape in f32_sums]
    scratch += [
        pltpu.VMEM((PAIRS, PAIR, 2 * PAIR), f32),
        pltpu.VMEM((PAIRS, PAIR, PAIR), f32),
        pltpu.VMEM((1, MODEL), f32),
        pltpu.VMEM((TILE, MODEL), f32),
        pltpu.VMEM((TILE, MODEL), f32),
        pltpu.VMEM((TILE, MODEL), bf16),
        pltpu.VMEM((TILE, width), bf16),
        pltpu.VMEM((TILE, width), bf16),
    ]
    scratch += [pltpu.VMEM(item.shape, bf16) for item in weights[1:]]
    scratch.append(pltpu.SemaphoreType.DMA((7 + 2 * (ff // MODEL),)))
    return pl.pallas_call(
        functools.partial(mid_kernel, first=first, resumes=resumes, final=final),
        name="middle",
        grid_spec=pltpu.PrefetchScalarGridSpec(
            num_scalar_prefetch=4,
            grid=(members, tiles),
            in_specs=[
                ANYWHERE,
                group_spec(rows.shape, first),
                group_spec(cot[0].shape, cot[1]),
                member_spec(first),
            ]
            + [fixed(weights[0].shape), fixed(vec.shape)]
            + [ANYWHERE] * (6 if resumes else 3),
            out_specs=out_specs,
            scratch_shapes=scratch,
        ),
        out_shape=out_shape,
        compiler_params=params(),
        input_output_aliases={4: 0},
        cost_estimate=pl.CostEstimate(
            flops=members * (24 << 30), bytes_accessed=members << 24, transcendentals=0
        ),
    )(*tables[:3], owner, target, rows, cot[0], inc, weights[0], vec, *weights[1:], *(before or ()))


def back_kernel(
    placing,
    restart,
    reach,
    owner,
    _,
    rows_ref,
    qkv_ref,
    gn_ref,
    gd_ref,
    branch_ref,
    states_ref,
    weight,
    vec,
    owner_col,
    *refs,
    first,
    resumes,
    final,
    widths,
    sums,
    hops,
):
    incs, refs = refs[:hops], refs[hops:]
    gain, shift = vector(vec, GAIN_ONE), vector(vec, SHIFT_ONE)
    before, refs = (refs[:1], refs[1:]) if resumes else ((), refs)
    vec_others, refs = refs[:sums], refs[sums:]
    grad_rows, vec_out = refs[:2]
    refs = refs[2:]
    if final:
        keep_out, send_out, acc = refs[:3]
        refs = refs[3:]
    else:
        acc = refs[0]
        refs = refs[1:]
    carry, x_scr, mixed_scr = refs[:3]
    sems = refs[3] if resumes else None
    member, step = pl.program_id(0), pl.program_id(1)
    micro = first + member
    per = TILE // STRETCH
    tile = pl.num_programs(1) - 1 - step
    opening = (member == 0) & (step == 0)
    lane = lanes(CHUNK, PAIR)
    inner = lane % HEAD_DIM

    @pl.when(opening)
    def _():
        vec_out[...] = jnp.zeros_like(vec_out)
        if resumes:
            pltpu.make_async_copy(before[0], acc, sems.at[0]).start()
        else:
            acc[...] = jnp.zeros_like(acc)

    @pl.when(step == 0)
    def _():
        only = jnp.concatenate([jnp.ones((PAIR, PAIR), f32), jnp.where(inner == 0, 1.0, 0.0)], axis=1)
        inc = jnp.zeros((HEAD_DIM + 8, MODEL), f32)
        for hop, ref in enumerate(incs):
            inc = inc + ref[0] * reach[micro, hop]
        for pair in range(PAIRS):
            carry[pair] = unpack_state(inc, pair) * only

    block = same_head()
    wide_block = jnp.concatenate([block, block], axis=1)
    upper = sublanes(CHUNK, PAIR) < STRETCH
    marks = jnp.where((inner < 2) | (inner == 3), 1.0, 0.0).astype(bf16)
    mark_low = jnp.where(lane < 2, 1.0, 0.0).astype(bf16)
    mark_high = jnp.where((lane == HEAD_DIM) | (lane == HEAD_DIM + 1), 1.0, 0.0).astype(bf16)
    marks_both = jnp.concatenate([mark_low, mark_high], axis=0)
    for i in range(per):
        x_scr[i * STRETCH : (i + 1) * STRETCH, :] = pick(rows_ref, placing[micro, tile * per + i])

    for chunk in reversed(range(TILE // CHUNK)):
        rows = slice(chunk * CHUNK, (chunk + 1) * CHUNK)
        r0 = flag(restart[micro, tile * per + 2 * chunk])
        r1 = flag(restart[micro, tile * per + 2 * chunk + 1])
        r2 = flag(restart[micro, tile * per + 2 * chunk + 2])
        mask = causal(r1, False)
        mask_t = causal(r1, True)
        keep_low = jnp.where(upper, 1.0, 1.0 - r1)
        keep_key = jnp.where(upper, 1.0 - r1, 1.0)
        for pair in range(PAIRS):
            q = qkv_ref[rows, pair * PAIR : (pair + 1) * PAIR]
            k = qkv_ref[rows, MODEL + pair * PAIR : MODEL + (pair + 1) * PAIR]
            v = qkv_ref[rows, 2 * MODEL + pair * PAIR : 2 * MODEL + (pair + 1) * PAIR]
            gn = gn_ref[rows, col(pair)]
            gdx = gd_ref[rows, col(pair)]
            state = states_ref[chunk, pair * PAIR : (pair + 1) * PAIR, :]
            grown = carry[pair] * (1.0 - r2)
            grown_b = grown.astype(bf16)
            rest = grown - grown_b.astype(f32)
            grown_low = rest[:, :PAIR].astype(bf16)
            z_low = pltpu.roll(rest[:, PAIR:], 3, 1).astype(bf16)
            z_both = jnp.where(inner < 2, grown_b[:, PAIR:], jnp.where(inner == 3, z_low, jnp.zeros_like(z_low)))
            grown_x = jnp.concatenate([grown_b[:, :PAIR], z_both], axis=1)
            k2 = by_head(k, CHUNK)
            q2 = by_head(q, CHUNK)
            v2 = by_head(v, CHUNK)
            gn2 = by_head(gn, CHUNK)
            gd2 = by_head(gdx, CHUNK)
            both = jnp.concatenate([gn, gdx], axis=1)
            mixing_t = (nt(k, q2) * mask_t).astype(bf16)
            g_mix = (nt(both, jnp.concatenate([v2, marks_both], axis=1)) * mask).astype(bf16)
            v_marks = jnp.concatenate([v, marks], axis=1)
            g_mix_t = (nt(v_marks, jnp.concatenate([gn2, gd2], axis=1)) * mask_t).astype(bf16)
            dq = nn(g_mix, k2) + (nt(both, state[:, : 2 * PAIR]) + nt(gn, state[:, 2 * PAIR :])) * keep_low
            dk = nn(g_mix_t, q2) + (nt(v_marks, grown_x) + nt(v, grown_low)) * keep_key
            dv = nn(mixing_t, gn2) + nn(k, grown_b[:, :PAIR]) * keep_key
            q_keep = (q.astype(f32) * keep_low).astype(bf16)
            added = tn(q_keep, both)
            carry[pair] = (grown * (1.0 - r1) + jnp.where(wide_block, added, 0.0)) * (1.0 - r0)
            mixed_scr[rows, pair * PAIR : (pair + 1) * PAIR] = (
                dq * jnp.minimum(q.astype(f32), 1.0)
            ).astype(bf16)
            mixed_scr[rows, MODEL + pair * PAIR : MODEL + (pair + 1) * PAIR] = (
                dk * jnp.minimum(k.astype(f32), 1.0)
            ).astype(bf16)
            mixed_scr[rows, 2 * MODEL + pair * PAIR : 2 * MODEL + (pair + 1) * PAIR] = dv.astype(bf16)

    mixed = mixed_scr[...]
    vec_out[0:1, :] += jnp.sum(mixed.astype(f32), axis=0, keepdims=True)
    upstream = nt(mixed, weight[...])
    n, scale = standardize(x_scr[...].astype(f32))
    normed_t = (n * gain + shift).astype(bf16).T
    if resumes:

        @pl.when(opening)
        def _():
            pltpu.make_async_copy(before[0], acc, sems.at[0]).wait()

    for part in range(3):
        at = slice(part * MODEL, (part + 1) * MODEL)
        acc[:, at] += nn(normed_t, mixed[:, at])
    vec_out[1:2, :MODEL] += jnp.sum(upstream * n, axis=0, keepdims=True)
    vec_out[1:2, MODEL : 2 * MODEL] += jnp.sum(upstream, axis=0, keepdims=True)
    total = (branch_ref[...].astype(f32) + norm_back(upstream, gain, n, scale)).astype(bf16)
    for i in range(per):
        put(grad_rows, placing[micro, tile * per + i], total[i * STRETCH : (i + 1) * STRETCH, :])

    if final:

        @pl.when((member == pl.num_programs(0) - 1) & (step == pl.num_programs(1) - 1))
        def _():
            half = keep_out.shape[0]
            devices = 2 * half
            less = MODEL // devices
            for j in range(devices):
                here = pl.ds(pl.multiple_of(owner[j] * less, less), less)
                target = keep_out if j < half else send_out
                for part in range(3):
                    target[j % half, part * less : (part + 1) * less, :] = acc[
                        here, part * MODEL : (part + 1) * MODEL
                    ].astype(target.dtype)
            mid = sum(ref[...] for ref in vec_others if ref.shape[1] == vec_others[0].shape[1])
            rear = vec_out[...] + sum(
                ref[...] for ref in vec_others if ref.shape[1] != vec_others[0].shape[1]
            )
            sources = (
                rear[1:2, :MODEL],
                rear[1:2, MODEL : 2 * MODEL],
                rear[0:1, : 2 * MODEL],
                rear[0:1, 2 * MODEL :],
                mid[1:2, 2 * MODEL : 3 * MODEL],
                mid[1:2, :MODEL],
                mid[1:2, MODEL : 2 * MODEL],
                mid[0:1, :],
                mid[1:2, 3 * MODEL : 4 * MODEL],
            )
            rows16 = sublanes(16, MODEL)
            pieces = []
            for source, width in zip(sources, widths, strict=True):
                size = devices * width
                mine = (lanes(devices, size) // width) == owner_col[...]
                picked = jnp.where(mine, source, 0.0)
                gather = jnp.where(
                    (sublanes(size, PAIR) % width) == lanes(size, PAIR), 1.0, 0.0
                ).astype(bf16)
                high = picked.astype(bf16)
                low = (picked - high.astype(f32)).astype(bf16)
                pieces.append(nn(high, gather) + nn(low, gather))
            rest = jnp.zeros((1, MODEL - PAIR), f32)
            for j in range(devices):
                block16 = jnp.zeros((16, MODEL), f32)
                for v, piece in enumerate(pieces):
                    row = jnp.concatenate([piece[j : j + 1, :], rest], axis=1)
                    block16 = block16 + jnp.where(rows16 == v, row, 0.0)
                target = keep_out if j < half else send_out
                target[j % half, 3 * less :, :] = block16.astype(target.dtype)


def run_back(tables, first, members, target, rows, mid, incs, weight, vec, before, owner, others, widths):
    (group, seat), (saved, at) = target, mid
    micro, count = tables[0].shape
    width = rows.shape[-1]
    count = count * STRETCH
    tiles = count // TILE
    resumes, final = before is not None, owner is not None
    devices = lax.axis_size(BOTH) if final else 0
    if not final:
        owner = jnp.zeros((8,), jnp.int32)
        others = []
    half = (devices // 2, 3 * MODEL // max(devices, 1) + 16, MODEL)
    out_specs = [group_spec(group.shape, seat), fixed((8, 3 * MODEL))]
    out_shape = [
        jax.ShapeDtypeStruct(group.shape, bf16),
        jax.ShapeDtypeStruct((8, 3 * MODEL), f32),
    ]
    scratch = []
    if final:
        out_specs += [fixed(half), fixed(half)]
        out_shape += [jax.ShapeDtypeStruct(half, bf16)] * 2
        scratch.append(pltpu.VMEM((width, 3 * MODEL), f32))
    else:
        out_specs.append(fixed((width, 3 * MODEL)))
        out_shape.append(jax.ShapeDtypeStruct((width, 3 * MODEL), f32))
    scratch += [
        pltpu.VMEM((PAIRS, PAIR, 2 * PAIR), f32),
        pltpu.VMEM((TILE, width), bf16),
        pltpu.VMEM((TILE, 3 * MODEL), bf16),
    ]
    if resumes:
        scratch.append(pltpu.SemaphoreType.DMA((1,)))

    def tile(width_):
        return pl.BlockSpec((TILE, width_), lambda i, t, *_: ((at + i) * tiles + tiles - 1 - t, 0))

    return pl.pallas_call(
        functools.partial(
            back_kernel,
            first=first,
            resumes=resumes,
            final=final,
            widths=widths,
            sums=len(others),
            hops=len(incs),
        ),
        name="back",
        grid_spec=pltpu.PrefetchScalarGridSpec(
            num_scalar_prefetch=4,
            grid=(members, tiles),
            in_specs=[
                ANYWHERE,
                group_spec(rows.shape, first),
                tile(3 * MODEL),
                tile(MODEL),
                tile(MODEL),
                tile(width),
                pl.BlockSpec(
                    (TILE // CHUNK, MODEL, 3 * PAIR),
                    lambda i, t, *_: ((at + i) * tiles + tiles - 1 - t, 0, 0),
                ),
                fixed(weight.shape),
                fixed(vec.shape),
                fixed((owner.shape[0], 1)),
            ]
            + [member_spec(at)] * len(incs)
            + ([ANYWHERE] if resumes else [])
            + [fixed(item.shape) for item in others],
            out_specs=out_specs,
            scratch_shapes=scratch,
        ),
        out_shape=out_shape,
        input_output_aliases={4: 0},
        compiler_params=params(),
        cost_estimate=pl.CostEstimate(
            flops=members * (15 << 30), bytes_accessed=members << 24, transcendentals=0
        ),
    )(
        tables[0],
        tables[1],
        tables[3],
        owner,
        group,
        rows,
        saved[1],
        saved[3],
        saved[4],
        saved[2],
        saved[5],
        weight,
        vec,
        owner[:, None],
        *incs,
        *(() if before is None else (before,)),
        *others,
    )


def send_kernel(slot, source, target, *, first):
    micro = first + pl.program_id(0)
    for i in range(source.shape[1]):
        put(target, slot[micro, i], source[0, i])


def run_send(slot, rows, first, members):
    micro, count, width = rows.shape
    stretches = count // STRETCH
    groups = lax.axis_size("dp")
    shape = (groups, members, stretches // groups, STRETCH, width)
    return pl.pallas_call(
        functools.partial(send_kernel, first=first),
        name="send",
        grid_spec=pltpu.PrefetchScalarGridSpec(
            num_scalar_prefetch=1,
            grid=(members,),
            in_specs=[
                pl.BlockSpec((1, stretches, STRETCH, width), lambda i, *_: (first + i, 0, 0, 0))
            ],
            out_specs=pl.BlockSpec((groups, 1) + shape[2:], lambda i, *_: (0, i, 0, 0, 0)),
        ),
        out_shape=jax.ShapeDtypeStruct(shape, rows.dtype),
        compiler_params=pltpu.CompilerParams(vmem_limit_bytes=VMEM_LIMIT),
        cost_estimate=pl.CostEstimate(
            flops=0, bytes_accessed=4 * members * count * width, transcendentals=0
        ),
    )(slot, rows.reshape(micro, stretches, STRETCH, width))


def land_kernel(slot, _, source, target, *, first):
    micro = first + pl.program_id(0)
    for i in range(target.shape[1]):
        target[0, i] = pick(source, slot[micro, i])


def run_land(slot, landed, output, first):
    members = landed.shape[1]
    shape = output.shape
    block = (landed.shape[0], 1) + landed.shape[2:]
    return pl.pallas_call(
        functools.partial(land_kernel, first=first),
        name="land",
        grid_spec=pltpu.PrefetchScalarGridSpec(
            num_scalar_prefetch=1,
            grid=(members,),
            in_specs=[
                pl.BlockSpec(memory_space=pl.ANY),
                pl.BlockSpec(block, lambda i, *_: (0, i, 0, 0, 0)),
            ],
            out_specs=pl.BlockSpec((1,) + shape[1:], lambda i, *_: (first + i, 0, 0, 0)),
        ),
        out_shape=jax.ShapeDtypeStruct(shape, output.dtype),
        input_output_aliases={1: 0},
        compiler_params=pltpu.CompilerParams(vmem_limit_bytes=VMEM_LIMIT),
        cost_estimate=pl.CostEstimate(flops=0, bytes_accessed=4 * landed.size, transcendentals=0),
    )(slot, output, landed)


def blank(shape):
    return pl.pallas_call(
        lambda ref: None,
        name="blank",
        out_specs=pl.BlockSpec(memory_space=pl.ANY),
        out_shape=jax.ShapeDtypeStruct(shape, bf16),
    )()


def index_tables(lengths, stretch_order, count):
    fsdp = lax.axis_size("fsdp")
    groups = lax.axis_size("dp")
    device = lax.axis_index(BOTH)
    base = device * count
    within = jnp.arange(count, dtype=jnp.int32)
    mine = base + within
    place = jnp.arange(stretch_order.shape[1], dtype=jnp.int32)
    here = place[None, None, :]
    landing = jnp.sum(
        jnp.where(stretch_order[:, None, :] == mine[None, :, None], here, 0), axis=-1
    )
    slot = jnp.sum((landing[:, None, :] < landing[:, :, None]).astype(jnp.int32), axis=-1)
    arrival = jnp.sum(
        jnp.where(here == mine[None, :, None], stretch_order[:, None, :], 0), axis=-1
    )
    source = arrival // count // fsdp
    ahead = (source[:, None, :] == source[:, :, None]) & (
        within[None, None, :] < within[None, :, None]
    )
    placing = source * (count // groups) + jnp.sum(ahead.astype(jnp.int32), axis=-1)
    index = jnp.arange(lengths.shape[1], dtype=jnp.int32)
    starts = jnp.sum(
        jnp.where(index[None, None, :] < index[None, :, None], lengths[:, None, :], 0), axis=-1
    )
    edge = base + jnp.arange(count + 1, dtype=jnp.int32)
    restart = jnp.any(starts[:, None, :] == edge[None, :, None], axis=-1).astype(jnp.int32)
    restart = jnp.where(edge[None, :] == stretch_order.shape[1], 1, restart)
    opened = 1 - jnp.any(
        (starts[:, None, :] >= base) & (starts[:, None, :] <= mine[None, :, None]), axis=-1
    ).astype(jnp.int32)
    last = base + count - 1
    closing = 1 - jnp.any(
        (starts[:, None, :] > mine[None, :, None]) & (starts[:, None, :] <= last), axis=-1
    ).astype(jnp.int32)
    hops = -(-(LONGEST - 1) // count)
    hop = jnp.arange(hops, dtype=jnp.int32)
    reach_back = base - 1 - hop * count
    from_before = 1.0 - jnp.any(
        (starts[:, None, :] > reach_back[None, :, None]) & (starts[:, None, :] <= base), axis=-1
    ).astype(f32)
    reach_on = base + (hop + 1) * count
    from_after = 1.0 - jnp.any(
        (starts[:, None, :] > last) & (starts[:, None, :] <= reach_on[None, :, None]), axis=-1
    ).astype(f32)
    first = base - hop * count
    unbroken = 1.0 - jnp.any(
        (starts[:, None, :] >= first[None, :, None]) & (starts[:, None, :] <= last), axis=-1
    ).astype(f32)
    return slot, placing, restart, opened, closing, from_before, from_after, unbroken


def exchange(states, hops, forward):
    size = lax.axis_size("fsdp")
    got = []
    for hop in range(min(hops, size - 1)):
        step = hop + 1
        pairs = [(i, i + step) if forward else (i + step, i) for i in range(size - step)]
        got.append(lax.ppermute(states, "fsdp", pairs))
    return got


def passed_on(states, weights, unbroken, beside):
    size = lax.axis_size("fsdp")
    total, own, step = jnp.zeros_like(states), states, 1
    while step <= weights.shape[1] and step < size:
        got = lax.ppermute(own, "fsdp", [(i, i + step) for i in range(size - step)])
        if step == 1:
            got = after(got, beside)
        total = total + got * weights[:, step - 1, None, None]
        own = own + got * unbroken[:, step - 1, None, None]
        step *= 2
    return total


def halving_stages():
    stages = []
    dp, fsdp = lax.axis_size("dp"), lax.axis_size("fsdp")
    if dp > 1:
        stages.append(("dp", 1))
    bit = 1
    while bit < fsdp:
        stages.append(("fsdp", bit))
        bit *= 2
    bit = 2
    while bit < dp:
        stages.append(("dp", bit))
        bit *= 2
    return stages


def order_tables():
    stages = halving_stages()
    fsdp = lax.axis_size("fsdp")
    devices = lax.axis_size(BOTH)
    me = lax.axis_index(BOTH)
    index = jnp.arange(devices, dtype=jnp.int32)
    bits = [bit * (fsdp if axis == "dp" else 1) for axis, bit in stages]
    place = jnp.zeros((devices,), jnp.int32)
    owner = jnp.zeros((devices,), jnp.int32)
    for s, bit in enumerate(bits):
        rank = len(bits) - 1 - s
        place = place + jnp.where(((index ^ me) & bit) != 0, 1 << rank, 0)
        owner = owner + jnp.where(((index >> rank) & 1) != 0, bit, 0)
    return place, owner ^ me


def after(x, *others):
    return lax.optimization_barrier((x, others))[0]


def swap(x, axis, bit):
    return lax.ppermute(x, axis, [(i, i ^ bit) for i in range(lax.axis_size(axis))])


def gather_halves(x, ties):
    stages = list(reversed(halving_stages()))
    steps = []
    for s, (axis, bit) in enumerate(stages[:-1]):
        if s in ties:
            x = after(x, ties[s])
        x = jnp.concatenate([x, swap(x, axis, bit)], axis=0)
        steps.append(x)
    return (x, swap(x, *stages[-1])), steps


def scatter_step(keep, send, s):
    stages = halving_stages()
    return scatter_join(keep, swap(send, *stages[s]), s == len(stages) - 1)


def scatter_join(keep, got, last):
    if last:
        return keep[0].astype(f32) + got[0].astype(f32), None
    half = keep.shape[0] // 2
    send = (keep[half:].astype(f32) + got[half:].astype(f32)).astype(bf16)
    return keep[:half].astype(f32) + got[:half].astype(f32), send


def finish_kernel(keep, got, qkv, *vectors):
    total = keep[0] + got[0].astype(f32)
    rows = qkv.shape[0]
    for part in range(3):
        qkv[:, part * MODEL : (part + 1) * MODEL] = total[part * rows : (part + 1) * rows, :]
    for v, ref in enumerate(vectors):
        ref[...] = total[3 * rows + v : 3 * rows + v + 1, : ref.shape[1]]


def run_finish(keep, got, widths):
    rows = (keep.shape[1] - 16) // 3
    return pl.pallas_call(
        finish_kernel,
        name="finish",
        out_shape=[jax.ShapeDtypeStruct((rows, 3 * MODEL), f32)]
        + [jax.ShapeDtypeStruct((1, width), f32) for width in widths],
    )(keep, got)


def pack_kernel(qkv, out, up, down, *refs):
    *small, first, second = refs
    rows = qkv.shape[0]
    for c in range(3):
        first[0, c * rows : (c + 1) * rows, :] = qkv[:, c * MODEL : (c + 1) * MODEL]
    row = sublanes(16, PAIR)
    side = jnp.zeros((16, PAIR), f32)
    for v, item in enumerate(small):
        width = item.shape[1]
        spread = jnp.where(sublanes(width, PAIR) == lanes(width, PAIR), 1.0, 0.0).astype(bf16)
        tall = jnp.broadcast_to(item[...].astype(f32), (16, width)).astype(bf16)
        side = side + jnp.where(row == v, nn(tall, spread), 0.0)
    side = jnp.concatenate([side, jnp.zeros((16, MODEL - PAIR), f32)], axis=1)
    first[0, 3 * rows : 3 * rows + 16, :] = side.astype(bf16)
    parts = up.shape[1] // MODEL
    for c in range(parts):
        second[0, c * rows : (c + 1) * rows, :] = up[:, c * MODEL : (c + 1) * MODEL]
    second[0, parts * rows : 2 * parts * rows, :] = down[...]
    second[0, 2 * parts * rows :, :] = out[...]


def run_pack(qkv, out, up, down, small):
    rows = qkv.shape[0]
    parts = up.shape[1] // MODEL
    return pl.pallas_call(
        pack_kernel,
        name="pack",
        out_shape=[
            jax.ShapeDtypeStruct((1, 3 * rows + 16, MODEL), bf16),
            jax.ShapeDtypeStruct((1, (2 * parts + 1) * rows, MODEL), bf16),
        ],
    )(qkv, out, up, down, *(item[None] for item in small))


def sort_first_kernel(place, own, got, owner, qkv, vectors, *, widths):
    half, total, _ = own.shape
    rows = total // 4

    def part(d):
        p = place[d]
        q = lax.rem(p, half)
        return jnp.where(p < half, own[q, : 3 * rows, :], got[q, : 3 * rows, :])

    for d in range(2 * half):
        block = part(d)
        for c in range(3):
            qkv[d * rows : (d + 1) * rows, c * MODEL : (c + 1) * MODEL] = block[
                c * rows : (c + 1) * rows, :
            ]
    small = jnp.concatenate(
        [own[:, 3 * rows :, :PAIR].astype(f32), got[:, 3 * rows :, :PAIR].astype(f32)], axis=0
    )
    row = lax.broadcasted_iota(jnp.int32, small.shape, 1)
    vectors[...] = jnp.zeros_like(vectors)
    for v, width in enumerate(widths):
        values = jnp.sum(jnp.where(row == v, small, 0.0), axis=1)
        size = 2 * half * width
        lane = lanes(PAIR, size) % width
        spread = jnp.where(lane == sublanes(PAIR, size), 1.0, 0.0).astype(bf16)
        wide = nn(values.astype(bf16), spread)
        mine = (lanes(2 * half, size) // width) == owner[...]
        vectors[v : v + 1, :size] = jnp.sum(jnp.where(mine, wide, 0.0), axis=0, keepdims=True)


def run_sort_first(place, owner, own, got, widths):
    devices = place.shape[0]
    rows = own.shape[1] // 4
    vmem = pl.BlockSpec(memory_space=pltpu.VMEM)
    return pl.pallas_call(
        functools.partial(sort_first_kernel, widths=widths),
        name="sort_first",
        in_specs=[pl.BlockSpec(memory_space=pltpu.SMEM), vmem, vmem, vmem],
        out_specs=[vmem, vmem],
        out_shape=[
            jax.ShapeDtypeStruct((devices * rows, 3 * MODEL), bf16),
            jax.ShapeDtypeStruct((8, devices * max(widths)), f32),
        ],
        compiler_params=pltpu.CompilerParams(vmem_limit_bytes=VMEM_LIMIT),
    )(place, own, got, owner[:, None])


def sort_second_kernel(gathered, up, down, out):
    devices, total, _ = gathered.shape
    parts = up.shape[1] // MODEL
    rows = total // (2 * parts + 1)
    tall = parts * rows
    for d in range(devices):
        for c in range(parts):
            up[d * rows : (d + 1) * rows, c * MODEL : (c + 1) * MODEL] = gathered[
                d, c * rows : (c + 1) * rows, :
            ]
        down[d * tall : (d + 1) * tall, :] = gathered[d, tall : 2 * tall, :]
        out[d * rows : (d + 1) * rows, :] = gathered[d, 2 * tall :, :]


def run_sort_second(gathered, ff):
    devices = gathered.shape[0]
    rows = gathered.shape[1] // (2 * (ff // MODEL) + 1)
    vmem = pl.BlockSpec(memory_space=pltpu.VMEM)
    return pl.pallas_call(
        sort_second_kernel,
        name="sort_second",
        in_specs=[vmem],
        out_specs=[vmem, vmem, vmem],
        out_shape=[
            jax.ShapeDtypeStruct((devices * rows, ff), bf16),
            jax.ShapeDtypeStruct((ff, MODEL), bf16),
            jax.ShapeDtypeStruct((devices * rows, MODEL), bf16),
        ],
        compiler_params=pltpu.CompilerParams(vmem_limit_bytes=VMEM_LIMIT),
    )(gathered)


def gather_all(x):
    return lax.all_gather(x, BOTH, axis=0, tiled=True)


def scatter_all(x):
    return lax.psum_scatter(x, BOTH, scatter_dimension=0, tiled=True)


def to_dp(group):
    return lax.all_to_all(group, "dp", split_axis=0, concat_axis=0, tiled=True)


def groups_of(micro):
    return [(0, micro - 1), (micro - 1, 1)] if micro > 1 else [(0, 1)]


def find(groups, m):
    for g, (first, members) in enumerate(groups):
        if first <= m < first + members:
            return g, m - first


def body(
    tokens,
    cotangent,
    lengths,
    stretch_order,
    ln1_gain,
    ln1_bias,
    w_qkv,
    b_qkv,
    w_out,
    b_out,
    ln2_gain,
    ln2_bias,
    w_up,
    b_up,
    w_down,
    b_down,
):
    micro, rows, width = tokens.shape
    count = rows // STRETCH
    devices = lax.axis_size(BOTH)
    ff = w_up.shape[1]
    dp = lax.axis_size("dp")
    slot, placing, restart, opened, closing, from_before, from_after, unbroken = index_tables(
        lengths, stretch_order, count
    )
    tables = (placing, restart, opened, from_after)
    small = (ln1_gain, ln1_bias, b_qkv, b_out, ln2_gain, ln2_bias, b_up, b_down)
    in_parts = (width // devices) % 16 == 0
    groups = groups_of(micro)
    sent = run_send(slot, tokens, 0, micro)
    if in_parts:
        place, owner = order_tables()
        first_part, second_part = run_pack(w_qkv, w_out, w_up, w_down, small)
        halves, steps = gather_halves(first_part, {1: sent, 2: tables + (closing, from_before, unbroken)})
        moved = to_dp(after(sent, steps[0]))
        qkv_all, vectors = run_sort_first(
            place, owner, *halves, [item.shape[0] for item in small]
        )
        ready = (qkv_all,)
        second_part = gather_all(second_part)
    else:
        owner, ready = None, ()
        moved = to_dp(sent)
        qkv_all, out_all = gather_all(w_qkv), gather_all(w_out)
        up_all, down_all = gather_all(w_up), gather_all(w_down)
        vectors = [gather_all(item).astype(f32) for item in small]
        vectors = jnp.stack([jnp.pad(item, (0, ff - item.shape[0])) for item in vectors])

    sent_grads = run_send(slot, after(cotangent, *ready), 0, micro)
    hops = from_before.shape[1]
    states = run_state(placing, closing, moved, qkv_all, vectors)
    cots = to_dp(sent_grads)
    if in_parts:
        up_all, down_all, out_all = run_sort_second(after(second_part, states), ff)
    incoming = passed_on(states, from_before, unbroken, out_all)
    weights = [qkv_all, out_all, up_all, down_all]
    mids, sums = [], None
    for g, (first, members) in enumerate(groups):
        target = blank((dp, members, count // dp, STRETCH, width))
        out = run_mid(
            tables,
            first,
            members,
            target,
            moved,
            (cots, first),
            incoming,
            weights,
            vectors,
            sums,
            owner if g == len(groups) - 1 else None,
        )
        sums = out[8:]
        mids.append(out)
    outgoing = [exchange(out[6], hops, False) for out in mids]
    homes = [to_dp(out[0]) for out in mids]
    sizes = [MODEL, MODEL, 2 * MODEL, MODEL, MODEL, MODEL, MODEL, ff, MODEL]
    widths = [size // devices for size in sizes]
    last = len(halving_stages()) - 1
    late = len(groups) - 1
    outgoing[0] = after(outgoing[0], *([mids[-1][7]] if late else []))
    if in_parts:
        keep, send = sums
        if late:
            send = after(send, outgoing[0], homes[0])
        keep, send = scatter_step(keep, send, 0)
        done = 0
    vec_mid = [f[7] for f in mids]
    vec_back, total = [], None
    grad_rows = []
    for g, (first, members) in enumerate(groups):
        if g:
            outgoing[g] = after(outgoing[g], vec_back[0], homes[g])
            grad_rows[0] = after(grad_rows[0], outgoing[g])
        saved = list(mids[g])
        if in_parts:
            saved[2], keep, send = lax.optimization_barrier((saved[2], keep, send))
            got = swap(send, *halving_stages()[done + 1])
        out = run_back(
            tables,
            first,
            members,
            (blank((dp, members, count // dp, STRETCH, width)), 0),
            moved,
            (saved, 0),
            outgoing[g],
            qkv_all,
            vectors,
            total,
            owner if g == late else None,
            vec_mid + vec_back,
            widths,
        )
        grad_rows.append(out[0])
        vec_back.append(out[1])
        total = out[2]
        if in_parts:
            done += 1
            keep, send = scatter_join(keep, after(got, out[1]), done == last)
            if g == late:
                grad_rows[g] = after(grad_rows[g], keep)
    narrow = out[2:]
    grad_homes = [to_dp(group) for group in grad_rows]
    result = blank((micro, count, STRETCH, width))
    input_grad = blank((micro, count, STRETCH, width))

    def land(output, pieces, *others):
        for (first, _), home in zip(groups, pieces, strict=True):
            output = run_land(slot, after(home, *others), output, first)
        return output

    if in_parts:
        part = width // devices
        narrow_keep, narrow_send = narrow
        if len(groups) > 1:
            narrow_send = after(narrow_send, grad_homes[0], keep, send)
        wide_keep, wide_send, got = keep, send, None
        if done < last:
            done += 1
            got = swap(send, *halving_stages()[done])
        keep, send = narrow_keep, narrow_send
        for step in range(last):
            keep, send = scatter_step(keep, send, step)
            if step == 0:
                result = land(result, homes, send)
            if step == 1:
                send = after(send, result)
                input_grad = land(input_grad, grad_homes, send)
            if step == 2:
                send = after(send, input_grad)
                if got is not None:
                    wide_keep, wide_send = scatter_join(wide_keep, after(got, send), done == last)
                while done < last:
                    done += 1
                    wide_keep, wide_send = scatter_step(wide_keep, wide_send, done)
        wide = wide_keep
        parts = ff // MODEL
        grad_up = jnp.concatenate([wide[c * part : (c + 1) * part] for c in range(parts)], axis=1)
        grad_down = wide[parts * part : 2 * parts * part]
        grad_out = wide[2 * parts * part :]
        grad_qkv, *owned_vec = run_finish(keep, swap(send, *halving_stages()[last]), widths)
        owned_vec = [item[0] for item in owned_vec]
    else:
        grad_up, grad_down, grad_out = (scatter_all(x) for x in (sums[0], sums[1].T, sums[2]))
        grad_qkv = scatter_all(total)
        mid, back = sum(vec_mid), sum(vec_back)
        vec = (
            back[1, :MODEL],
            back[1, MODEL : 2 * MODEL],
            back[0, : 2 * MODEL],
            back[0, 2 * MODEL :],
            mid[1, 2 * MODEL : 3 * MODEL],
            mid[1, :MODEL],
            mid[1, MODEL : 2 * MODEL],
            mid[0],
            mid[1, 3 * MODEL :],
        )
        owned_vec = [scatter_all(item) for item in vec]
        result, input_grad = land(result, homes), land(input_grad, grad_homes)
    result = result.reshape(micro, rows, width)
    input_grad = input_grad.reshape(micro, rows, width)
    g_gain1, g_bias1, g_qk, g_value, g_bout, g_gain2, g_bias2, g_bup, g_bdown = owned_vec
    return (
        result,
        input_grad,
        g_gain1,
        g_bias1,
        grad_qkv,
        g_qk,
        g_value,
        grad_out,
        g_bout,
        g_gain2,
        g_bias2,
        grad_up,
        g_bup,
        grad_down,
        g_bdown,
    )


def solution(mesh):
    rows = P(None, BOTH, None)
    vector = P(BOTH)
    matrix = P(BOTH, None)
    in_specs = (
        rows, rows, P(), P(), vector, vector, matrix, vector, matrix, vector, vector, vector,
        matrix, vector, matrix, vector,
    )
    out_specs = (
        rows, rows, vector, vector, matrix, vector, vector, matrix, vector, vector, vector,
        matrix, vector, matrix, vector,
    )
    return jax.shard_map(body, mesh=mesh, in_specs=in_specs, out_specs=out_specs, check_vma=False)
```

```python
import functools

import jax
import jax.numpy as jnp
from jax import lax
from jax.experimental import pallas as pl
from jax.experimental.pallas import tpu as pltpu
from jax.sharding import PartitionSpec as P

HEADS = 8
HEAD_DIM = 64
STRETCH = 64
LONGEST = 48
CHUNK = 2 * STRETCH
TILE = 4 * CHUNK
STATE_TILE = 8 * CHUNK
PAIRS = HEADS // 2
PAIR = 2 * HEAD_DIM
MODEL = HEADS * HEAD_DIM
BOTH = ("dp", "fsdp")
EPS = 1e-05
VMEM_LIMIT = 60 * 1024 * 1024

f32 = jnp.float32
bf16 = jnp.bfloat16


def nn(a, b):
    return lax.dot_general(a, b, (((1,), (0,)), ((), ())), preferred_element_type=f32)


def nt(a, b):
    return lax.dot_general(a, b, (((1,), (1,)), ((), ())), preferred_element_type=f32)


def tn(a, b):
    return lax.dot_general(a, b, (((0,), (0,)), ((), ())), preferred_element_type=f32)


def lanes(rows, width):
    return lax.broadcasted_iota(jnp.int32, (rows, width), 1)


def sublanes(rows, width):
    return lax.broadcasted_iota(jnp.int32, (rows, width), 0)


def first_head(rows):
    return lanes(rows, PAIR) < HEAD_DIM


def same_head():
    return (sublanes(PAIR, PAIR) // HEAD_DIM) == (lanes(PAIR, PAIR) // HEAD_DIM)


def by_head(x, rows):
    low = first_head(rows)
    zero = jnp.zeros_like(x)
    return jnp.concatenate([jnp.where(low, x, zero), jnp.where(low, zero, x)], axis=0)


def flag(value):
    return value.astype(f32)


def col(pair):
    return slice(pair * PAIR, (pair + 1) * PAIR)


def standardize(x):
    centre = jnp.mean(x, axis=-1, keepdims=True)
    centred = x - centre
    spread = jnp.mean(centred * centred, axis=-1, keepdims=True)
    scale = lax.rsqrt(spread + EPS)
    return centred * scale, scale


def norm_back(upstream, gain, n, scale):
    ug = upstream * gain
    return scale * (
        ug
        - jnp.mean(ug, axis=-1, keepdims=True)
        - n * jnp.mean(ug * n, axis=-1, keepdims=True)
    )


def unpack_state(block, pair):
    part = block[:HEAD_DIM, col(pair)]
    low = first_head(HEAD_DIM)
    zero = jnp.zeros_like(part)
    state = jnp.concatenate([jnp.where(low, part, zero), jnp.where(low, zero, part)], axis=0)
    row = block[HEAD_DIM : HEAD_DIM + 1, col(pair)]
    eye = sublanes(PAIR, PAIR) == lanes(PAIR, PAIR)
    diagonal = jnp.where(eye, row, 0.0)
    ones = jnp.where(same_head(), 1.0, 0.0).astype(bf16)
    high = diagonal.astype(bf16)
    low_part = (diagonal - high.astype(f32)).astype(bf16)
    sums = nn(high, ones) + nn(low_part, ones)
    return jnp.concatenate([state, sums], axis=1)


def pack_state(ref, pair, state, row):
    low = first_head(HEAD_DIM)
    ref[0, :HEAD_DIM, col(pair)] = jnp.where(low, state[:HEAD_DIM], state[HEAD_DIM:])
    ref[0, HEAD_DIM : HEAD_DIM + 1, col(pair)] = row
    ref[0, HEAD_DIM + 1 :, col(pair)] = jnp.zeros((7, PAIR), f32)


def pick(ref, place):
    per = ref.shape[2]
    return ref[lax.div(place, per), 0, lax.rem(place, per)]


def put(ref, place, value):
    per = ref.shape[2]
    ref[lax.div(place, per), 0, lax.rem(place, per)] = value


def group_spec(shape, first):
    block = (shape[0], 1) + tuple(shape[2:])
    return pl.BlockSpec(block, lambda i, *_: (0, first + i, 0, 0, 0))


def fixed(shape):
    zeros = (0,) * len(shape)
    return pl.BlockSpec(tuple(shape), lambda *_: zeros, pipeline_mode=pl.Buffered(1))


def member_spec(first=0):
    return pl.BlockSpec((1, HEAD_DIM + 8, MODEL), lambda i, *_: (first + i, 0, 0))


def tile_spec(width, tiles, reverse=False):
    if reverse:
        return pl.BlockSpec((TILE, width), lambda i, t, *_: (i * tiles + tiles - 1 - t, 0))
    return pl.BlockSpec((TILE, width), lambda i, t, *_: (i * tiles + t, 0))


def states_spec(tiles, reverse=False):
    block = (TILE // CHUNK, 3 * HEAD_DIM, MODEL)
    if reverse:
        return pl.BlockSpec(block, lambda i, t, *_: (i * tiles + tiles - 1 - t, 0, 0))
    return pl.BlockSpec(block, lambda i, t, *_: (i * tiles + t, 0, 0))


def params():
    return pltpu.CompilerParams(
        dimension_semantics=("arbitrary", "arbitrary"), vmem_limit_bytes=VMEM_LIMIT
    )


ANYWHERE = pl.BlockSpec(memory_space=pl.ANY)


GAIN_ONE, SHIFT_ONE, BIAS_QKV, BIAS_OUT, GAIN_TWO, SHIFT_TWO, BIAS_UP, BIAS_DOWN = range(8)


def vector(ref, row):
    width = 3 * MODEL if row == BIAS_QKV else ref.shape[1] if row == BIAS_UP else MODEL
    return ref[row : row + 1, :width]


def featured(mixed):
    return jnp.where(mixed > 0, mixed + 1.0, jnp.exp(jnp.minimum(mixed, 0.0))).astype(bf16)


def state_kernel(placing, closing, rows, weight, vec, state_out, x_scr, acc, sums):
    gain, shift, bias = vector(vec, GAIN_ONE), vector(vec, SHIFT_ONE), vector(vec, BIAS_QKV)
    micro, step = pl.program_id(0), pl.program_id(1)
    per = STATE_TILE // STRETCH

    @pl.when(step == 0)
    def _():
        acc[...] = jnp.zeros_like(acc)
        sums[...] = jnp.zeros_like(sums)

    for i in range(per):
        x_scr[i * STRETCH : (i + 1) * STRETCH, :] = pick(rows, placing[micro, step * per + i])
    n, _ = standardize(x_scr[...].astype(f32))
    normed = (n * gain + shift).astype(bf16)
    keep = jnp.concatenate(
        [jnp.full((STRETCH, 1), flag(closing[micro, step * per + i]), f32) for i in range(per)],
        axis=0,
    )
    at = slice(MODEL, 2 * MODEL)
    keys = featured(nn(normed, weight[:, at]) + bias[:, at]).astype(f32) * keep
    sums[...] += jnp.sum(keys, axis=0, keepdims=True)
    keys = keys.astype(bf16)
    at = slice(2 * MODEL, 3 * MODEL)
    values = (nn(normed, weight[:, at]) + bias[:, at]).astype(bf16)
    for pair in range(PAIRS):
        acc[pair] += tn(keys[:, col(pair)], values[:, col(pair)])

    @pl.when(step == pl.num_programs(1) - 1)
    def _():
        for pair in range(PAIRS):
            pack_state(state_out, pair, acc[pair], sums[:, col(pair)])


def run_state(placing, closing, rows, weight, vec):
    micro, count = placing.shape
    width = rows.shape[-1]
    tiles = count * STRETCH // STATE_TILE
    return pl.pallas_call(
        state_kernel,
        name="end_state",
        grid_spec=pltpu.PrefetchScalarGridSpec(
            num_scalar_prefetch=2,
            grid=(micro, tiles),
            in_specs=[
                group_spec(rows.shape, 0),
                fixed(weight.shape),
                fixed(vec.shape),
            ],
            out_specs=member_spec(),
            scratch_shapes=[
                pltpu.VMEM((STATE_TILE, width), bf16),
                pltpu.VMEM((PAIRS, PAIR, PAIR), f32),
                pltpu.VMEM((1, MODEL), f32),
            ],
        ),
        out_shape=jax.ShapeDtypeStruct((micro, HEAD_DIM + 8, MODEL), f32),
        compiler_params=params(),
        cost_estimate=pl.CostEstimate(
            flops=11 << 30, bytes_accessed=5 << 20, transcendentals=0
        ),
    )(placing, closing, rows, weight, vec)


def causal(second, transposed):
    i = sublanes(CHUNK, 2 * CHUNK)
    j = lanes(CHUNK, 2 * CHUNK) % CHUNK
    if transposed:
        i, j = j, i
    crosses = (i >= STRETCH) & (j < STRETCH)
    return jnp.where(crosses, 1.0 - second, jnp.where(j <= i, 1.0, 0.0))


def start_all(when, copies):
    @pl.when(when)
    def _():
        for copy in copies:
            copy.start()


def mid_kernel(
    placing,
    restart,
    opened,
    owner,
    _,
    rows_ref,
    cot_ref,
    inc_ref,
    w_qkv,
    vec,
    w_out_far,
    w_up_far,
    w_down_far,
    *refs,
    first,
    resumes,
    final,
):
    gain_one, shift_one, b_qkv = vector(vec, GAIN_ONE), vector(vec, SHIFT_ONE), vector(vec, BIAS_QKV)
    gain, shift = vector(vec, GAIN_TWO), vector(vec, SHIFT_TWO)
    b_out, b_up, b_down = vector(vec, BIAS_OUT), vector(vec, BIAS_UP), vector(vec, BIAS_DOWN)
    before, refs = (refs[:3], refs[3:]) if resumes else ((), refs)
    result, qkv_ref, branch_out, gn_out, gd_out, states_out, state_out, vec_out = refs[:8]
    refs = refs[8:]
    if final:
        keep_out, send_out, turned, acc_up, acc_down, acc_out = refs[:6]
        refs = refs[6:]
    else:
        far_up, far_down, far_out, acc_up, acc_down, acc_out = refs[:6]
        refs = refs[6:]
    carry, back, back_sum, att_scr, inv_scr, att_b, x_scr, cot_scr, w_out, w_up, w_down, sems = refs
    member, step = pl.program_id(0), pl.program_id(1)
    micro = first + member
    per = TILE // STRETCH
    opening = (member == 0) & (step == 0)
    closing = (member == pl.num_programs(0) - 1) & (step == pl.num_programs(1) - 1)
    arriving = [
        pltpu.make_async_copy(source, target, sems.at[n])
        for n, (source, target) in enumerate(
            [(w_out_far, w_out), (w_up_far, w_up), (w_down_far, w_down)]
            + list(zip(before, (acc_up, acc_down, acc_out)))
        )
    ]
    leaving = []

    @pl.when(opening)
    def _():
        vec_out[...] = jnp.zeros_like(vec_out)
        for copy in arriving:
            copy.start()
        if not resumes:
            acc_up[...] = jnp.zeros_like(acc_up)
            acc_down[...] = jnp.zeros_like(acc_down)
            acc_out[...] = jnp.zeros_like(acc_out)

    @pl.when(step == 0)
    def _():
        for pair in range(PAIRS):
            carry[pair] = unpack_state(inc_ref[0], pair)
        back[...] = jnp.zeros_like(back)
        back_sum[...] = jnp.zeros_like(back_sum)

    block = same_head()
    ones_head = jnp.where(block, 1.0, 0.0).astype(bf16)
    ones_twice = jnp.concatenate([ones_head, ones_head], axis=0)
    low = first_head(CHUNK)
    one_low = jnp.where(low, 1.0, 0.0).astype(bf16)
    one_high = jnp.where(low, 0.0, 1.0).astype(bf16)
    ones_both = jnp.concatenate([one_low, one_high], axis=0)
    ones_all = jnp.ones((CHUNK, PAIR), bf16)
    wide_block = jnp.concatenate([block, block], axis=1)
    upper = sublanes(CHUNK, PAIR) < STRETCH
    inner = lanes(PAIR, PAIR) % HEAD_DIM
    zero_s = jnp.zeros((PAIR, PAIR), bf16)
    low_half = first_head(HEAD_DIM)
    for i in range(per):
        x_scr[i * STRETCH : (i + 1) * STRETCH, :] = pick(rows_ref, placing[micro, step * per + i])
        cot_scr[i * STRETCH : (i + 1) * STRETCH, :] = pick(cot_ref, placing[micro, step * per + i])

    x = x_scr[...].astype(f32)
    n, _ = standardize(x)
    normed = (n * gain_one + shift_one).astype(bf16)
    for part in range(2):
        at = slice(part * MODEL, (part + 1) * MODEL)
        qkv_ref[:, at] = featured(nn(normed, w_qkv[:, at]) + b_qkv[:, at])
    at = slice(2 * MODEL, 3 * MODEL)
    qkv_ref[:, at] = (nn(normed, w_qkv[:, at]) + b_qkv[:, at]).astype(bf16)

    for chunk in range(TILE // CHUNK):
        rows = slice(chunk * CHUNK, (chunk + 1) * CHUNK)
        r0 = flag(restart[micro, step * per + 2 * chunk])
        r1 = flag(restart[micro, step * per + 2 * chunk + 1])
        mask = causal(r1, False)
        keep_low = jnp.where(upper, 1.0, 1.0 - r1)
        keep_key = jnp.where(upper, 1.0 - r1, 1.0)
        for pair in range(PAIRS):
            q = qkv_ref[rows, pair * PAIR : (pair + 1) * PAIR]
            k = qkv_ref[rows, MODEL + pair * PAIR : MODEL + (pair + 1) * PAIR]
            v = qkv_ref[rows, 2 * MODEL + pair * PAIR : 2 * MODEL + (pair + 1) * PAIR]
            state = carry[pair] * (1.0 - r0)
            state_b = state.astype(bf16)
            state_low = (state - state_b.astype(f32)).astype(bf16)
            marked = jnp.where(
                inner < 2, state_b[:, PAIR:], jnp.where(inner == 2, state_low[:, PAIR:], zero_s)
            )
            for n_, item in enumerate((state_b[:, :PAIR], marked, state_low[:, :PAIR])):
                states_out[chunk, n_ * HEAD_DIM : (n_ + 1) * HEAD_DIM, col(pair)] = jnp.where(
                    low_half, item[:HEAD_DIM], item[HEAD_DIM:]
                )
            mixing = nt(q, by_head(k, CHUNK)) * mask
            values = jnp.concatenate([by_head(v, CHUNK), ones_both], axis=1)
            out = nn(mixing.astype(bf16), values)
            out = out + nn((q.astype(f32) * keep_low).astype(bf16), state_b)
            inv = 1.0 / out[:, PAIR:]
            att = out[:, :PAIR] * inv
            att_scr[rows, col(pair)] = att
            inv_scr[rows, col(pair)] = inv
            att_b[rows, col(pair)] = att.astype(bf16)
            k_keep = (k.astype(f32) * keep_key).astype(bf16)
            added = tn(k_keep, jnp.concatenate([v, ones_all], axis=1))
            carry[pair] = state * (1.0 - r1) + jnp.where(wide_block, added, 0.0)

    @pl.when(opening)
    def _():
        for copy in arriving:
            copy.wait()

    middle = x_scr[...].astype(f32) + nn(att_b[...], w_out[...]) + b_out
    n, scale = standardize(middle)
    normed = (n * gain + shift).astype(bf16)
    normed_t = normed.T
    cot = cot_scr[...]
    cot_t = cot.T
    ff = w_up.shape[1]
    total = middle + b_down
    up_grad = jnp.zeros((TILE, MODEL), f32)
    for part in range(ff // MODEL):
        at = slice(part * MODEL, (part + 1) * MODEL)
        u = nn(normed, w_up[:, at]) + b_up[:, at]
        u2 = u * u
        t = jnp.tanh(u * (0.7978845608028654 + 0.035677408136300125 * u2))
        half = 0.5 + 0.5 * t
        act = (u * half).astype(bf16)
        rise = 1.5957691216057308 + 0.21406444881780074 * u2
        slope = half + u * half * (1.0 - half) * rise
        g = (nt(cot, w_down[at, :]) * slope).astype(bf16)
        total = total + nn(act, w_down[at, :])
        acc_down[:, at] += nn(cot_t, act)
        vec_out[0:1, at] += jnp.sum(g.astype(f32), axis=0, keepdims=True)
        up_grad = up_grad + nt(g, w_up[:, at])
        acc_up[:, at] += nn(normed_t, g)
        if not final:
            leaving.append(pltpu.make_async_copy(acc_down.at[:, at], far_down.at[:, at], sems.at[6 + 2 * part]))
            leaving.append(pltpu.make_async_copy(acc_up.at[:, at], far_up.at[:, at], sems.at[7 + 2 * part]))
            start_all(closing, leaving[-2:])
    total = total.astype(bf16)
    for i in range(per):
        put(result, placing[micro, step * per + i], total[i * STRETCH : (i + 1) * STRETCH, :])

    cot_f = cot.astype(f32)
    vec_out[1:2, :MODEL] += jnp.sum(up_grad * n, axis=0, keepdims=True)
    vec_out[1:2, MODEL : 2 * MODEL] += jnp.sum(up_grad, axis=0, keepdims=True)
    vec_out[1:2, 3 * MODEL : 4 * MODEL] += jnp.sum(cot_f, axis=0, keepdims=True)
    branch = (cot_f + norm_back(up_grad, gain, n, scale)).astype(bf16)
    branch_out[...] = branch
    vec_out[1:2, 2 * MODEL : 3 * MODEL] += jnp.sum(branch.astype(f32), axis=0, keepdims=True)
    grad_att = nt(branch, w_out[...])
    acc_out[...] += tn(att_b[...], branch)
    if not final:
        leaving.append(pltpu.make_async_copy(acc_out, far_out, sems.at[6 + 2 * (ff // MODEL)]))
        start_all(closing, leaving[-1:])
    lane = lanes(CHUNK, PAIR) % HEAD_DIM
    for chunk in range(TILE // CHUNK):
        rows = slice(chunk * CHUNK, (chunk + 1) * CHUNK)
        o0 = flag(opened[micro, step * per + 2 * chunk])
        o1 = flag(opened[micro, step * per + 2 * chunk + 1])
        keep = jnp.where(upper, o0, o1)
        for pair in range(PAIRS):
            inv = inv_scr[rows, col(pair)]
            gn = (grad_att[rows, col(pair)].astype(bf16).astype(f32) * inv).astype(bf16)
            product = gn.astype(f32) * att_scr[rows, col(pair)]
            high = product.astype(bf16)
            low_part = (product - high.astype(f32)).astype(bf16)
            gd = -nn(jnp.concatenate([high, low_part], axis=1), ones_twice)
            gd_high = gd.astype(bf16)
            gd_low = (gd - gd_high.astype(f32)).astype(bf16)
            zero = jnp.zeros_like(gd_high)
            gn_out[rows, col(pair)] = gn
            gd_out[rows, col(pair)] = jnp.where(
                (lane == 0) | (lane == 2), gd_high, jnp.where(lane == 1, gd_low, zero)
            )
            q = qkv_ref[rows, pair * PAIR : (pair + 1) * PAIR].astype(f32) * keep
            back[pair] += tn(q.astype(bf16), gn)
            back_sum[:, col(pair)] += jnp.sum(q * gd, axis=0, keepdims=True)

    @pl.when(step == pl.num_programs(1) - 1)
    def _():
        for pair in range(PAIRS):
            pack_state(state_out, pair, back[pair], back_sum[:, col(pair)])

    if not final:

        @pl.when(closing)
        def _():
            for copy in leaving:
                copy.wait()

    else:

        @pl.when(closing)
        def _():
            parts = ff // MODEL
            devices = 2 * keep_out.shape[0]
            less = MODEL // devices
            more = parts * less
            for part in range(parts):
                at = slice(part * MODEL, (part + 1) * MODEL)
                turned[at, :] = acc_down[:, at].T
            for j in range(devices):
                d = owner[j]
                target = keep_out if j < devices // 2 else send_out
                seat = j % (devices // 2)
                here = pl.ds(pl.multiple_of(d * less, less), less)
                for part in range(parts):
                    target[seat, part * less : (part + 1) * less, :] = acc_up[
                        here, part * MODEL : (part + 1) * MODEL
                    ].astype(target.dtype)
                there = pl.ds(pl.multiple_of(d * more, more), more)
                target[seat, more : 2 * more, :] = turned[there, :].astype(target.dtype)
                target[seat, 2 * more :, :] = acc_out[here, :].astype(target.dtype)


def run_mid(tables, first, members, target, rows, cot, inc, weights, vec, before, owner):
    micro, count = tables[0].shape
    width = rows.shape[-1]
    ff = weights[2].shape[1]
    count = count * STRETCH
    tiles = count // TILE
    total = members * count
    resumes, final = before is not None, owner is not None
    f32_sums = [(width, ff), (width, ff), (MODEL, width)]
    out_specs = [
        group_spec(target.shape, 0),
        tile_spec(3 * MODEL, tiles),
        tile_spec(width, tiles),
        tile_spec(MODEL, tiles),
        tile_spec(MODEL, tiles),
        states_spec(tiles),
        member_spec(),
        fixed((8, ff)),
    ]
    out_shape = [
        jax.ShapeDtypeStruct(target.shape, bf16),
        jax.ShapeDtypeStruct((total, 3 * MODEL), bf16),
        jax.ShapeDtypeStruct((total, width), bf16),
        jax.ShapeDtypeStruct((total, MODEL), bf16),
        jax.ShapeDtypeStruct((total, MODEL), bf16),
        jax.ShapeDtypeStruct((total // CHUNK, 3 * HEAD_DIM, MODEL), bf16),
        jax.ShapeDtypeStruct((members, HEAD_DIM + 8, MODEL), f32),
        jax.ShapeDtypeStruct((8, ff), f32),
    ]
    if final:
        devices = owner.shape[0]
        half = (devices // 2, (2 * ff + MODEL) // devices, MODEL)
        out_specs += [fixed(half), fixed(half)]
        out_shape += [jax.ShapeDtypeStruct(half, bf16)] * 2
    else:
        out_specs += [ANYWHERE] * 3
        out_shape += [jax.ShapeDtypeStruct(shape, f32) for shape in f32_sums]
    if not final:
        owner = jnp.zeros((8,), jnp.int32)
    scratch = [pltpu.VMEM((ff, width), f32)] if final else []
    scratch += [pltpu.VMEM(shape, f32) for shape in f32_sums]
    scratch += [
        pltpu.VMEM((PAIRS, PAIR, 2 * PAIR), f32),
        pltpu.VMEM((PAIRS, PAIR, PAIR), f32),
        pltpu.VMEM((1, MODEL), f32),
        pltpu.VMEM((TILE, MODEL), f32),
        pltpu.VMEM((TILE, MODEL), f32),
        pltpu.VMEM((TILE, MODEL), bf16),
        pltpu.VMEM((TILE, width), bf16),
        pltpu.VMEM((TILE, width), bf16),
    ]
    scratch += [pltpu.VMEM(item.shape, bf16) for item in weights[1:]]
    scratch.append(pltpu.SemaphoreType.DMA((7 + 2 * (ff // MODEL),)))
    return pl.pallas_call(
        functools.partial(mid_kernel, first=first, resumes=resumes, final=final),
        name="middle",
        grid_spec=pltpu.PrefetchScalarGridSpec(
            num_scalar_prefetch=4,
            grid=(members, tiles),
            in_specs=[
                ANYWHERE,
                group_spec(rows.shape, first),
                group_spec(cot[0].shape, cot[1]),
                member_spec(first),
            ]
            + [fixed(weights[0].shape), fixed(vec.shape)]
            + [ANYWHERE] * (6 if resumes else 3),
            out_specs=out_specs,
            scratch_shapes=scratch,
        ),
        out_shape=out_shape,
        compiler_params=params(),
        input_output_aliases={4: 0},
        cost_estimate=pl.CostEstimate(
            flops=members * (24 << 30), bytes_accessed=members << 24, transcendentals=0
        ),
    )(*tables[:3], owner, target, rows, cot[0], inc, weights[0], vec, *weights[1:], *(before or ()))


def back_kernel(
    placing,
    restart,
    reach,
    owner,
    _,
    rows_ref,
    qkv_ref,
    gn_ref,
    gd_ref,
    branch_ref,
    states_ref,
    weight_far,
    vec,
    owner_col,
    *refs,
    first,
    resumes,
    final,
    widths,
    sums,
    hops,
):
    incs, refs = refs[:hops], refs[hops:]
    gain, shift = vector(vec, GAIN_ONE), vector(vec, SHIFT_ONE)
    before, refs = (refs[:1], refs[1:]) if resumes else ((), refs)
    vec_others, refs = refs[:sums], refs[sums:]
    grad_rows, vec_out = refs[:2]
    refs = refs[2:]
    if final:
        keep_out, send_out, acc = refs[:3]
        refs = refs[3:]
    else:
        far_acc, acc = refs[:2]
        refs = refs[2:]
    carry, x_scr, mixed_scr, weight, sems = refs
    member, step = pl.program_id(0), pl.program_id(1)
    micro = first + member
    per = TILE // STRETCH
    tile = pl.num_programs(1) - 1 - step
    opening = (member == 0) & (step == 0)
    lane = lanes(CHUNK, PAIR)
    inner = lane % HEAD_DIM

    closing = (member == pl.num_programs(0) - 1) & (step == pl.num_programs(1) - 1)
    arriving = [pltpu.make_async_copy(weight_far, weight, sems.at[0])]
    if resumes:
        arriving.append(pltpu.make_async_copy(before[0], acc, sems.at[1]))
    leaving = [] if final else [pltpu.make_async_copy(acc, far_acc, sems.at[2])]

    @pl.when(opening)
    def _():
        vec_out[...] = jnp.zeros_like(vec_out)
        for copy in arriving:
            copy.start()
        if not resumes:
            acc[...] = jnp.zeros_like(acc)

    @pl.when(step == 0)
    def _():
        only = jnp.concatenate([jnp.ones((PAIR, PAIR), f32), jnp.where(inner == 0, 1.0, 0.0)], axis=1)
        inc = jnp.zeros((HEAD_DIM + 8, MODEL), f32)
        for hop, ref in enumerate(incs):
            inc = inc + ref[0] * reach[micro, hop]
        for pair in range(PAIRS):
            carry[pair] = unpack_state(inc, pair) * only

    block = same_head()
    wide_block = jnp.concatenate([block, block], axis=1)
    upper = sublanes(CHUNK, PAIR) < STRETCH
    marks = jnp.where((inner < 2) | (inner == 3), 1.0, 0.0).astype(bf16)
    mark_low = jnp.where(lane < 2, 1.0, 0.0).astype(bf16)
    mark_high = jnp.where((lane == HEAD_DIM) | (lane == HEAD_DIM + 1), 1.0, 0.0).astype(bf16)
    marks_both = jnp.concatenate([mark_low, mark_high], axis=0)
    for i in range(per):
        x_scr[i * STRETCH : (i + 1) * STRETCH, :] = pick(rows_ref, placing[micro, tile * per + i])

    for chunk in reversed(range(TILE // CHUNK)):
        rows = slice(chunk * CHUNK, (chunk + 1) * CHUNK)
        r0 = flag(restart[micro, tile * per + 2 * chunk])
        r1 = flag(restart[micro, tile * per + 2 * chunk + 1])
        r2 = flag(restart[micro, tile * per + 2 * chunk + 2])
        mask = causal(r1, False)
        mask_t = causal(r1, True)
        keep_low = jnp.where(upper, 1.0, 1.0 - r1)
        keep_key = jnp.where(upper, 1.0 - r1, 1.0)
        for pair in range(PAIRS):
            q = qkv_ref[rows, pair * PAIR : (pair + 1) * PAIR]
            k = qkv_ref[rows, MODEL + pair * PAIR : MODEL + (pair + 1) * PAIR]
            v = qkv_ref[rows, 2 * MODEL + pair * PAIR : 2 * MODEL + (pair + 1) * PAIR]
            gn = gn_ref[rows, col(pair)]
            gdx = gd_ref[rows, col(pair)]
            state, state_z, state_low = (
                by_head(states_ref[chunk, n * HEAD_DIM : (n + 1) * HEAD_DIM, col(pair)], HEAD_DIM)
                for n in range(3)
            )
            grown = carry[pair] * (1.0 - r2)
            grown_b = grown.astype(bf16)
            rest = grown - grown_b.astype(f32)
            grown_low = rest[:, :PAIR].astype(bf16)
            z_low = pltpu.roll(rest[:, PAIR:], 3, 1).astype(bf16)
            z_both = jnp.where(inner < 2, grown_b[:, PAIR:], jnp.where(inner == 3, z_low, jnp.zeros_like(z_low)))
            grown_x = jnp.concatenate([grown_b[:, :PAIR], z_both], axis=1)
            k2 = by_head(k, CHUNK)
            q2 = by_head(q, CHUNK)
            v2 = by_head(v, CHUNK)
            gn2 = by_head(gn, CHUNK)
            gd2 = by_head(gdx, CHUNK)
            both = jnp.concatenate([gn, gdx], axis=1)
            mixing_t = (nt(k, q2) * mask_t).astype(bf16)
            g_mix = (nt(both, jnp.concatenate([v2, marks_both], axis=1)) * mask).astype(bf16)
            v_marks = jnp.concatenate([v, marks], axis=1)
            g_mix_t = (nt(v_marks, jnp.concatenate([gn2, gd2], axis=1)) * mask_t).astype(bf16)
            dq = nn(g_mix, k2) + (
                nt(both, jnp.concatenate([state, state_z], axis=1)) + nt(gn, state_low)
            ) * keep_low
            dk = nn(g_mix_t, q2) + (nt(v_marks, grown_x) + nt(v, grown_low)) * keep_key
            dv = nn(mixing_t, gn2) + nn(k, grown_b[:, :PAIR]) * keep_key
            q_keep = (q.astype(f32) * keep_low).astype(bf16)
            added = tn(q_keep, both)
            carry[pair] = (grown * (1.0 - r1) + jnp.where(wide_block, added, 0.0)) * (1.0 - r0)
            mixed_scr[rows, pair * PAIR : (pair + 1) * PAIR] = (
                dq * jnp.minimum(q.astype(f32), 1.0)
            ).astype(bf16)
            mixed_scr[rows, MODEL + pair * PAIR : MODEL + (pair + 1) * PAIR] = (
                dk * jnp.minimum(k.astype(f32), 1.0)
            ).astype(bf16)
            mixed_scr[rows, 2 * MODEL + pair * PAIR : 2 * MODEL + (pair + 1) * PAIR] = dv.astype(bf16)

    @pl.when(opening)
    def _():
        for copy in arriving:
            copy.wait()

    mixed = mixed_scr[...]
    vec_out[0:1, :] += jnp.sum(mixed.astype(f32), axis=0, keepdims=True)
    upstream = nt(mixed, weight[...])
    n, scale = standardize(x_scr[...].astype(f32))
    normed_t = (n * gain + shift).astype(bf16).T
    for part in range(3):
        at = slice(part * MODEL, (part + 1) * MODEL)
        acc[:, at] += nn(normed_t, mixed[:, at])
    start_all(closing, leaving)
    vec_out[1:2, :MODEL] += jnp.sum(upstream * n, axis=0, keepdims=True)
    vec_out[1:2, MODEL : 2 * MODEL] += jnp.sum(upstream, axis=0, keepdims=True)
    total = (branch_ref[...].astype(f32) + norm_back(upstream, gain, n, scale)).astype(bf16)
    for i in range(per):
        put(grad_rows, placing[micro, tile * per + i], total[i * STRETCH : (i + 1) * STRETCH, :])

    if not final:

        @pl.when(closing)
        def _():
            for copy in leaving:
                copy.wait()

    else:

        @pl.when((member == pl.num_programs(0) - 1) & (step == pl.num_programs(1) - 1))
        def _():
            half = keep_out.shape[0]
            devices = 2 * half
            less = MODEL // devices
            for j in range(devices):
                here = pl.ds(pl.multiple_of(owner[j] * less, less), less)
                target = keep_out if j < half else send_out
                for part in range(3):
                    target[j % half, part * less : (part + 1) * less, :] = acc[
                        here, part * MODEL : (part + 1) * MODEL
                    ].astype(target.dtype)
            mid = sum(ref[...] for ref in vec_others if ref.shape[1] == vec_others[0].shape[1])
            rear = vec_out[...] + sum(
                ref[...] for ref in vec_others if ref.shape[1] != vec_others[0].shape[1]
            )
            sources = (
                rear[1:2, :MODEL],
                rear[1:2, MODEL : 2 * MODEL],
                rear[0:1, : 2 * MODEL],
                rear[0:1, 2 * MODEL :],
                mid[1:2, 2 * MODEL : 3 * MODEL],
                mid[1:2, :MODEL],
                mid[1:2, MODEL : 2 * MODEL],
                mid[0:1, :],
                mid[1:2, 3 * MODEL : 4 * MODEL],
            )
            rows8 = sublanes(8, MODEL)
            pieces = []
            for source, width in zip(sources, widths, strict=True):
                size = devices * width
                mine = (lanes(devices, size) // width) == owner_col[...]
                picked = jnp.where(mine, source, 0.0)
                gather = jnp.where(
                    (sublanes(size, PAIR) % width) == lanes(size, PAIR), 1.0, 0.0
                ).astype(bf16)
                high = picked.astype(bf16)
                low = (picked - high.astype(f32)).astype(bf16)
                pieces.append(nn(high, gather) + nn(low, gather))
            rest = jnp.zeros((1, MODEL - 2 * PAIR), f32)
            blank_row = jnp.zeros((1, PAIR), f32)
            for j in range(devices):
                block8 = jnp.zeros((8, MODEL), f32)
                for v, piece in enumerate(pieces[:8]):
                    more = pieces[8 + v][j : j + 1, :] if 8 + v < len(pieces) else blank_row
                    row = jnp.concatenate([piece[j : j + 1, :], more, rest], axis=1)
                    block8 = block8 + jnp.where(rows8 == v, row, 0.0)
                target = keep_out if j < half else send_out
                target[j % half, 3 * less :, :] = block8.astype(target.dtype)


def run_back(tables, first, members, target, rows, mid, incs, weight, vec, before, owner, others, widths):
    (group, seat), (saved, at) = target, mid
    micro, count = tables[0].shape
    width = rows.shape[-1]
    count = count * STRETCH
    tiles = count // TILE
    resumes, final = before is not None, owner is not None
    devices = lax.axis_size(BOTH) if final else 0
    if not final:
        owner = jnp.zeros((8,), jnp.int32)
        others = []
    half = (devices // 2, 3 * MODEL // max(devices, 1) + 8, MODEL)
    out_specs = [group_spec(group.shape, seat), fixed((8, 3 * MODEL))]
    out_shape = [
        jax.ShapeDtypeStruct(group.shape, bf16),
        jax.ShapeDtypeStruct((8, 3 * MODEL), f32),
    ]
    scratch = []
    if final:
        out_specs += [fixed(half), fixed(half)]
        out_shape += [jax.ShapeDtypeStruct(half, bf16)] * 2
    else:
        out_specs.append(ANYWHERE)
        out_shape.append(jax.ShapeDtypeStruct((width, 3 * MODEL), f32))
    scratch += [
        pltpu.VMEM((width, 3 * MODEL), f32),
        pltpu.VMEM((PAIRS, PAIR, 2 * PAIR), f32),
        pltpu.VMEM((TILE, width), bf16),
        pltpu.VMEM((TILE, 3 * MODEL), bf16),
        pltpu.VMEM(weight.shape, bf16),
        pltpu.SemaphoreType.DMA((3,)),
    ]

    def tile(width_):
        return pl.BlockSpec((TILE, width_), lambda i, t, *_: ((at + i) * tiles + tiles - 1 - t, 0))

    return pl.pallas_call(
        functools.partial(
            back_kernel,
            first=first,
            resumes=resumes,
            final=final,
            widths=widths,
            sums=len(others),
            hops=len(incs),
        ),
        name="back",
        grid_spec=pltpu.PrefetchScalarGridSpec(
            num_scalar_prefetch=4,
            grid=(members, tiles),
            in_specs=[
                ANYWHERE,
                group_spec(rows.shape, first),
                tile(3 * MODEL),
                tile(MODEL),
                tile(MODEL),
                tile(width),
                pl.BlockSpec(
                    (TILE // CHUNK, 3 * HEAD_DIM, MODEL),
                    lambda i, t, *_: ((at + i) * tiles + tiles - 1 - t, 0, 0),
                ),
                ANYWHERE,
                fixed(vec.shape),
                fixed((owner.shape[0], 1)),
            ]
            + [member_spec(at)] * len(incs)
            + ([ANYWHERE] if resumes else [])
            + [fixed(item.shape) for item in others],
            out_specs=out_specs,
            scratch_shapes=scratch,
        ),
        out_shape=out_shape,
        input_output_aliases={4: 0},
        compiler_params=params(),
        cost_estimate=pl.CostEstimate(
            flops=members * (15 << 30), bytes_accessed=members << 24, transcendentals=0
        ),
    )(
        tables[0],
        tables[1],
        tables[3],
        owner,
        group,
        rows,
        saved[1],
        saved[3],
        saved[4],
        saved[2],
        saved[5],
        weight,
        vec,
        owner[:, None],
        *incs,
        *(() if before is None else (before,)),
        *others,
    )


def send_kernel(slot, source, target, *, first):
    micro = first + pl.program_id(0)
    for i in range(source.shape[1]):
        put(target, slot[micro, i], source[0, i])


def run_send(slot, rows, first, members):
    micro, count, width = rows.shape
    stretches = count // STRETCH
    groups = lax.axis_size("dp")
    shape = (groups, members, stretches // groups, STRETCH, width)
    return pl.pallas_call(
        functools.partial(send_kernel, first=first),
        name="send",
        grid_spec=pltpu.PrefetchScalarGridSpec(
            num_scalar_prefetch=1,
            grid=(members,),
            in_specs=[
                pl.BlockSpec((1, stretches, STRETCH, width), lambda i, *_: (first + i, 0, 0, 0))
            ],
            out_specs=pl.BlockSpec((groups, 1) + shape[2:], lambda i, *_: (0, i, 0, 0, 0)),
        ),
        out_shape=jax.ShapeDtypeStruct(shape, rows.dtype),
        compiler_params=pltpu.CompilerParams(vmem_limit_bytes=VMEM_LIMIT),
        cost_estimate=pl.CostEstimate(
            flops=0, bytes_accessed=4 * members * count * width, transcendentals=0
        ),
    )(slot, rows.reshape(micro, stretches, STRETCH, width))


def land_kernel(slot, _, source, target, *, first):
    micro = first + pl.program_id(0)
    for i in range(target.shape[1]):
        target[0, i] = pick(source, slot[micro, i])


def run_land(slot, landed, output, first):
    members = landed.shape[1]
    shape = output.shape
    block = (landed.shape[0], 1) + landed.shape[2:]
    return pl.pallas_call(
        functools.partial(land_kernel, first=first),
        name="land",
        grid_spec=pltpu.PrefetchScalarGridSpec(
            num_scalar_prefetch=1,
            grid=(members,),
            in_specs=[
                pl.BlockSpec(memory_space=pl.ANY),
                pl.BlockSpec(block, lambda i, *_: (0, i, 0, 0, 0)),
            ],
            out_specs=pl.BlockSpec((1,) + shape[1:], lambda i, *_: (first + i, 0, 0, 0)),
        ),
        out_shape=jax.ShapeDtypeStruct(shape, output.dtype),
        input_output_aliases={1: 0},
        compiler_params=pltpu.CompilerParams(vmem_limit_bytes=VMEM_LIMIT),
        cost_estimate=pl.CostEstimate(flops=0, bytes_accessed=4 * landed.size, transcendentals=0),
    )(slot, output, landed)


def blank(shape):
    return pl.pallas_call(
        lambda ref: None,
        name="blank",
        out_specs=pl.BlockSpec(memory_space=pl.ANY),
        out_shape=jax.ShapeDtypeStruct(shape, bf16),
    )()


def index_tables(lengths, stretch_order, count):
    fsdp = lax.axis_size("fsdp")
    groups = lax.axis_size("dp")
    device = lax.axis_index(BOTH)
    base = device * count
    within = jnp.arange(count, dtype=jnp.int32)
    mine = base + within
    place = jnp.arange(stretch_order.shape[1], dtype=jnp.int32)
    here = place[None, None, :]
    landing = jnp.sum(
        jnp.where(stretch_order[:, None, :] == mine[None, :, None], here, 0), axis=-1
    )
    slot = jnp.sum((landing[:, None, :] < landing[:, :, None]).astype(jnp.int32), axis=-1)
    arrival = jnp.sum(
        jnp.where(here == mine[None, :, None], stretch_order[:, None, :], 0), axis=-1
    )
    source = arrival // count // fsdp
    ahead = (source[:, None, :] == source[:, :, None]) & (
        within[None, None, :] < within[None, :, None]
    )
    placing = source * (count // groups) + jnp.sum(ahead.astype(jnp.int32), axis=-1)
    index = jnp.arange(lengths.shape[1], dtype=jnp.int32)
    starts = jnp.sum(
        jnp.where(index[None, None, :] < index[None, :, None], lengths[:, None, :], 0), axis=-1
    )
    edge = base + jnp.arange(count + 1, dtype=jnp.int32)
    restart = jnp.any(starts[:, None, :] == edge[None, :, None], axis=-1).astype(jnp.int32)
    restart = jnp.where(edge[None, :] == stretch_order.shape[1], 1, restart)
    opened = 1 - jnp.any(
        (starts[:, None, :] >= base) & (starts[:, None, :] <= mine[None, :, None]), axis=-1
    ).astype(jnp.int32)
    last = base + count - 1
    closing = 1 - jnp.any(
        (starts[:, None, :] > mine[None, :, None]) & (starts[:, None, :] <= last), axis=-1
    ).astype(jnp.int32)
    hops = -(-(LONGEST - 1) // count)
    hop = jnp.arange(hops, dtype=jnp.int32)
    reach_back = base - 1 - hop * count
    from_before = 1.0 - jnp.any(
        (starts[:, None, :] > reach_back[None, :, None]) & (starts[:, None, :] <= base), axis=-1
    ).astype(f32)
    reach_on = base + (hop + 1) * count
    from_after = 1.0 - jnp.any(
        (starts[:, None, :] > last) & (starts[:, None, :] <= reach_on[None, :, None]), axis=-1
    ).astype(f32)
    first = base - hop * count
    unbroken = 1.0 - jnp.any(
        (starts[:, None, :] >= first[None, :, None]) & (starts[:, None, :] <= last), axis=-1
    ).astype(f32)
    return slot, placing, restart, opened, closing, from_before, from_after, unbroken


def exchange(states, hops, forward):
    size = lax.axis_size("fsdp")
    got = []
    for hop in range(min(hops, size - 1)):
        step = hop + 1
        pairs = [(i, i + step) if forward else (i + step, i) for i in range(size - step)]
        got.append(lax.ppermute(states, "fsdp", pairs))
    return got


def passed_on(states, weights, unbroken, beside):
    size = lax.axis_size("fsdp")
    total, own, step = jnp.zeros_like(states), states, 1
    while step <= weights.shape[1] and step < size:
        got = lax.ppermute(own, "fsdp", [(i, i + step) for i in range(size - step)])
        if step == 1:
            got = after(got, beside)
        total = total + got * weights[:, step - 1, None, None]
        own = own + got * unbroken[:, step - 1, None, None]
        step *= 2
    return total


def halving_stages():
    stages = []
    dp, fsdp = lax.axis_size("dp"), lax.axis_size("fsdp")
    if dp > 1:
        stages.append(("dp", 1))
    bit = 1
    while bit < fsdp:
        stages.append(("fsdp", bit))
        bit *= 2
    bit = 2
    while bit < dp:
        stages.append(("dp", bit))
        bit *= 2
    return stages


def order_tables():
    stages = halving_stages()
    fsdp = lax.axis_size("fsdp")
    devices = lax.axis_size(BOTH)
    me = lax.axis_index(BOTH)
    index = jnp.arange(devices, dtype=jnp.int32)
    bits = [bit * (fsdp if axis == "dp" else 1) for axis, bit in stages]
    place = jnp.zeros((devices,), jnp.int32)
    owner = jnp.zeros((devices,), jnp.int32)
    for s, bit in enumerate(bits):
        rank = len(bits) - 1 - s
        place = place + jnp.where(((index ^ me) & bit) != 0, 1 << rank, 0)
        owner = owner + jnp.where(((index >> rank) & 1) != 0, bit, 0)
    return place, owner ^ me


def after(x, *others):
    return lax.optimization_barrier((x, others))[0]


def swap(x, axis, bit):
    return lax.ppermute(x, axis, [(i, i ^ bit) for i in range(lax.axis_size(axis))])


def gather_halves(x, ties):
    stages = list(reversed(halving_stages()))
    steps = []
    for s, (axis, bit) in enumerate(stages[:-1]):
        if s in ties:
            x = after(x, ties[s])
        x = jnp.concatenate([x, swap(x, axis, bit)], axis=0)
        steps.append(x)
    return (x, swap(x, *stages[-1])), steps


def scatter_step(keep, send, s):
    stages = halving_stages()
    return scatter_join(keep, swap(send, *stages[s]), s == len(stages) - 1)


def scatter_join(keep, got, last):
    if last:
        return keep[0].astype(f32) + got[0].astype(f32), None
    half = keep.shape[0] // 2
    send = (keep[half:].astype(f32) + got[half:].astype(f32)).astype(bf16)
    return keep[:half].astype(f32) + got[:half].astype(f32), send


def finish_kernel(keep, got, qkv, *vectors):
    total = keep[0] + got[0].astype(f32)
    rows = qkv.shape[0]
    for part in range(3):
        qkv[:, part * MODEL : (part + 1) * MODEL] = total[part * rows : (part + 1) * rows, :]
    for v, ref in enumerate(vectors):
        row, at = 3 * rows + v % 8, v // 8 * PAIR
        ref[...] = total[row : row + 1, at : at + ref.shape[1]]


def run_finish(keep, got, widths):
    rows = (keep.shape[1] - 8) // 3
    return pl.pallas_call(
        finish_kernel,
        name="finish",
        out_shape=[jax.ShapeDtypeStruct((rows, 3 * MODEL), f32)]
        + [jax.ShapeDtypeStruct((1, width), f32) for width in widths],
    )(keep, got)


def pack_kernel(qkv, out, up, down, *refs):
    *small, first, second = refs
    rows = qkv.shape[0]
    for c in range(3):
        first[0, c * rows : (c + 1) * rows, :] = qkv[:, c * MODEL : (c + 1) * MODEL]
    row = sublanes(16, PAIR)
    side = jnp.zeros((16, PAIR), f32)
    for v, item in enumerate(small):
        width = item.shape[1]
        spread = jnp.where(sublanes(width, PAIR) == lanes(width, PAIR), 1.0, 0.0).astype(bf16)
        tall = jnp.broadcast_to(item[...].astype(f32), (16, width)).astype(bf16)
        side = side + jnp.where(row == v, nn(tall, spread), 0.0)
    side = jnp.concatenate([side, jnp.zeros((16, MODEL - PAIR), f32)], axis=1)
    first[0, 3 * rows : 3 * rows + 16, :] = side.astype(bf16)
    parts = up.shape[1] // MODEL
    for c in range(parts):
        second[0, c * rows : (c + 1) * rows, :] = up[:, c * MODEL : (c + 1) * MODEL]
    second[0, parts * rows : 2 * parts * rows, :] = down[...]
    second[0, 2 * parts * rows :, :] = out[...]


def run_pack(qkv, out, up, down, small):
    rows = qkv.shape[0]
    parts = up.shape[1] // MODEL
    return pl.pallas_call(
        pack_kernel,
        name="pack",
        out_shape=[
            jax.ShapeDtypeStruct((1, 3 * rows + 16, MODEL), bf16),
            jax.ShapeDtypeStruct((1, (2 * parts + 1) * rows, MODEL), bf16),
        ],
    )(qkv, out, up, down, *(item[None] for item in small))


def sort_first_kernel(place, own, got, owner, qkv, vectors, *, widths):
    half, total, _ = own.shape
    rows = total // 4

    def part(d):
        p = place[d]
        q = lax.rem(p, half)
        return jnp.where(p < half, own[q, : 3 * rows, :], got[q, : 3 * rows, :])

    for d in range(2 * half):
        block = part(d)
        for c in range(3):
            qkv[d * rows : (d + 1) * rows, c * MODEL : (c + 1) * MODEL] = block[
                c * rows : (c + 1) * rows, :
            ]
    small = jnp.concatenate(
        [own[:, 3 * rows :, :PAIR].astype(f32), got[:, 3 * rows :, :PAIR].astype(f32)], axis=0
    )
    row = lax.broadcasted_iota(jnp.int32, small.shape, 1)
    vectors[...] = jnp.zeros_like(vectors)
    for v, width in enumerate(widths):
        values = jnp.sum(jnp.where(row == v, small, 0.0), axis=1)
        size = 2 * half * width
        lane = lanes(PAIR, size) % width
        spread = jnp.where(lane == sublanes(PAIR, size), 1.0, 0.0).astype(bf16)
        wide = nn(values.astype(bf16), spread)
        mine = (lanes(2 * half, size) // width) == owner[...]
        vectors[v : v + 1, :size] = jnp.sum(jnp.where(mine, wide, 0.0), axis=0, keepdims=True)


def run_sort_first(place, owner, own, got, widths):
    devices = place.shape[0]
    rows = own.shape[1] // 4
    vmem = pl.BlockSpec(memory_space=pltpu.VMEM)
    return pl.pallas_call(
        functools.partial(sort_first_kernel, widths=widths),
        name="sort_first",
        in_specs=[pl.BlockSpec(memory_space=pltpu.SMEM), vmem, vmem, vmem],
        out_specs=[vmem, vmem],
        out_shape=[
            jax.ShapeDtypeStruct((devices * rows, 3 * MODEL), bf16),
            jax.ShapeDtypeStruct((8, devices * max(widths)), f32),
        ],
        compiler_params=pltpu.CompilerParams(vmem_limit_bytes=VMEM_LIMIT),
    )(place, own, got, owner[:, None])


def sort_second_kernel(gathered, up, down, out):
    devices, total, _ = gathered.shape
    parts = up.shape[1] // MODEL
    rows = total // (2 * parts + 1)
    tall = parts * rows
    for d in range(devices):
        for c in range(parts):
            up[d * rows : (d + 1) * rows, c * MODEL : (c + 1) * MODEL] = gathered[
                d, c * rows : (c + 1) * rows, :
            ]
        down[d * tall : (d + 1) * tall, :] = gathered[d, tall : 2 * tall, :]
        out[d * rows : (d + 1) * rows, :] = gathered[d, 2 * tall :, :]


def run_sort_second(gathered, ff):
    devices = gathered.shape[0]
    rows = gathered.shape[1] // (2 * (ff // MODEL) + 1)
    vmem = pl.BlockSpec(memory_space=pltpu.VMEM)
    return pl.pallas_call(
        sort_second_kernel,
        name="sort_second",
        in_specs=[vmem],
        out_specs=[vmem, vmem, vmem],
        out_shape=[
            jax.ShapeDtypeStruct((devices * rows, ff), bf16),
            jax.ShapeDtypeStruct((ff, MODEL), bf16),
            jax.ShapeDtypeStruct((devices * rows, MODEL), bf16),
        ],
        compiler_params=pltpu.CompilerParams(vmem_limit_bytes=VMEM_LIMIT),
    )(gathered)


def gather_all(x):
    return lax.all_gather(x, BOTH, axis=0, tiled=True)


def scatter_all(x):
    return lax.psum_scatter(x, BOTH, scatter_dimension=0, tiled=True)


def to_dp(group):
    return lax.all_to_all(group, "dp", split_axis=0, concat_axis=0, tiled=True)


def groups_of(micro):
    return [(0, micro - 1), (micro - 1, 1)] if micro > 1 else [(0, 1)]


def find(groups, m):
    for g, (first, members) in enumerate(groups):
        if first <= m < first + members:
            return g, m - first


def body(
    tokens,
    cotangent,
    lengths,
    stretch_order,
    ln1_gain,
    ln1_bias,
    w_qkv,
    b_qkv,
    w_out,
    b_out,
    ln2_gain,
    ln2_bias,
    w_up,
    b_up,
    w_down,
    b_down,
):
    micro, rows, width = tokens.shape
    count = rows // STRETCH
    devices = lax.axis_size(BOTH)
    ff = w_up.shape[1]
    dp = lax.axis_size("dp")
    slot, placing, restart, opened, closing, from_before, from_after, unbroken = index_tables(
        lengths, stretch_order, count
    )
    tables = (placing, restart, opened, from_after)
    small = (ln1_gain, ln1_bias, b_qkv, b_out, ln2_gain, ln2_bias, b_up, b_down)
    in_parts = (width // devices) % 16 == 0
    groups = groups_of(micro)
    sent = run_send(slot, tokens, 0, micro)
    if in_parts:
        place, owner = order_tables()
        first_part, second_part = run_pack(w_qkv, w_out, w_up, w_down, small)
        halves, steps = gather_halves(first_part, {1: sent, 2: tables + (closing, from_before, unbroken)})
        moved = to_dp(after(sent, steps[0]))
        qkv_all, vectors = run_sort_first(
            place, owner, *halves, [item.shape[0] for item in small]
        )
        ready = (qkv_all,)
        second_part = gather_all(second_part)
    else:
        owner, ready = None, ()
        moved = to_dp(sent)
        qkv_all, out_all = gather_all(w_qkv), gather_all(w_out)
        up_all, down_all = gather_all(w_up), gather_all(w_down)
        vectors = [gather_all(item).astype(f32) for item in small]
        vectors = jnp.stack([jnp.pad(item, (0, ff - item.shape[0])) for item in vectors])

    sent_grads = run_send(slot, after(cotangent, *ready), 0, micro)
    hops = from_before.shape[1]
    states = run_state(placing, closing, moved, qkv_all, vectors)
    cots = to_dp(sent_grads)
    if in_parts:
        up_all, down_all, out_all = run_sort_second(after(second_part, states), ff)
    incoming = passed_on(states, from_before, unbroken, out_all)
    weights = [qkv_all, out_all, up_all, down_all]
    mids, sums = [], None
    for g, (first, members) in enumerate(groups):
        target = blank((dp, members, count // dp, STRETCH, width))
        out = run_mid(
            tables,
            first,
            members,
            target,
            moved,
            (cots, first),
            incoming,
            weights,
            vectors,
            sums,
            owner if g == len(groups) - 1 else None,
        )
        sums = out[8:]
        mids.append(out)
    outgoing = [exchange(out[6], hops, False) for out in mids]
    homes = [to_dp(out[0]) for out in mids]
    sizes = [MODEL, MODEL, 2 * MODEL, MODEL, MODEL, MODEL, MODEL, ff, MODEL]
    widths = [size // devices for size in sizes]
    last = len(halving_stages()) - 1
    late = len(groups) - 1
    outgoing[0] = after(outgoing[0], *([mids[-1][7]] if late else []))
    if in_parts:
        keep, send = sums
        if late:
            send = after(send, outgoing[0], homes[0])
        keep, send = scatter_step(keep, send, 0)
        done = 0
    vec_mid = [f[7] for f in mids]
    vec_back, total = [], None
    grad_rows = []
    for g, (first, members) in enumerate(groups):
        if g:
            outgoing[g] = after(outgoing[g], vec_back[0], homes[g])
            grad_rows[0] = after(grad_rows[0], outgoing[g])
        saved = list(mids[g])
        if in_parts:
            saved[2], keep, send = lax.optimization_barrier((saved[2], keep, send))
            got = swap(send, *halving_stages()[done + 1])
        out = run_back(
            tables,
            first,
            members,
            (blank((dp, members, count // dp, STRETCH, width)), 0),
            moved,
            (saved, 0),
            outgoing[g],
            qkv_all,
            vectors,
            total,
            owner if g == late else None,
            vec_mid + vec_back,
            widths,
        )
        grad_rows.append(out[0])
        vec_back.append(out[1])
        total = out[2]
        if in_parts:
            done += 1
            keep, send = scatter_join(keep, after(got, out[1]), done == last)
            if g == late:
                grad_rows[g] = after(grad_rows[g], keep)
    narrow = out[2:]
    grad_homes = [to_dp(group) for group in grad_rows]
    result = blank((micro, count, STRETCH, width))
    input_grad = blank((micro, count, STRETCH, width))

    def land(output, pieces, *others):
        for (first, _), home in zip(groups, pieces, strict=True):
            output = run_land(slot, after(home, *others), output, first)
        return output

    if in_parts:
        part = width // devices
        narrow_keep, narrow_send = narrow
        if len(groups) > 1:
            narrow_send = after(narrow_send, grad_homes[0], keep, send)
        wide_keep, wide_send, got = keep, send, None
        if done < last:
            done += 1
            got = swap(send, *halving_stages()[done])
        keep, send = narrow_keep, narrow_send
        for step in range(last):
            keep, send = scatter_step(keep, send, step)
            if step == 0:
                result = land(result, homes, send)
            if step == 1:
                send = after(send, result, *(() if got is None else (got,)))
                input_grad = land(input_grad, grad_homes, send)
            if step == 2:
                send = after(send, input_grad)
                if got is not None:
                    wide_keep, wide_send = scatter_join(wide_keep, after(got, send), done == last)
                while done < last:
                    done += 1
                    wide_keep, wide_send = scatter_step(wide_keep, wide_send, done)
        wide = wide_keep
        parts = ff // MODEL
        grad_up = jnp.concatenate([wide[c * part : (c + 1) * part] for c in range(parts)], axis=1)
        grad_down = wide[parts * part : 2 * parts * part]
        grad_out = wide[2 * parts * part :]
        grad_qkv, *owned_vec = run_finish(keep, swap(send, *halving_stages()[last]), widths)
        owned_vec = [item[0] for item in owned_vec]
    else:
        grad_up, grad_down, grad_out = (scatter_all(x) for x in (sums[0], sums[1].T, sums[2]))
        grad_qkv = scatter_all(total)
        mid, back = sum(vec_mid), sum(vec_back)
        vec = (
            back[1, :MODEL],
            back[1, MODEL : 2 * MODEL],
            back[0, : 2 * MODEL],
            back[0, 2 * MODEL :],
            mid[1, 2 * MODEL : 3 * MODEL],
            mid[1, :MODEL],
            mid[1, MODEL : 2 * MODEL],
            mid[0],
            mid[1, 3 * MODEL :],
        )
        owned_vec = [scatter_all(item) for item in vec]
        result, input_grad = land(result, homes), land(input_grad, grad_homes)
    result = result.reshape(micro, rows, width)
    input_grad = input_grad.reshape(micro, rows, width)
    g_gain1, g_bias1, g_qk, g_value, g_bout, g_gain2, g_bias2, g_bup, g_bdown = owned_vec
    return (
        result,
        input_grad,
        g_gain1,
        g_bias1,
        grad_qkv,
        g_qk,
        g_value,
        grad_out,
        g_bout,
        g_gain2,
        g_bias2,
        grad_up,
        g_bup,
        grad_down,
        g_bdown,
    )


def solution(mesh):
    rows = P(None, BOTH, None)
    vector = P(BOTH)
    matrix = P(BOTH, None)
    in_specs = (
        rows, rows, P(), P(), vector, vector, matrix, vector, matrix, vector, vector, vector,
        matrix, vector, matrix, vector,
    )
    out_specs = (
        rows, rows, vector, vector, matrix, vector, vector, matrix, vector, vector, vector,
        matrix, vector, matrix, vector,
    )
    return jax.shard_map(body, mesh=mesh, in_specs=in_specs, out_specs=out_specs, check_vma=False)
```

```python
import functools

import jax
import jax.numpy as jnp
from jax import lax
from jax.experimental import pallas as pl
from jax.experimental.pallas import tpu as pltpu
from jax.sharding import PartitionSpec as P

HEADS = 8
HEAD_DIM = 64
STRETCH = 64
LONGEST = 48
CHUNK = 2 * STRETCH
TILE = 4 * CHUNK
STATE_TILE = 8 * CHUNK
PAIRS = HEADS // 2
PAIR = 2 * HEAD_DIM
MODEL = HEADS * HEAD_DIM
BOTH = ("dp", "fsdp")
EPS = 1e-05
VMEM_LIMIT = 60 * 1024 * 1024

f32 = jnp.float32
bf16 = jnp.bfloat16


def nn(a, b):
    return lax.dot_general(a, b, (((1,), (0,)), ((), ())), preferred_element_type=f32)


def nt(a, b):
    return lax.dot_general(a, b, (((1,), (1,)), ((), ())), preferred_element_type=f32)


def tn(a, b):
    return lax.dot_general(a, b, (((0,), (0,)), ((), ())), preferred_element_type=f32)


def lanes(rows, width):
    return lax.broadcasted_iota(jnp.int32, (rows, width), 1)


def sublanes(rows, width):
    return lax.broadcasted_iota(jnp.int32, (rows, width), 0)


def first_head(rows):
    return lanes(rows, PAIR) < HEAD_DIM


def same_head():
    return (sublanes(PAIR, PAIR) // HEAD_DIM) == (lanes(PAIR, PAIR) // HEAD_DIM)


def by_head(x, rows):
    low = first_head(rows)
    zero = jnp.zeros_like(x)
    return jnp.concatenate([jnp.where(low, x, zero), jnp.where(low, zero, x)], axis=0)


def flag(value):
    return value.astype(f32)


def col(pair):
    return slice(pair * PAIR, (pair + 1) * PAIR)


def standardize(x):
    centre = jnp.mean(x, axis=-1, keepdims=True)
    centred = x - centre
    spread = jnp.mean(centred * centred, axis=-1, keepdims=True)
    scale = lax.rsqrt(spread + EPS)
    return centred * scale, scale


def norm_back(upstream, gain, n, scale):
    ug = upstream * gain
    return scale * (
        ug
        - jnp.mean(ug, axis=-1, keepdims=True)
        - n * jnp.mean(ug * n, axis=-1, keepdims=True)
    )


def unpack_state(block, pair):
    part = block[:HEAD_DIM, col(pair)]
    low = first_head(HEAD_DIM)
    zero = jnp.zeros_like(part)
    state = jnp.concatenate([jnp.where(low, part, zero), jnp.where(low, zero, part)], axis=0)
    row = block[HEAD_DIM : HEAD_DIM + 1, col(pair)]
    eye = sublanes(PAIR, PAIR) == lanes(PAIR, PAIR)
    diagonal = jnp.where(eye, row, 0.0)
    ones = jnp.where(same_head(), 1.0, 0.0).astype(bf16)
    high = diagonal.astype(bf16)
    low_part = (diagonal - high.astype(f32)).astype(bf16)
    sums = nn(high, ones) + nn(low_part, ones)
    return jnp.concatenate([state, sums], axis=1)


def pack_state(ref, pair, state, row):
    low = first_head(HEAD_DIM)
    ref[0, :HEAD_DIM, col(pair)] = jnp.where(low, state[:HEAD_DIM], state[HEAD_DIM:])
    ref[0, HEAD_DIM : HEAD_DIM + 1, col(pair)] = row
    ref[0, HEAD_DIM + 1 :, col(pair)] = jnp.zeros((7, PAIR), f32)


def pick(ref, place):
    per = ref.shape[2]
    return ref[lax.div(place, per), 0, lax.rem(place, per)]


def put(ref, place, value):
    per = ref.shape[2]
    ref[lax.div(place, per), 0, lax.rem(place, per)] = value


def group_spec(shape, first):
    block = (shape[0], 1) + tuple(shape[2:])
    return pl.BlockSpec(block, lambda i, *_: (0, first + i, 0, 0, 0))


def fixed(shape):
    zeros = (0,) * len(shape)
    return pl.BlockSpec(tuple(shape), lambda *_: zeros, pipeline_mode=pl.Buffered(1))


def member_spec(first=0):
    return pl.BlockSpec((1, HEAD_DIM + 8, MODEL), lambda i, *_: (first + i, 0, 0))


def tile_spec(width, tiles, reverse=False):
    if reverse:
        return pl.BlockSpec((TILE, width), lambda i, t, *_: (i * tiles + tiles - 1 - t, 0))
    return pl.BlockSpec((TILE, width), lambda i, t, *_: (i * tiles + t, 0))


def states_spec(tiles, reverse=False):
    block = (TILE // CHUNK, 3 * HEAD_DIM, MODEL)
    if reverse:
        return pl.BlockSpec(block, lambda i, t, *_: (i * tiles + tiles - 1 - t, 0, 0))
    return pl.BlockSpec(block, lambda i, t, *_: (i * tiles + t, 0, 0))


def params():
    return pltpu.CompilerParams(
        dimension_semantics=("arbitrary", "arbitrary"), vmem_limit_bytes=VMEM_LIMIT
    )


ANYWHERE = pl.BlockSpec(memory_space=pl.ANY)


GAIN_ONE, SHIFT_ONE, BIAS_QKV, BIAS_OUT, GAIN_TWO, SHIFT_TWO, BIAS_UP, BIAS_DOWN = range(8)


def vector(ref, row):
    width = 3 * MODEL if row == BIAS_QKV else ref.shape[1] if row == BIAS_UP else MODEL
    return ref[row : row + 1, :width]


def featured(mixed):
    return jnp.where(mixed > 0, mixed + 1.0, jnp.exp(jnp.minimum(mixed, 0.0))).astype(bf16)


def state_kernel(placing, closing, rows, weight, vec, state_out, x_scr, acc, sums):
    gain, shift, bias = vector(vec, GAIN_ONE), vector(vec, SHIFT_ONE), vector(vec, BIAS_QKV)
    micro, step = pl.program_id(0), pl.program_id(1)
    per = STATE_TILE // STRETCH

    @pl.when(step == 0)
    def _():
        acc[...] = jnp.zeros_like(acc)
        sums[...] = jnp.zeros_like(sums)

    for i in range(per):
        x_scr[i * STRETCH : (i + 1) * STRETCH, :] = pick(rows, placing[micro, step * per + i])
    n, _ = standardize(x_scr[...].astype(f32))
    normed = (n * gain + shift).astype(bf16)
    keep = jnp.concatenate(
        [jnp.full((STRETCH, 1), flag(closing[micro, step * per + i]), f32) for i in range(per)],
        axis=0,
    )
    at = slice(MODEL, 2 * MODEL)
    keys = featured(nn(normed, weight[:, at]) + bias[:, at]).astype(f32) * keep
    sums[...] += jnp.sum(keys, axis=0, keepdims=True)
    keys = keys.astype(bf16)
    at = slice(2 * MODEL, 3 * MODEL)
    values = (nn(normed, weight[:, at]) + bias[:, at]).astype(bf16)
    for pair in range(PAIRS):
        acc[pair] += tn(keys[:, col(pair)], values[:, col(pair)])

    @pl.when(step == pl.num_programs(1) - 1)
    def _():
        for pair in range(PAIRS):
            pack_state(state_out, pair, acc[pair], sums[:, col(pair)])


def run_state(placing, closing, rows, weight, vec):
    micro, count = placing.shape
    width = rows.shape[-1]
    tiles = count * STRETCH // STATE_TILE
    return pl.pallas_call(
        state_kernel,
        name="end_state",
        grid_spec=pltpu.PrefetchScalarGridSpec(
            num_scalar_prefetch=2,
            grid=(micro, tiles),
            in_specs=[
                group_spec(rows.shape, 0),
                fixed(weight.shape),
                fixed(vec.shape),
            ],
            out_specs=member_spec(),
            scratch_shapes=[
                pltpu.VMEM((STATE_TILE, width), bf16),
                pltpu.VMEM((PAIRS, PAIR, PAIR), f32),
                pltpu.VMEM((1, MODEL), f32),
            ],
        ),
        out_shape=jax.ShapeDtypeStruct((micro, HEAD_DIM + 8, MODEL), f32),
        compiler_params=params(),
        cost_estimate=pl.CostEstimate(
            flops=11 << 30, bytes_accessed=5 << 20, transcendentals=0
        ),
    )(placing, closing, rows, weight, vec)


def causal(second, transposed):
    i = sublanes(CHUNK, 2 * CHUNK)
    j = lanes(CHUNK, 2 * CHUNK) % CHUNK
    if transposed:
        i, j = j, i
    crosses = (i >= STRETCH) & (j < STRETCH)
    return jnp.where(crosses, 1.0 - second, jnp.where(j <= i, 1.0, 0.0))


def start_all(when, copies):
    @pl.when(when)
    def _():
        for copy in copies:
            copy.start()


def mid_kernel(
    placing,
    restart,
    opened,
    owner,
    _,
    rows_ref,
    cot_ref,
    inc_ref,
    w_qkv,
    vec,
    w_out_far,
    w_up_far,
    w_down_far,
    *refs,
    first,
    resumes,
    final,
):
    gain_one, shift_one, b_qkv = vector(vec, GAIN_ONE), vector(vec, SHIFT_ONE), vector(vec, BIAS_QKV)
    gain, shift = vector(vec, GAIN_TWO), vector(vec, SHIFT_TWO)
    b_out, b_up, b_down = vector(vec, BIAS_OUT), vector(vec, BIAS_UP), vector(vec, BIAS_DOWN)
    before, refs = (refs[:3], refs[3:]) if resumes else ((), refs)
    result, qkv_ref, branch_out, gn_out, gd_out, states_out, state_out, vec_out = refs[:8]
    refs = refs[8:]
    if final:
        keep_out, send_out, turned, acc_up, acc_down, acc_out = refs[:6]
        refs = refs[6:]
    else:
        far_up, far_down, far_out, acc_up, acc_down, acc_out = refs[:6]
        refs = refs[6:]
    carry, back, back_sum, att_scr, inv_scr, att_b, x_scr, cot_scr, w_out, w_up, w_down, sems = refs
    member, step = pl.program_id(0), pl.program_id(1)
    micro = first + member
    per = TILE // STRETCH
    opening = (member == 0) & (step == 0)
    closing = (member == pl.num_programs(0) - 1) & (step == pl.num_programs(1) - 1)
    arriving = [
        pltpu.make_async_copy(source, target, sems.at[n])
        for n, (source, target) in enumerate(
            [(w_out_far, w_out), (w_up_far, w_up), (w_down_far, w_down)]
            + list(zip(before, (acc_up, acc_down, acc_out)))
        )
    ]
    leaving = []

    @pl.when(opening)
    def _():
        vec_out[...] = jnp.zeros_like(vec_out)
        for copy in arriving:
            copy.start()
        if not resumes:
            acc_up[...] = jnp.zeros_like(acc_up)
            acc_down[...] = jnp.zeros_like(acc_down)
            acc_out[...] = jnp.zeros_like(acc_out)

    @pl.when(step == 0)
    def _():
        for pair in range(PAIRS):
            carry[pair] = unpack_state(inc_ref[0], pair)
        back[...] = jnp.zeros_like(back)
        back_sum[...] = jnp.zeros_like(back_sum)

    block = same_head()
    ones_head = jnp.where(block, 1.0, 0.0).astype(bf16)
    ones_twice = jnp.concatenate([ones_head, ones_head], axis=0)
    low = first_head(CHUNK)
    one_low = jnp.where(low, 1.0, 0.0).astype(bf16)
    one_high = jnp.where(low, 0.0, 1.0).astype(bf16)
    ones_both = jnp.concatenate([one_low, one_high], axis=0)
    ones_all = jnp.ones((CHUNK, PAIR), bf16)
    wide_block = jnp.concatenate([block, block], axis=1)
    upper = sublanes(CHUNK, PAIR) < STRETCH
    inner = lanes(PAIR, PAIR) % HEAD_DIM
    zero_s = jnp.zeros((PAIR, PAIR), bf16)
    low_half = first_head(HEAD_DIM)
    for i in range(per):
        x_scr[i * STRETCH : (i + 1) * STRETCH, :] = pick(rows_ref, placing[micro, step * per + i])
        cot_scr[i * STRETCH : (i + 1) * STRETCH, :] = pick(cot_ref, placing[micro, step * per + i])

    x = x_scr[...].astype(f32)
    n, _ = standardize(x)
    normed = (n * gain_one + shift_one).astype(bf16)
    for part in range(2):
        at = slice(part * MODEL, (part + 1) * MODEL)
        qkv_ref[:, at] = featured(nn(normed, w_qkv[:, at]) + b_qkv[:, at])
    at = slice(2 * MODEL, 3 * MODEL)
    qkv_ref[:, at] = (nn(normed, w_qkv[:, at]) + b_qkv[:, at]).astype(bf16)

    for chunk in range(TILE // CHUNK):
        rows = slice(chunk * CHUNK, (chunk + 1) * CHUNK)
        r0 = flag(restart[micro, step * per + 2 * chunk])
        r1 = flag(restart[micro, step * per + 2 * chunk + 1])
        mask = causal(r1, False)
        keep_low = jnp.where(upper, 1.0, 1.0 - r1)
        keep_key = jnp.where(upper, 1.0 - r1, 1.0)
        for pair in range(PAIRS):
            q = qkv_ref[rows, pair * PAIR : (pair + 1) * PAIR]
            k = qkv_ref[rows, MODEL + pair * PAIR : MODEL + (pair + 1) * PAIR]
            v = qkv_ref[rows, 2 * MODEL + pair * PAIR : 2 * MODEL + (pair + 1) * PAIR]
            state = carry[pair] * (1.0 - r0)
            state_b = state.astype(bf16)
            state_low = (state - state_b.astype(f32)).astype(bf16)
            marked = jnp.where(
                inner < 2, state_b[:, PAIR:], jnp.where(inner == 2, state_low[:, PAIR:], zero_s)
            )
            for n_, item in enumerate((state_b[:, :PAIR], marked, state_low[:, :PAIR])):
                states_out[chunk, n_ * HEAD_DIM : (n_ + 1) * HEAD_DIM, col(pair)] = jnp.where(
                    low_half, item[:HEAD_DIM], item[HEAD_DIM:]
                )
            mixing = nt(q, by_head(k, CHUNK)) * mask
            values = jnp.concatenate([by_head(v, CHUNK), ones_both], axis=1)
            out = nn(mixing.astype(bf16), values)
            out = out + nn((q.astype(f32) * keep_low).astype(bf16), state_b)
            inv = 1.0 / out[:, PAIR:]
            att = out[:, :PAIR] * inv
            att_scr[rows, col(pair)] = att
            inv_scr[rows, col(pair)] = inv
            att_b[rows, col(pair)] = att.astype(bf16)
            k_keep = (k.astype(f32) * keep_key).astype(bf16)
            added = tn(k_keep, jnp.concatenate([v, ones_all], axis=1))
            carry[pair] = state * (1.0 - r1) + jnp.where(wide_block, added, 0.0)

    @pl.when(opening)
    def _():
        for copy in arriving:
            copy.wait()

    middle = x_scr[...].astype(f32) + nn(att_b[...], w_out[...]) + b_out
    n, scale = standardize(middle)
    normed = (n * gain + shift).astype(bf16)
    normed_t = normed.T
    cot = cot_scr[...]
    cot_t = cot.T
    ff = w_up.shape[1]
    total = middle + b_down
    up_grad = jnp.zeros((TILE, MODEL), f32)
    for part in range(ff // MODEL):
        at = slice(part * MODEL, (part + 1) * MODEL)
        u = nn(normed, w_up[:, at]) + b_up[:, at]
        u2 = u * u
        t = jnp.tanh(u * (0.7978845608028654 + 0.035677408136300125 * u2))
        half = 0.5 + 0.5 * t
        act = (u * half).astype(bf16)
        rise = 1.5957691216057308 + 0.21406444881780074 * u2
        slope = half + u * half * (1.0 - half) * rise
        g = (nt(cot, w_down[at, :]) * slope).astype(bf16)
        total = total + nn(act, w_down[at, :])
        acc_down[:, at] += nn(cot_t, act)
        vec_out[0:1, at] += jnp.sum(g.astype(f32), axis=0, keepdims=True)
        up_grad = up_grad + nt(g, w_up[:, at])
        acc_up[:, at] += nn(normed_t, g)
        if not final:
            leaving.append(pltpu.make_async_copy(acc_down.at[:, at], far_down.at[:, at], sems.at[6 + 2 * part]))
            leaving.append(pltpu.make_async_copy(acc_up.at[:, at], far_up.at[:, at], sems.at[7 + 2 * part]))
            start_all(closing, leaving[-2:])
    total = total.astype(bf16)
    for i in range(per):
        put(result, placing[micro, step * per + i], total[i * STRETCH : (i + 1) * STRETCH, :])

    cot_f = cot.astype(f32)
    vec_out[1:2, :MODEL] += jnp.sum(up_grad * n, axis=0, keepdims=True)
    vec_out[1:2, MODEL : 2 * MODEL] += jnp.sum(up_grad, axis=0, keepdims=True)
    vec_out[1:2, 3 * MODEL : 4 * MODEL] += jnp.sum(cot_f, axis=0, keepdims=True)
    branch = (cot_f + norm_back(up_grad, gain, n, scale)).astype(bf16)
    branch_out[...] = branch
    vec_out[1:2, 2 * MODEL : 3 * MODEL] += jnp.sum(branch.astype(f32), axis=0, keepdims=True)
    grad_att = nt(branch, w_out[...])
    acc_out[...] += tn(att_b[...], branch)
    if not final:
        leaving.append(pltpu.make_async_copy(acc_out, far_out, sems.at[6 + 2 * (ff // MODEL)]))
        start_all(closing, leaving[-1:])
    lane = lanes(CHUNK, PAIR) % HEAD_DIM
    for chunk in range(TILE // CHUNK):
        rows = slice(chunk * CHUNK, (chunk + 1) * CHUNK)
        o0 = flag(opened[micro, step * per + 2 * chunk])
        o1 = flag(opened[micro, step * per + 2 * chunk + 1])
        keep = jnp.where(upper, o0, o1)
        for pair in range(PAIRS):
            inv = inv_scr[rows, col(pair)]
            gn = (grad_att[rows, col(pair)].astype(bf16).astype(f32) * inv).astype(bf16)
            product = gn.astype(f32) * att_scr[rows, col(pair)]
            high = product.astype(bf16)
            low_part = (product - high.astype(f32)).astype(bf16)
            gd = -nn(jnp.concatenate([high, low_part], axis=1), ones_twice)
            gd_high = gd.astype(bf16)
            gd_low = (gd - gd_high.astype(f32)).astype(bf16)
            zero = jnp.zeros_like(gd_high)
            gn_out[rows, col(pair)] = gn
            gd_out[rows, col(pair)] = jnp.where(
                (lane == 0) | (lane == 2), gd_high, jnp.where(lane == 1, gd_low, zero)
            )
            q = qkv_ref[rows, pair * PAIR : (pair + 1) * PAIR].astype(f32) * keep
            back[pair] += tn(q.astype(bf16), gn)
            back_sum[:, col(pair)] += jnp.sum(q * gd, axis=0, keepdims=True)

    @pl.when(step == pl.num_programs(1) - 1)
    def _():
        for pair in range(PAIRS):
            pack_state(state_out, pair, back[pair], back_sum[:, col(pair)])

    if not final:

        @pl.when(closing)
        def _():
            for copy in leaving:
                copy.wait()

    else:

        @pl.when(closing)
        def _():
            parts = ff // MODEL
            devices = 2 * keep_out.shape[0]
            less = MODEL // devices
            more = parts * less
            for part in range(parts):
                at = slice(part * MODEL, (part + 1) * MODEL)
                turned[at, :] = acc_down[:, at].T
            for j in range(devices):
                d = owner[j]
                target = keep_out if j < devices // 2 else send_out
                seat = j % (devices // 2)
                here = pl.ds(pl.multiple_of(d * less, less), less)
                for part in range(parts):
                    target[seat, part * less : (part + 1) * less, :] = acc_up[
                        here, part * MODEL : (part + 1) * MODEL
                    ].astype(target.dtype)
                there = pl.ds(pl.multiple_of(d * more, more), more)
                target[seat, more : 2 * more, :] = turned[there, :].astype(target.dtype)
                target[seat, 2 * more :, :] = acc_out[here, :].astype(target.dtype)


def run_mid(tables, first, members, target, rows, cot, inc, weights, vec, before, owner):
    micro, count = tables[0].shape
    width = rows.shape[-1]
    ff = weights[2].shape[1]
    count = count * STRETCH
    tiles = count // TILE
    total = members * count
    resumes, final = before is not None, owner is not None
    f32_sums = [(width, ff), (width, ff), (MODEL, width)]
    out_specs = [
        group_spec(target.shape, 0),
        tile_spec(3 * MODEL, tiles),
        tile_spec(width, tiles),
        tile_spec(MODEL, tiles),
        tile_spec(MODEL, tiles),
        states_spec(tiles),
        member_spec(),
        fixed((8, ff)),
    ]
    out_shape = [
        jax.ShapeDtypeStruct(target.shape, bf16),
        jax.ShapeDtypeStruct((total, 3 * MODEL), bf16),
        jax.ShapeDtypeStruct((total, width), bf16),
        jax.ShapeDtypeStruct((total, MODEL), bf16),
        jax.ShapeDtypeStruct((total, MODEL), bf16),
        jax.ShapeDtypeStruct((total // CHUNK, 3 * HEAD_DIM, MODEL), bf16),
        jax.ShapeDtypeStruct((members, HEAD_DIM + 8, MODEL), f32),
        jax.ShapeDtypeStruct((8, ff), f32),
    ]
    if final:
        devices = owner.shape[0]
        half = (devices // 2, (2 * ff + MODEL) // devices, MODEL)
        out_specs += [fixed(half), fixed(half)]
        out_shape += [jax.ShapeDtypeStruct(half, bf16)] * 2
    else:
        out_specs += [ANYWHERE] * 3
        out_shape += [jax.ShapeDtypeStruct(shape, f32) for shape in f32_sums]
    if not final:
        owner = jnp.zeros((8,), jnp.int32)
    scratch = [pltpu.VMEM((ff, width), f32)] if final else []
    scratch += [pltpu.VMEM(shape, f32) for shape in f32_sums]
    scratch += [
        pltpu.VMEM((PAIRS, PAIR, 2 * PAIR), f32),
        pltpu.VMEM((PAIRS, PAIR, PAIR), f32),
        pltpu.VMEM((1, MODEL), f32),
        pltpu.VMEM((TILE, MODEL), f32),
        pltpu.VMEM((TILE, MODEL), f32),
        pltpu.VMEM((TILE, MODEL), bf16),
        pltpu.VMEM((TILE, width), bf16),
        pltpu.VMEM((TILE, width), bf16),
    ]
    scratch += [pltpu.VMEM(item.shape, bf16) for item in weights[1:]]
    scratch.append(pltpu.SemaphoreType.DMA((7 + 2 * (ff // MODEL),)))
    return pl.pallas_call(
        functools.partial(mid_kernel, first=first, resumes=resumes, final=final),
        name="middle",
        grid_spec=pltpu.PrefetchScalarGridSpec(
            num_scalar_prefetch=4,
            grid=(members, tiles),
            in_specs=[
                ANYWHERE,
                group_spec(rows.shape, first),
                group_spec(cot[0].shape, cot[1]),
                member_spec(first),
            ]
            + [fixed(weights[0].shape), fixed(vec.shape)]
            + [ANYWHERE] * (6 if resumes else 3),
            out_specs=out_specs,
            scratch_shapes=scratch,
        ),
        out_shape=out_shape,
        compiler_params=params(),
        input_output_aliases={4: 0},
        cost_estimate=pl.CostEstimate(
            flops=members * (24 << 30), bytes_accessed=members << 24, transcendentals=0
        ),
    )(*tables[:3], owner, target, rows, cot[0], inc, weights[0], vec, *weights[1:], *(before or ()))


def back_kernel(
    placing,
    restart,
    reach,
    owner,
    _,
    rows_ref,
    qkv_ref,
    gn_ref,
    gd_ref,
    branch_ref,
    states_ref,
    weight_far,
    vec,
    owner_col,
    *refs,
    first,
    resumes,
    final,
    widths,
    sums,
    hops,
):
    incs, refs = refs[:hops], refs[hops:]
    gain, shift = vector(vec, GAIN_ONE), vector(vec, SHIFT_ONE)
    before, refs = (refs[:1], refs[1:]) if resumes else ((), refs)
    vec_others, refs = refs[:sums], refs[sums:]
    grad_rows, vec_out = refs[:2]
    refs = refs[2:]
    if final:
        keep_out, send_out, acc = refs[:3]
        refs = refs[3:]
    else:
        far_acc, acc = refs[:2]
        refs = refs[2:]
    carry, x_scr, mixed_scr, weight, sems = refs
    member, step = pl.program_id(0), pl.program_id(1)
    micro = first + member
    per = TILE // STRETCH
    tile = pl.num_programs(1) - 1 - step
    opening = (member == 0) & (step == 0)
    lane = lanes(CHUNK, PAIR)
    inner = lane % HEAD_DIM

    closing = (member == pl.num_programs(0) - 1) & (step == pl.num_programs(1) - 1)
    arriving = [pltpu.make_async_copy(weight_far, weight, sems.at[0])]
    if resumes:
        arriving.append(pltpu.make_async_copy(before[0], acc, sems.at[1]))
    leaving = [] if final else [pltpu.make_async_copy(acc, far_acc, sems.at[2])]

    @pl.when(opening)
    def _():
        vec_out[...] = jnp.zeros_like(vec_out)
        for copy in arriving:
            copy.start()
        if not resumes:
            acc[...] = jnp.zeros_like(acc)

    @pl.when(step == 0)
    def _():
        only = jnp.concatenate([jnp.ones((PAIR, PAIR), f32), jnp.where(inner == 0, 1.0, 0.0)], axis=1)
        inc = jnp.zeros((HEAD_DIM + 8, MODEL), f32)
        for hop, ref in enumerate(incs):
            inc = inc + ref[0] * reach[micro, hop]
        for pair in range(PAIRS):
            carry[pair] = unpack_state(inc, pair) * only

    block = same_head()
    wide_block = jnp.concatenate([block, block], axis=1)
    upper = sublanes(CHUNK, PAIR) < STRETCH
    marks = jnp.where((inner < 2) | (inner == 3), 1.0, 0.0).astype(bf16)
    mark_low = jnp.where(lane < 2, 1.0, 0.0).astype(bf16)
    mark_high = jnp.where((lane == HEAD_DIM) | (lane == HEAD_DIM + 1), 1.0, 0.0).astype(bf16)
    marks_both = jnp.concatenate([mark_low, mark_high], axis=0)
    for i in range(per):
        x_scr[i * STRETCH : (i + 1) * STRETCH, :] = pick(rows_ref, placing[micro, tile * per + i])

    for chunk in reversed(range(TILE // CHUNK)):
        rows = slice(chunk * CHUNK, (chunk + 1) * CHUNK)
        r0 = flag(restart[micro, tile * per + 2 * chunk])
        r1 = flag(restart[micro, tile * per + 2 * chunk + 1])
        r2 = flag(restart[micro, tile * per + 2 * chunk + 2])
        mask = causal(r1, False)
        mask_t = causal(r1, True)
        keep_low = jnp.where(upper, 1.0, 1.0 - r1)
        keep_key = jnp.where(upper, 1.0 - r1, 1.0)
        for pair in range(PAIRS):
            q = qkv_ref[rows, pair * PAIR : (pair + 1) * PAIR]
            k = qkv_ref[rows, MODEL + pair * PAIR : MODEL + (pair + 1) * PAIR]
            v = qkv_ref[rows, 2 * MODEL + pair * PAIR : 2 * MODEL + (pair + 1) * PAIR]
            gn = gn_ref[rows, col(pair)]
            gdx = gd_ref[rows, col(pair)]
            state, state_z, state_low = (
                by_head(states_ref[chunk, n * HEAD_DIM : (n + 1) * HEAD_DIM, col(pair)], HEAD_DIM)
                for n in range(3)
            )
            grown = carry[pair] * (1.0 - r2)
            grown_b = grown.astype(bf16)
            rest = grown - grown_b.astype(f32)
            grown_low = rest[:, :PAIR].astype(bf16)
            z_low = pltpu.roll(rest[:, PAIR:], 3, 1).astype(bf16)
            z_both = jnp.where(inner < 2, grown_b[:, PAIR:], jnp.where(inner == 3, z_low, jnp.zeros_like(z_low)))
            grown_x = jnp.concatenate([grown_b[:, :PAIR], z_both], axis=1)
            k2 = by_head(k, CHUNK)
            q2 = by_head(q, CHUNK)
            v2 = by_head(v, CHUNK)
            gn2 = by_head(gn, CHUNK)
            gd2 = by_head(gdx, CHUNK)
            both = jnp.concatenate([gn, gdx], axis=1)
            mixing_t = (nt(k, q2) * mask_t).astype(bf16)
            g_mix = (nt(both, jnp.concatenate([v2, marks_both], axis=1)) * mask).astype(bf16)
            v_marks = jnp.concatenate([v, marks], axis=1)
            g_mix_t = (nt(v_marks, jnp.concatenate([gn2, gd2], axis=1)) * mask_t).astype(bf16)
            dq = nn(g_mix, k2) + (
                nt(both, jnp.concatenate([state, state_z], axis=1)) + nt(gn, state_low)
            ) * keep_low
            dk = nn(g_mix_t, q2) + (nt(v_marks, grown_x) + nt(v, grown_low)) * keep_key
            dv = nn(mixing_t, gn2) + nn(k, grown_b[:, :PAIR]) * keep_key
            q_keep = (q.astype(f32) * keep_low).astype(bf16)
            added = tn(q_keep, both)
            carry[pair] = (grown * (1.0 - r1) + jnp.where(wide_block, added, 0.0)) * (1.0 - r0)
            mixed_scr[rows, pair * PAIR : (pair + 1) * PAIR] = (
                dq * jnp.minimum(q.astype(f32), 1.0)
            ).astype(bf16)
            mixed_scr[rows, MODEL + pair * PAIR : MODEL + (pair + 1) * PAIR] = (
                dk * jnp.minimum(k.astype(f32), 1.0)
            ).astype(bf16)
            mixed_scr[rows, 2 * MODEL + pair * PAIR : 2 * MODEL + (pair + 1) * PAIR] = dv.astype(bf16)

    @pl.when(opening)
    def _():
        for copy in arriving:
            copy.wait()

    mixed = mixed_scr[...]
    vec_out[0:1, :] += jnp.sum(mixed.astype(f32), axis=0, keepdims=True)
    upstream = nt(mixed, weight[...])
    n, scale = standardize(x_scr[...].astype(f32))
    normed_t = (n * gain + shift).astype(bf16).T
    for part in range(3):
        at = slice(part * MODEL, (part + 1) * MODEL)
        acc[:, at] += nn(normed_t, mixed[:, at])
    start_all(closing, leaving)
    vec_out[1:2, :MODEL] += jnp.sum(upstream * n, axis=0, keepdims=True)
    vec_out[1:2, MODEL : 2 * MODEL] += jnp.sum(upstream, axis=0, keepdims=True)
    total = (branch_ref[...].astype(f32) + norm_back(upstream, gain, n, scale)).astype(bf16)
    for i in range(per):
        put(grad_rows, placing[micro, tile * per + i], total[i * STRETCH : (i + 1) * STRETCH, :])

    if not final:

        @pl.when(closing)
        def _():
            for copy in leaving:
                copy.wait()

    else:

        @pl.when((member == pl.num_programs(0) - 1) & (step == pl.num_programs(1) - 1))
        def _():
            half = keep_out.shape[0]
            devices = 2 * half
            less = MODEL // devices
            for j in range(devices):
                here = pl.ds(pl.multiple_of(owner[j] * less, less), less)
                target = keep_out if j < half else send_out
                for part in range(3):
                    target[j % half, part * less : (part + 1) * less, :] = acc[
                        here, part * MODEL : (part + 1) * MODEL
                    ].astype(target.dtype)
            mid = sum(ref[...] for ref in vec_others if ref.shape[1] == vec_others[0].shape[1])
            rear = vec_out[...] + sum(
                ref[...] for ref in vec_others if ref.shape[1] != vec_others[0].shape[1]
            )
            sources = (
                rear[1:2, :MODEL],
                rear[1:2, MODEL : 2 * MODEL],
                rear[0:1, : 2 * MODEL],
                rear[0:1, 2 * MODEL :],
                mid[1:2, 2 * MODEL : 3 * MODEL],
                mid[1:2, :MODEL],
                mid[1:2, MODEL : 2 * MODEL],
                mid[0:1, :],
                mid[1:2, 3 * MODEL : 4 * MODEL],
            )
            rows8 = sublanes(8, MODEL)
            pieces = []
            for source, width in zip(sources, widths, strict=True):
                size = devices * width
                mine = (lanes(devices, size) // width) == owner_col[...]
                picked = jnp.where(mine, source, 0.0)
                gather = jnp.where(
                    (sublanes(size, PAIR) % width) == lanes(size, PAIR), 1.0, 0.0
                ).astype(bf16)
                high = picked.astype(bf16)
                low = (picked - high.astype(f32)).astype(bf16)
                pieces.append(nn(high, gather) + nn(low, gather))
            rest = jnp.zeros((1, MODEL - 2 * PAIR), f32)
            blank_row = jnp.zeros((1, PAIR), f32)
            for j in range(devices):
                block8 = jnp.zeros((8, MODEL), f32)
                for v, piece in enumerate(pieces[:8]):
                    more = pieces[8 + v][j : j + 1, :] if 8 + v < len(pieces) else blank_row
                    row = jnp.concatenate([piece[j : j + 1, :], more, rest], axis=1)
                    block8 = block8 + jnp.where(rows8 == v, row, 0.0)
                target = keep_out if j < half else send_out
                target[j % half, 3 * less :, :] = block8.astype(target.dtype)


def run_back(tables, first, members, target, rows, mid, incs, weight, vec, before, owner, others, widths):
    (group, seat), (saved, at) = target, mid
    micro, count = tables[0].shape
    width = rows.shape[-1]
    count = count * STRETCH
    tiles = count // TILE
    resumes, final = before is not None, owner is not None
    devices = lax.axis_size(BOTH) if final else 0
    if not final:
        owner = jnp.zeros((8,), jnp.int32)
        others = []
    half = (devices // 2, 3 * MODEL // max(devices, 1) + 8, MODEL)
    out_specs = [group_spec(group.shape, seat), fixed((8, 3 * MODEL))]
    out_shape = [
        jax.ShapeDtypeStruct(group.shape, bf16),
        jax.ShapeDtypeStruct((8, 3 * MODEL), f32),
    ]
    scratch = []
    if final:
        out_specs += [fixed(half), fixed(half)]
        out_shape += [jax.ShapeDtypeStruct(half, bf16)] * 2
    else:
        out_specs.append(ANYWHERE)
        out_shape.append(jax.ShapeDtypeStruct((width, 3 * MODEL), f32))
    scratch += [
        pltpu.VMEM((width, 3 * MODEL), f32),
        pltpu.VMEM((PAIRS, PAIR, 2 * PAIR), f32),
        pltpu.VMEM((TILE, width), bf16),
        pltpu.VMEM((TILE, 3 * MODEL), bf16),
        pltpu.VMEM(weight.shape, bf16),
        pltpu.SemaphoreType.DMA((3,)),
    ]

    def tile(width_):
        return pl.BlockSpec((TILE, width_), lambda i, t, *_: ((at + i) * tiles + tiles - 1 - t, 0))

    return pl.pallas_call(
        functools.partial(
            back_kernel,
            first=first,
            resumes=resumes,
            final=final,
            widths=widths,
            sums=len(others),
            hops=len(incs),
        ),
        name="back",
        grid_spec=pltpu.PrefetchScalarGridSpec(
            num_scalar_prefetch=4,
            grid=(members, tiles),
            in_specs=[
                ANYWHERE,
                group_spec(rows.shape, first),
                tile(3 * MODEL),
                tile(MODEL),
                tile(MODEL),
                tile(width),
                pl.BlockSpec(
                    (TILE // CHUNK, 3 * HEAD_DIM, MODEL),
                    lambda i, t, *_: ((at + i) * tiles + tiles - 1 - t, 0, 0),
                ),
                ANYWHERE,
                fixed(vec.shape),
                fixed((owner.shape[0], 1)),
            ]
            + [member_spec(at)] * len(incs)
            + ([ANYWHERE] if resumes else [])
            + [fixed(item.shape) for item in others],
            out_specs=out_specs,
            scratch_shapes=scratch,
        ),
        out_shape=out_shape,
        input_output_aliases={4: 0},
        compiler_params=params(),
        cost_estimate=pl.CostEstimate(
            flops=members * (15 << 30), bytes_accessed=members << 24, transcendentals=0
        ),
    )(
        tables[0],
        tables[1],
        tables[3],
        owner,
        group,
        rows,
        saved[1],
        saved[3],
        saved[4],
        saved[2],
        saved[5],
        weight,
        vec,
        owner[:, None],
        *incs,
        *(() if before is None else (before,)),
        *others,
    )


def send_kernel(slot, source, target, *, first):
    micro = first + pl.program_id(0)
    for i in range(source.shape[1]):
        put(target, slot[micro, i], source[0, i])


def run_send(slot, rows, first, members):
    micro, count, width = rows.shape
    stretches = count // STRETCH
    groups = lax.axis_size("dp")
    shape = (groups, members, stretches // groups, STRETCH, width)
    return pl.pallas_call(
        functools.partial(send_kernel, first=first),
        name="send",
        grid_spec=pltpu.PrefetchScalarGridSpec(
            num_scalar_prefetch=1,
            grid=(members,),
            in_specs=[
                pl.BlockSpec((1, stretches, STRETCH, width), lambda i, *_: (first + i, 0, 0, 0))
            ],
            out_specs=pl.BlockSpec((groups, 1) + shape[2:], lambda i, *_: (0, i, 0, 0, 0)),
        ),
        out_shape=jax.ShapeDtypeStruct(shape, rows.dtype),
        compiler_params=pltpu.CompilerParams(vmem_limit_bytes=VMEM_LIMIT),
        cost_estimate=pl.CostEstimate(
            flops=0, bytes_accessed=4 * members * count * width, transcendentals=0
        ),
    )(slot, rows.reshape(micro, stretches, STRETCH, width))


def land_kernel(slot, _, source, target, *, first):
    micro = first + pl.program_id(0)
    for i in range(target.shape[1]):
        target[0, i] = pick(source, slot[micro, i])


def run_land(slot, landed, output, first):
    members = landed.shape[1]
    shape = output.shape
    block = (landed.shape[0], 1) + landed.shape[2:]
    return pl.pallas_call(
        functools.partial(land_kernel, first=first),
        name="land",
        grid_spec=pltpu.PrefetchScalarGridSpec(
            num_scalar_prefetch=1,
            grid=(members,),
            in_specs=[
                pl.BlockSpec(memory_space=pl.ANY),
                pl.BlockSpec(block, lambda i, *_: (0, i, 0, 0, 0)),
            ],
            out_specs=pl.BlockSpec((1,) + shape[1:], lambda i, *_: (first + i, 0, 0, 0)),
        ),
        out_shape=jax.ShapeDtypeStruct(shape, output.dtype),
        input_output_aliases={1: 0},
        compiler_params=pltpu.CompilerParams(vmem_limit_bytes=VMEM_LIMIT),
        cost_estimate=pl.CostEstimate(flops=0, bytes_accessed=4 * landed.size, transcendentals=0),
    )(slot, output, landed)


def blank(shape):
    return pl.pallas_call(
        lambda ref: None,
        name="blank",
        out_specs=pl.BlockSpec(memory_space=pl.ANY),
        out_shape=jax.ShapeDtypeStruct(shape, bf16),
    )()


def index_tables(lengths, stretch_order, count):
    fsdp = lax.axis_size("fsdp")
    groups = lax.axis_size("dp")
    device = lax.axis_index(BOTH)
    base = device * count
    within = jnp.arange(count, dtype=jnp.int32)
    mine = base + within
    place = jnp.arange(stretch_order.shape[1], dtype=jnp.int32)
    here = place[None, None, :]
    landing = jnp.sum(
        jnp.where(stretch_order[:, None, :] == mine[None, :, None], here, 0), axis=-1
    )
    slot = jnp.sum((landing[:, None, :] < landing[:, :, None]).astype(jnp.int32), axis=-1)
    arrival = jnp.sum(
        jnp.where(here == mine[None, :, None], stretch_order[:, None, :], 0), axis=-1
    )
    source = arrival // count // fsdp
    ahead = (source[:, None, :] == source[:, :, None]) & (
        within[None, None, :] < within[None, :, None]
    )
    placing = source * (count // groups) + jnp.sum(ahead.astype(jnp.int32), axis=-1)
    index = jnp.arange(lengths.shape[1], dtype=jnp.int32)
    starts = jnp.sum(
        jnp.where(index[None, None, :] < index[None, :, None], lengths[:, None, :], 0), axis=-1
    )
    edge = base + jnp.arange(count + 1, dtype=jnp.int32)
    restart = jnp.any(starts[:, None, :] == edge[None, :, None], axis=-1).astype(jnp.int32)
    restart = jnp.where(edge[None, :] == stretch_order.shape[1], 1, restart)
    opened = 1 - jnp.any(
        (starts[:, None, :] >= base) & (starts[:, None, :] <= mine[None, :, None]), axis=-1
    ).astype(jnp.int32)
    last = base + count - 1
    closing = 1 - jnp.any(
        (starts[:, None, :] > mine[None, :, None]) & (starts[:, None, :] <= last), axis=-1
    ).astype(jnp.int32)
    hops = -(-(LONGEST - 1) // count)
    hop = jnp.arange(hops, dtype=jnp.int32)
    reach_back = base - 1 - hop * count
    from_before = 1.0 - jnp.any(
        (starts[:, None, :] > reach_back[None, :, None]) & (starts[:, None, :] <= base), axis=-1
    ).astype(f32)
    reach_on = base + (hop + 1) * count
    from_after = 1.0 - jnp.any(
        (starts[:, None, :] > last) & (starts[:, None, :] <= reach_on[None, :, None]), axis=-1
    ).astype(f32)
    first = base - hop * count
    unbroken = 1.0 - jnp.any(
        (starts[:, None, :] >= first[None, :, None]) & (starts[:, None, :] <= last), axis=-1
    ).astype(f32)
    return slot, placing, restart, opened, closing, from_before, from_after, unbroken


def exchange(states, hops, forward):
    size = lax.axis_size("fsdp")
    got = []
    for hop in range(min(hops, size - 1)):
        step = hop + 1
        pairs = [(i, i + step) if forward else (i + step, i) for i in range(size - step)]
        got.append(lax.ppermute(states, "fsdp", pairs))
    return got


def passed_on(states, weights, unbroken, beside):
    size = lax.axis_size("fsdp")
    total, own, step = jnp.zeros_like(states), states, 1
    while step <= weights.shape[1] and step < size:
        got = lax.ppermute(own, "fsdp", [(i, i + step) for i in range(size - step)])
        if step == 1:
            got = after(got, beside)
        total = total + got * weights[:, step - 1, None, None]
        own = own + got * unbroken[:, step - 1, None, None]
        step *= 2
    return total


def halving_stages():
    stages = []
    dp, fsdp = lax.axis_size("dp"), lax.axis_size("fsdp")
    if dp > 1:
        stages.append(("dp", 1))
    bit = 1
    while bit < fsdp:
        stages.append(("fsdp", bit))
        bit *= 2
    bit = 2
    while bit < dp:
        stages.append(("dp", bit))
        bit *= 2
    return stages


def order_tables():
    stages = halving_stages()
    fsdp = lax.axis_size("fsdp")
    devices = lax.axis_size(BOTH)
    me = lax.axis_index(BOTH)
    index = jnp.arange(devices, dtype=jnp.int32)
    bits = [bit * (fsdp if axis == "dp" else 1) for axis, bit in stages]
    place = jnp.zeros((devices,), jnp.int32)
    owner = jnp.zeros((devices,), jnp.int32)
    for s, bit in enumerate(bits):
        rank = len(bits) - 1 - s
        place = place + jnp.where(((index ^ me) & bit) != 0, 1 << rank, 0)
        owner = owner + jnp.where(((index >> rank) & 1) != 0, bit, 0)
    return place, owner ^ me


def after(x, *others):
    return lax.optimization_barrier((x, others))[0]


def swap(x, axis, bit):
    return lax.ppermute(x, axis, [(i, i ^ bit) for i in range(lax.axis_size(axis))])


def gather_halves(x, ties):
    stages = list(reversed(halving_stages()))
    steps = []
    for s, (axis, bit) in enumerate(stages[:-1]):
        if s in ties:
            x = after(x, ties[s])
        x = jnp.concatenate([x, swap(x, axis, bit)], axis=0)
        steps.append(x)
    return (x, swap(x, *stages[-1])), steps


def scatter_step(keep, send, s):
    stages = halving_stages()
    return scatter_join(keep, swap(send, *stages[s]), s == len(stages) - 1)


def scatter_join(keep, got, last):
    if last:
        return keep[0].astype(f32) + got[0].astype(f32), None
    half = keep.shape[0] // 2
    send = (keep[half:].astype(f32) + got[half:].astype(f32)).astype(bf16)
    return keep[:half].astype(f32) + got[:half].astype(f32), send


def finish_kernel(keep, got, qkv, *vectors):
    total = keep[0] + got[0].astype(f32)
    rows = qkv.shape[0]
    for part in range(3):
        qkv[:, part * MODEL : (part + 1) * MODEL] = total[part * rows : (part + 1) * rows, :]
    for v, ref in enumerate(vectors):
        row, at = 3 * rows + v % 8, v // 8 * PAIR
        ref[...] = total[row : row + 1, at : at + ref.shape[1]]


def run_finish(keep, got, widths):
    rows = (keep.shape[1] - 8) // 3
    return pl.pallas_call(
        finish_kernel,
        name="finish",
        out_shape=[jax.ShapeDtypeStruct((rows, 3 * MODEL), f32)]
        + [jax.ShapeDtypeStruct((1, width), f32) for width in widths],
    )(keep, got)


def pack_kernel(qkv, out, up, down, *refs):
    *small, first, second = refs
    rows = qkv.shape[0]
    for c in range(3):
        first[0, c * rows : (c + 1) * rows, :] = qkv[:, c * MODEL : (c + 1) * MODEL]
    row = sublanes(16, PAIR)
    side = jnp.zeros((16, PAIR), f32)
    for v, item in enumerate(small):
        width = item.shape[1]
        spread = jnp.where(sublanes(width, PAIR) == lanes(width, PAIR), 1.0, 0.0).astype(bf16)
        tall = jnp.broadcast_to(item[...].astype(f32), (16, width)).astype(bf16)
        side = side + jnp.where(row == v, nn(tall, spread), 0.0)
    side = jnp.concatenate([side, jnp.zeros((16, MODEL - PAIR), f32)], axis=1)
    first[0, 3 * rows : 3 * rows + 16, :] = side.astype(bf16)
    parts = up.shape[1] // MODEL
    for c in range(parts):
        second[0, c * rows : (c + 1) * rows, :] = up[:, c * MODEL : (c + 1) * MODEL]
    second[0, parts * rows : 2 * parts * rows, :] = down[...]
    second[0, 2 * parts * rows :, :] = out[...]


def run_pack(qkv, out, up, down, small):
    rows = qkv.shape[0]
    parts = up.shape[1] // MODEL
    return pl.pallas_call(
        pack_kernel,
        name="pack",
        out_shape=[
            jax.ShapeDtypeStruct((1, 3 * rows + 16, MODEL), bf16),
            jax.ShapeDtypeStruct((1, (2 * parts + 1) * rows, MODEL), bf16),
        ],
    )(qkv, out, up, down, *(item[None] for item in small))


def sort_first_kernel(place, own, got, owner, qkv, vectors, *, widths):
    half, total, _ = own.shape
    rows = total // 4

    def part(d):
        p = place[d]
        q = lax.rem(p, half)
        return jnp.where(p < half, own[q, : 3 * rows, :], got[q, : 3 * rows, :])

    for d in range(2 * half):
        block = part(d)
        for c in range(3):
            qkv[d * rows : (d + 1) * rows, c * MODEL : (c + 1) * MODEL] = block[
                c * rows : (c + 1) * rows, :
            ]
    small = jnp.concatenate(
        [own[:, 3 * rows :, :PAIR].astype(f32), got[:, 3 * rows :, :PAIR].astype(f32)], axis=0
    )
    row = lax.broadcasted_iota(jnp.int32, small.shape, 1)
    vectors[...] = jnp.zeros_like(vectors)
    for v, width in enumerate(widths):
        values = jnp.sum(jnp.where(row == v, small, 0.0), axis=1)
        size = 2 * half * width
        lane = lanes(PAIR, size) % width
        spread = jnp.where(lane == sublanes(PAIR, size), 1.0, 0.0).astype(bf16)
        wide = nn(values.astype(bf16), spread)
        mine = (lanes(2 * half, size) // width) == owner[...]
        vectors[v : v + 1, :size] = jnp.sum(jnp.where(mine, wide, 0.0), axis=0, keepdims=True)


def run_sort_first(place, owner, own, got, widths):
    devices = place.shape[0]
    rows = own.shape[1] // 4
    vmem = pl.BlockSpec(memory_space=pltpu.VMEM)
    return pl.pallas_call(
        functools.partial(sort_first_kernel, widths=widths),
        name="sort_first",
        in_specs=[pl.BlockSpec(memory_space=pltpu.SMEM), vmem, vmem, vmem],
        out_specs=[vmem, vmem],
        out_shape=[
            jax.ShapeDtypeStruct((devices * rows, 3 * MODEL), bf16),
            jax.ShapeDtypeStruct((8, devices * max(widths)), f32),
        ],
        compiler_params=pltpu.CompilerParams(vmem_limit_bytes=VMEM_LIMIT),
    )(place, own, got, owner[:, None])


def sort_second_kernel(gathered, up, down, out):
    devices, total, _ = gathered.shape
    parts = up.shape[1] // MODEL
    rows = total // (2 * parts + 1)
    tall = parts * rows
    for d in range(devices):
        for c in range(parts):
            up[d * rows : (d + 1) * rows, c * MODEL : (c + 1) * MODEL] = gathered[
                d, c * rows : (c + 1) * rows, :
            ]
        down[d * tall : (d + 1) * tall, :] = gathered[d, tall : 2 * tall, :]
        out[d * rows : (d + 1) * rows, :] = gathered[d, 2 * tall :, :]


def run_sort_second(gathered, ff):
    devices = gathered.shape[0]
    rows = gathered.shape[1] // (2 * (ff // MODEL) + 1)
    vmem = pl.BlockSpec(memory_space=pltpu.VMEM)
    return pl.pallas_call(
        sort_second_kernel,
        name="sort_second",
        in_specs=[vmem],
        out_specs=[vmem, vmem, vmem],
        out_shape=[
            jax.ShapeDtypeStruct((devices * rows, ff), bf16),
            jax.ShapeDtypeStruct((ff, MODEL), bf16),
            jax.ShapeDtypeStruct((devices * rows, MODEL), bf16),
        ],
        compiler_params=pltpu.CompilerParams(vmem_limit_bytes=VMEM_LIMIT),
    )(gathered)


def gather_all(x):
    return lax.all_gather(x, BOTH, axis=0, tiled=True)


def scatter_all(x):
    return lax.psum_scatter(x, BOTH, scatter_dimension=0, tiled=True)


def to_dp(group):
    return lax.all_to_all(group, "dp", split_axis=0, concat_axis=0, tiled=True)


def groups_of(micro):
    return [(0, micro - 1), (micro - 1, 1)] if micro > 1 else [(0, 1)]


def find(groups, m):
    for g, (first, members) in enumerate(groups):
        if first <= m < first + members:
            return g, m - first


def body(
    tokens,
    cotangent,
    lengths,
    stretch_order,
    ln1_gain,
    ln1_bias,
    w_qkv,
    b_qkv,
    w_out,
    b_out,
    ln2_gain,
    ln2_bias,
    w_up,
    b_up,
    w_down,
    b_down,
):
    micro, rows, width = tokens.shape
    count = rows // STRETCH
    devices = lax.axis_size(BOTH)
    ff = w_up.shape[1]
    dp = lax.axis_size("dp")
    slot, placing, restart, opened, closing, from_before, from_after, unbroken = index_tables(
        lengths, stretch_order, count
    )
    tables = (placing, restart, opened, from_after)
    small = (ln1_gain, ln1_bias, b_qkv, b_out, ln2_gain, ln2_bias, b_up, b_down)
    in_parts = (width // devices) % 16 == 0
    groups = groups_of(micro)
    sent = run_send(slot, tokens, 0, micro)
    if in_parts:
        place, owner = order_tables()
        first_part, second_part = run_pack(w_qkv, w_out, w_up, w_down, small)
        halves, steps = gather_halves(first_part, {1: sent, 3: tables + (closing, from_before, unbroken)})
        moved = to_dp(after(sent, steps[0]))
        qkv_all, vectors = run_sort_first(
            place, owner, *halves, [item.shape[0] for item in small]
        )
        ready = (qkv_all,)
        second_part = gather_all(second_part)
    else:
        owner, ready = None, ()
        moved = to_dp(sent)
        qkv_all, out_all = gather_all(w_qkv), gather_all(w_out)
        up_all, down_all = gather_all(w_up), gather_all(w_down)
        vectors = [gather_all(item).astype(f32) for item in small]
        vectors = jnp.stack([jnp.pad(item, (0, ff - item.shape[0])) for item in vectors])

    sent_grads = run_send(slot, after(cotangent, *ready), 0, micro)
    hops = from_before.shape[1]
    states = run_state(placing, closing, moved, qkv_all, vectors)
    cots = to_dp(sent_grads)
    if in_parts:
        up_all, down_all, out_all = run_sort_second(after(second_part, states), ff)
    incoming = passed_on(states, from_before, unbroken, out_all)
    weights = [qkv_all, out_all, up_all, down_all]
    mids, sums = [], None
    for g, (first, members) in enumerate(groups):
        target = blank((dp, members, count // dp, STRETCH, width))
        out = run_mid(
            tables,
            first,
            members,
            target,
            moved,
            (cots, first),
            incoming,
            weights,
            vectors,
            sums,
            owner if g == len(groups) - 1 else None,
        )
        sums = out[8:]
        mids.append(out)
    outgoing = [exchange(out[6], hops, False) for out in mids]
    homes = [to_dp(out[0]) for out in mids]
    sizes = [MODEL, MODEL, 2 * MODEL, MODEL, MODEL, MODEL, MODEL, ff, MODEL]
    widths = [size // devices for size in sizes]
    last = len(halving_stages()) - 1
    late = len(groups) - 1
    outgoing[0] = after(outgoing[0], *([mids[-1][7]] if late else []))
    if in_parts:
        keep, send = sums
        if late:
            send = after(send, outgoing[0], homes[0])
        keep, send = scatter_step(keep, send, 0)
        done = 0
    vec_mid = [f[7] for f in mids]
    vec_back, total = [], None
    grad_rows = []
    for g, (first, members) in enumerate(groups):
        if g:
            outgoing[g] = after(outgoing[g], vec_back[0], homes[g])
            grad_rows[0] = after(grad_rows[0], outgoing[g])
        saved = list(mids[g])
        if in_parts:
            saved[2], keep, send = lax.optimization_barrier((saved[2], keep, send))
            got = swap(send, *halving_stages()[done + 1])
        out = run_back(
            tables,
            first,
            members,
            (blank((dp, members, count // dp, STRETCH, width)), 0),
            moved,
            (saved, 0),
            outgoing[g],
            qkv_all,
            vectors,
            total,
            owner if g == late else None,
            vec_mid + vec_back,
            widths,
        )
        grad_rows.append(out[0])
        vec_back.append(out[1])
        total = out[2]
        if in_parts:
            done += 1
            keep, send = scatter_join(keep, after(got, out[1]), done == last)
            if g == late:
                grad_rows[g] = after(grad_rows[g], keep)
    narrow = out[2:]
    grad_homes = [to_dp(group) for group in grad_rows]
    result = blank((micro, count, STRETCH, width))
    input_grad = blank((micro, count, STRETCH, width))

    def land(output, pieces, *others):
        for (first, _), home in zip(groups, pieces, strict=True):
            output = run_land(slot, after(home, *others), output, first)
        return output

    if in_parts:
        part = width // devices
        narrow_keep, narrow_send = narrow
        if len(groups) > 1:
            narrow_send = after(narrow_send, grad_homes[0], keep, send)
        wide_keep, wide_send, got = keep, send, None
        if done < last:
            done += 1
            got = swap(send, *halving_stages()[done])
        keep, send = narrow_keep, narrow_send
        for step in range(last):
            keep, send = scatter_step(keep, send, step)
            if step == 0:
                result = land(result, homes, send)
            if step == 1:
                send = after(send, result, *(() if got is None else (got,)))
                input_grad = land(input_grad, grad_homes, send)
            if step == 2:
                send = after(send, input_grad)
                if got is not None:
                    wide_keep, wide_send = scatter_join(wide_keep, after(got, send), done == last)
                while done < last:
                    done += 1
                    wide_keep, wide_send = scatter_step(wide_keep, wide_send, done)
        wide = wide_keep
        parts = ff // MODEL
        grad_up = jnp.concatenate([wide[c * part : (c + 1) * part] for c in range(parts)], axis=1)
        grad_down = wide[parts * part : 2 * parts * part]
        grad_out = wide[2 * parts * part :]
        grad_qkv, *owned_vec = run_finish(keep, swap(send, *halving_stages()[last]), widths)
        owned_vec = [item[0] for item in owned_vec]
    else:
        grad_up, grad_down, grad_out = (scatter_all(x) for x in (sums[0], sums[1].T, sums[2]))
        grad_qkv = scatter_all(total)
        mid, back = sum(vec_mid), sum(vec_back)
        vec = (
            back[1, :MODEL],
            back[1, MODEL : 2 * MODEL],
            back[0, : 2 * MODEL],
            back[0, 2 * MODEL :],
            mid[1, 2 * MODEL : 3 * MODEL],
            mid[1, :MODEL],
            mid[1, MODEL : 2 * MODEL],
            mid[0],
            mid[1, 3 * MODEL :],
        )
        owned_vec = [scatter_all(item) for item in vec]
        result, input_grad = land(result, homes), land(input_grad, grad_homes)
    result = result.reshape(micro, rows, width)
    input_grad = input_grad.reshape(micro, rows, width)
    g_gain1, g_bias1, g_qk, g_value, g_bout, g_gain2, g_bias2, g_bup, g_bdown = owned_vec
    return (
        result,
        input_grad,
        g_gain1,
        g_bias1,
        grad_qkv,
        g_qk,
        g_value,
        grad_out,
        g_bout,
        g_gain2,
        g_bias2,
        grad_up,
        g_bup,
        grad_down,
        g_bdown,
    )


def solution(mesh):
    rows = P(None, BOTH, None)
    vector = P(BOTH)
    matrix = P(BOTH, None)
    in_specs = (
        rows, rows, P(), P(), vector, vector, matrix, vector, matrix, vector, vector, vector,
        matrix, vector, matrix, vector,
    )
    out_specs = (
        rows, rows, vector, vector, matrix, vector, vector, matrix, vector, vector, vector,
        matrix, vector, matrix, vector,
    )
    return jax.shard_map(body, mesh=mesh, in_specs=in_specs, out_specs=out_specs, check_vma=False)
```
